32 devices in a mesh: grp: 2 (over core), seq: 4 (over y, x), row: 4 (over z).
Axes of the slice: x: 2, y: 2, z: 4, core: 2. Of those that a mesh axis runs over, the one named last changes fastest.
Arguments:
- tokens: bfloat16 [512, 70, 1150], P(('grp', 'seq')), may hold values from -6 to 6
- in_mask: int32 [512, 1150], P(('grp', 'seq')), may hold values 0 or 1
- out_mask: int32 [512, 400], P(('grp', 'seq')), may hold values 0 or 1
- lengths: int32 [512], P(('grp', 'seq')), may hold values from 35 to 70, as said below
- groups: int32 [512], P(('grp', 'seq')), may hold values from 0 to 1, as said below
- input_gate_weight: bfloat16 [1600, 1150], P('row'), may hold values from -0.1875 to 0.1875
- w_recur: bfloat16 [1600, 400], P('row'), may hold values from -0.3125 to 0.3125
- weight_mask: int32 [1600, 400], P('row'), may hold values 0 or 1
- bias: float32 [1600], P('row'), may hold values from -3 to 3
- cotangent: bfloat16 [512, 70, 400], P(('grp', 'seq')), may hold values from -6 to 6
Outputs:
- input_grad: float32 [512, 70, 1150], P(('grp', 'seq', 'row'))
- grad_input_weight: float32 [2, 1600, 1150], P('grp', 'row')
- grad_recur_weight: float32 [2, 1600, 400], P('grp', 'row')
- grad_bias: float32 [2, 1600], P('grp', 'row')
- gram: float32 [2, 2], replicated
The draws below stay inside these ranges and needn't reach their ends.
Inputs may be any that keep to these rules, and one draw needn't show every extreme that they name: `lengths`: each sequence has the full length or fewer steps; some sequence of the batch has exactly 70 steps and some exactly 35. Both groups have sequences.
All inputs are finite; a program needn't handle non-finite values. No bound on the sum of `in_mask` or of `out_mask` or of `weight_mask` on one device may be relied on, other than what follows from the above.
Results may differ from the reference program's by a relative error of at most 0.0063.
Values may be sent and summed in bfloat16 or wider, within the bound.
No kernel may reach another device: no remote copies, remote signals or barrier semaphores. Data moves between devices by JAX's collectives and lax.ppermute only.
A program may use at most 256 MiB of HBM per device.

```python
import math
import jax
import jax.numpy as jnp
from jax import lax

IN = 1150
HID = 400
GATES = 1600
SEQ_LEN = 70
SEQS = 512


def draw_lengths(key, part):
    values = jax.random.randint(key, (SEQS,), SEQ_LEN // 2, SEQ_LEN + 1).astype(jnp.int32)
    return values.at[0].set(SEQ_LEN).at[1].set(SEQ_LEN // 2)


def draw_groups(key, part):
    picked = jax.random.randint(key, (SEQS,), 0, 4)
    labels = (picked == 0).astype(jnp.int32)
    return labels.at[0].set(0).at[1].set(1)


def place_ends(result, rng, low, largest):
    shape = result.shape
    index_at = [jax.random.randint(jax.random.fold_in(rng, axis), (), 0, shape[axis]) for axis in range(len(shape))]
    result = result.at[tuple(index_at)].set(low)
    longest = shape.index(max(shape))
    index_at[longest] = (index_at[longest] + 1) % shape[longest]
    return result.at[tuple(index_at)].set(largest)


def steps_of(key, shape, cuts, least, high):
    factor_of = 1.0
    for axis_at, blocks in cuts:
        heights = jax.random.uniform(jax.random.fold_in(jax.random.fold_in(key, 6), axis_at), (blocks,), jnp.float32, least / len(cuts), high / len(cuts))
        factor_of = factor_of * jnp.repeat(jnp.exp(heights), shape[axis_at] // blocks).reshape((-1,) + (1,) * (len(shape) - 1 - axis_at))
    return factor_of


def normal_values(stream_key, extent, spread, limit, pieces=(), held_as=jnp.bfloat16):
    factor_of = steps_of(stream_key, extent, pieces, -0.22, 0.18) if pieces else 1.0
    drawn = jax.random.normal(stream_key, extent, jnp.float32) * spread * factor_of
    return jnp.minimum(jnp.maximum(drawn, -limit), limit).astype(held_as)


def setup_inputs(seed: int = 0) -> dict:
    seeds = jax.random.split(jax.random.key(seed), 11)
    return {
        "tokens": normal_values(seeds[0], (SEQS, SEQ_LEN, IN), 1.0, 6.0, ((0, 8),)),
        "in_mask": place_ends((jax.random.randint(seeds[1], (SEQS, IN), 0, 4) < 3).astype(jnp.int32), jax.random.fold_in(seeds[1], 1), 0, 1),
        "out_mask": place_ends((jax.random.randint(seeds[2], (SEQS, HID), 0, 5) < 3).astype(jnp.int32), jax.random.fold_in(seeds[2], 1), 0, 1),
        "lengths": draw_lengths(jax.random.fold_in(seeds[10], 71), 0),
        "groups": draw_groups(jax.random.fold_in(seeds[10], 71), 0),
        "input_gate_weight": normal_values(seeds[5], (GATES, IN), IN ** -0.5, 0.1875, ((0, 4),)),
        "w_recur": normal_values(seeds[6], (GATES, HID), HID ** -0.5, 0.3125, ((0, 4),)),
        "weight_mask": place_ends((jax.random.randint(seeds[7], (GATES, HID), 0, 2) < 1).astype(jnp.int32), jax.random.fold_in(seeds[7], 1), 0, 1),
        "bias": normal_values(seeds[8], (GATES,), 0.5, 3.0, ((0, 4),), jnp.float32),
        "cotangent": normal_values(seeds[9], (SEQS, SEQ_LEN, HID), 1.0, 6.0, ((0, 8),)),
    }


ACTIVATION_COEF = 2.0
TAR_BETA = 1.0
KEEP_INPUT = 0.75
KEEP_OUTPUT = 0.6
KEEP_WEIGHT = 0.5
HIGHEST = lax.Precision.HIGHEST

@jax.custom_vjp
def low(v):
    return lax.optimization_barrier(v.astype(jnp.bfloat16)).astype(jnp.float32)

@jax.custom_vjp
def low_back(v):
    return v

def low_keep(v):
    return (low(v), None)

def low_pass(kept, grad):
    return (grad,)

def back_keep(v):
    return (v, None)

def back_low(kept, grad):
    return (low(grad),)
low.defvjp(low_keep, low_pass)
low_back.defvjp(back_keep, back_low)

def process_block(tokens_blk, input_gate_weight, w_recur, bias, keep_in, keep_out, w_scale, valid_blk, ratio_blk, group_blk, cot_blk):
    hidden = w_recur.shape[1]
    dropped_weight = low(tokens_blk * keep_in[:, None, :])
    projected = jnp.einsum('blk,gk->lbg', dropped_weight, input_gate_weight, precision=HIGHEST)
    w_eff = w_recur * w_scale

    def forward_step(carry, proj_step):
        cell_state, hidden_low = carry
        pre_act = low_back(proj_step + jnp.dot(hidden_low, w_eff.T, precision=HIGHEST) + bias[None, :])
        gate_input_part = jax.nn.sigmoid(pre_act[:, :hidden])
        gate_forget = jax.nn.sigmoid(pre_act[:, hidden:2 * hidden])
        gate_cell = jnp.tanh(pre_act[:, 2 * hidden:3 * hidden])
        gate_output_part = jax.nn.sigmoid(pre_act[:, 3 * hidden:])
        new_cell = gate_forget * cell_state + gate_input_part * gate_cell
        new_hidden = gate_output_part * jnp.tanh(new_cell)
        return ((new_cell, low(new_hidden)), new_hidden)
    zero_state = jnp.zeros((tokens_blk.shape[0], hidden), jnp.float32)
    _, hidden_seq = lax.scan(jax.checkpoint(forward_step), (zero_state, zero_state), projected)
    outputs = hidden_seq * keep_out[None, :, :]
    valid_time = valid_blk.T
    hidden_prev = jnp.concatenate([zero_state[None], hidden_seq[:-1]], 0)
    later = (jnp.arange(hidden_seq.shape[0]) >= 1).astype(jnp.float32)
    penalty = ACTIVATION_COEF * lax.optimization_barrier(jnp.sum(outputs * outputs, -1))
    penalty = penalty + TAR_BETA * later[:, None] * lax.optimization_barrier(jnp.sum((hidden_seq - hidden_prev) ** 2, -1))
    readout = lax.optimization_barrier(jnp.sum(jnp.swapaxes(cot_blk, 0, 1) * outputs, -1))
    per_seq = lax.optimization_barrier(jnp.sum(valid_time * (readout + ratio_blk[None, :] * penalty), 0))
    return lax.optimization_barrier(jnp.sum(per_seq[:, None] * group_blk, 0))

def reference(tokens, in_mask, out_mask, lengths, groups, input_gate_weight, w_recur, weight_mask, bias, cotangent):
    seq_count, time_steps, width_in = tokens.shape
    hidden = w_recur.shape[1]
    group_hot = (groups[:, None] == jnp.arange(2, dtype=jnp.int32)[None, :]).astype(jnp.float32)
    valid_mask = (jnp.arange(time_steps, dtype=jnp.int32)[None, :] < lengths[:, None]).astype(jnp.float32)
    counts = lax.optimization_barrier(jnp.sum(group_hot * lax.optimization_barrier(jnp.sum(valid_mask, 1))[:, None], 0))
    group_ratio = jnp.sum(counts) / counts
    seq_ratio = lax.optimization_barrier(jnp.sum(group_hot * group_ratio[None, :], 1))
    keep_in = in_mask.astype(jnp.float32) / KEEP_INPUT
    keep_out = out_mask.astype(jnp.float32) / KEEP_OUTPUT
    w_scale = weight_mask.astype(jnp.float32) / KEEP_WEIGHT
    w_in_f = input_gate_weight.astype(jnp.float32)
    w_rec_f = w_recur.astype(jnp.float32)
    block_size = math.gcd(seq_count, 32)
    nblocks = seq_count // block_size

    def blocked(array):
        return array.reshape((nblocks, block_size) + array.shape[1:])
    inputs_all = (blocked(tokens.astype(jnp.float32)), blocked(keep_in), blocked(keep_out), blocked(valid_mask), blocked(seq_ratio), blocked(group_hot), blocked(cotangent.astype(jnp.float32)))

    def one_block(totals, inputs_blk):
        tokens_blk, keep_in_blk, keep_out_blk, valid_blk, ratio_blk, group_blk, cot_blk = inputs_blk

        def forward(tokens_v, w_in_v, recurrent_weight_view, bias_v):
            return process_block(tokens_v, w_in_v, recurrent_weight_view, bias_v, keep_in_blk, keep_out_blk, w_scale, valid_blk, ratio_blk, group_blk, cot_blk)
        loss_pair, pullback = jax.vjp(forward, tokens_blk, w_in_f, w_rec_f, bias)
        grads_zero = pullback(jnp.array([1.0, 0.0], dtype=loss_pair.dtype))
        grads_one = pullback(jnp.array([0.0, 1.0], dtype=loss_pair.dtype))
        new_totals = tuple((total + jnp.stack([first, second]) for total, first, second in zip(totals, grads_zero[1:], grads_one[1:])))
        return (new_totals, grads_zero[0] + grads_one[0])
    init = (jnp.zeros((2,) + input_gate_weight.shape, jnp.float32), jnp.zeros((2,) + w_recur.shape, jnp.float32), jnp.zeros((2,) + bias.shape, jnp.float32))
    totals, token_grads = lax.scan(one_block, init, inputs_all)
    input_grad = token_grads.reshape(seq_count, time_steps, width_in)
    grad_in, grad_rec, grad_bias = totals
    gram = jnp.zeros((2, 2), jnp.float32)
    for member in (grad_in, grad_rec, grad_bias):
        flat = member.reshape(2, -1)
        gram = gram + jnp.einsum('gx,hx->gh', flat, flat, precision=HIGHEST)
    return (input_grad, grad_in, grad_rec, grad_bias, gram)
```

```python
import functools

import jax
import jax.numpy as jnp
from jax import lax
from jax.experimental import pallas as pl
from jax.experimental.pallas import tpu as pltpu
from jax.sharding import PartitionSpec as P

ACTIVATION_COEF = 2.0
TAR_BETA = 1.0
KEEP_INPUT = 0.75
KEEP_OUTPUT = 0.6
KEEP_WEIGHT = 0.5
LANES = 128
VMEM_LIMIT = 56 << 20
BF16 = jnp.bfloat16
F32 = jnp.float32


def ceil_to(value, step):
    return -(-value // step) * step


def flip(block, axis, bit):
    count = lax.axis_size(axis)
    return lax.ppermute(block, axis, [(at, at ^ bit) for at in range(count)])


def butterfly_sum(block, axes):
    for axis in axes:
        count = lax.axis_size(axis)
        if count & (count - 1):
            block = lax.psum(block, axis)
            continue
        bit = 1
        while bit < count:
            block = block + flip(block, axis, bit)
            bit *= 2
    return block


def spread(block, axis):
    count = lax.axis_size(axis)
    copies = jnp.broadcast_to(block[None], (count,) + block.shape)
    return lax.all_to_all(copies, axis, 0, 0, tiled=True)


def sigmoid(value):
    return 0.5 * jnp.tanh(0.5 * value) + 0.5


def forward_kernel(
    hid, drop_ref, win_ref, wrec_ref, act_ref, cell_ref, prev_ref, proj, cell_s, low_s
):
    steps, seqs, width = drop_ref.shape

    @pl.when(pl.program_id(0) == 0)
    def _():
        cell_s[...] = jnp.zeros_like(cell_s)
        low_s[...] = jnp.zeros_like(low_s)

    rows = drop_ref[...].reshape(steps * seqs, width)
    proj[...] = jnp.dot(rows, win_ref[...], preferred_element_type=F32)
    cell = cell_s[...]
    low = low_s[...]
    for k in range(steps):
        prev_ref[k] = low
        pre = proj[k * seqs : (k + 1) * seqs] + jnp.dot(
            low, wrec_ref[...], preferred_element_type=F32
        )
        gate_i = sigmoid(pre[:, :hid])
        gate_f = sigmoid(pre[:, hid : 2 * hid])
        gate_g = jnp.tanh(pre[:, 2 * hid : 3 * hid])
        gate_o = sigmoid(pre[:, 3 * hid :])
        cell = gate_f * cell + gate_i * gate_g
        low = (gate_o * jnp.tanh(cell)).astype(BF16)
        act_ref[k, :, :hid] = gate_i
        act_ref[k, :, hid : 2 * hid] = gate_f
        act_ref[k, :, 2 * hid : 3 * hid] = gate_g
        act_ref[k, :, 3 * hid :] = gate_o
        cell_ref[k] = cell
    cell_s[...] = cell
    low_s[...] = low


def backward_kernel(
    hid,
    act_ref,
    cell_ref,
    before_ref,
    out_before_ref,
    cot_ref,
    scale_ref,
    act_coef_ref,
    smooth_ref,
    length_ref,
    wrec_ref,
    grad_ref,
    cell_grad_s,
    recur_s,
    smooth_s,
):
    steps, seqs, _ = act_ref.shape
    place = pl.program_id(0)
    block = pl.num_programs(0) - 1 - place

    @pl.when(place == 0)
    def _():
        cell_grad_s[...] = jnp.zeros_like(cell_grad_s)
        recur_s[...] = jnp.zeros_like(recur_s)
        smooth_s[...] = jnp.zeros_like(smooth_s)

    inner = (block > 0).astype(F32)
    dcell = cell_grad_s[...]
    recur = recur_s[...]
    smooth_next = smooth_s[...]
    scale = scale_ref[...]
    length = length_ref[...]
    cell = cell_ref[steps - 1]
    tanh_cell = jnp.tanh(cell)
    gate_o = act_ref[steps - 1, :, 3 * hid :]
    hidden = gate_o * tanh_cell
    for k in range(steps - 1, -1, -1):
        if k > 0:
            cell_before = cell_ref[k - 1]
            out_before = act_ref[k - 1, :, 3 * hid :]
        else:
            cell_before = before_ref[0] * inner
            out_before = out_before_ref[0]
        tanh_before = jnp.tanh(cell_before)
        hidden_before = out_before * tanh_before
        gate_i = act_ref[k, :, :hid]
        gate_f = act_ref[k, :, hid : 2 * hid]
        gate_g = act_ref[k, :, 2 * hid : 3 * hid]
        valid = length > block * steps + k
        smooth = smooth_ref[...] * (hidden - hidden_before)
        if k == 0:
            smooth = smooth * inner
        smooth = jnp.where(valid, smooth, 0.0)
        cot = cot_ref[k].astype(F32)
        direct = jnp.where(valid, scale * cot + act_coef_ref[...] * hidden, 0.0)
        dhidden = direct + smooth - smooth_next + recur
        smooth_next = smooth
        dcell = dcell + dhidden * gate_o * (1.0 - tanh_cell * tanh_cell)
        grad_ref[k, :, :hid] = (dcell * gate_g * gate_i * (1.0 - gate_i)).astype(BF16)
        grad_ref[k, :, hid : 2 * hid] = (dcell * cell_before * gate_f * (1.0 - gate_f)).astype(BF16)
        grad_ref[k, :, 2 * hid : 3 * hid] = (dcell * gate_i * (1.0 - gate_g * gate_g)).astype(BF16)
        grad_ref[k, :, 3 * hid :] = (dhidden * tanh_cell * gate_o * (1.0 - gate_o)).astype(BF16)
        dcell = dcell * gate_f
        recur = jnp.dot(grad_ref[k], wrec_ref[...], preferred_element_type=F32)
        tanh_cell = tanh_before
        hidden = hidden_before
        gate_o = out_before
    cell_grad_s[...] = dcell
    recur_s[...] = recur
    smooth_s[...] = smooth_next


def weight_kernel(rows_ref, drop_ref, prev_ref, pick_ref, in_ref, rec_ref):
    steps, seqs, own = rows_ref.shape

    @pl.when(pl.program_id(0) == 0)
    def _():
        in_ref[...] = jnp.zeros_like(in_ref)
        rec_ref[...] = jnp.zeros_like(rec_ref)

    grads = rows_ref[...]
    first = (grads * pick_ref[...][None]).reshape(steps * seqs, own)
    second = grads.reshape(steps * seqs, own) - first
    drop = drop_ref[...].reshape(steps * seqs, drop_ref.shape[2])
    prev = prev_ref[...].reshape(steps * seqs, prev_ref.shape[2])
    over = (((0,), (0,)), ((), ()))
    for at, part in enumerate((first, second)):
        in_ref[at] += lax.dot_general(part, drop, over, preferred_element_type=F32)
        rec_ref[at] += lax.dot_general(part, prev, over, preferred_element_type=F32)


def params(count=1):
    return pltpu.CompilerParams(
        dimension_semantics=("arbitrary",) * count, vmem_limit_bytes=VMEM_LIMIT
    )


def block_steps(time_steps, most):
    return max(s for s in range(1, most + 1) if time_steps % s == 0)


def local(
    tokens,
    in_mask,
    out_mask,
    lengths,
    groups,
    input_gate_weight,
    w_recur,
    weight_mask,
    bias,
    cotangent,
):
    seq_count, time_steps, width_in = tokens.shape
    hidden = cotangent.shape[2]
    row_count = input_gate_weight.shape[0]
    row_at = lax.axis_index("row")
    grp_at = lax.axis_index("grp")
    seq_at = lax.axis_index("seq")
    rows_n, grp_n, seq_n = (lax.axis_size(a) for a in ("row", "grp", "seq"))
    gates = rows_n * row_count
    hid = ceil_to(hidden, LANES)
    wide = ceil_to(width_in + 2, LANES)
    share = seq_count // rows_n
    pieces = grp_n * seq_n

    w_scale = weight_mask.astype(F32) / KEEP_WEIGHT
    w_eff = (w_recur.astype(F32) * w_scale).astype(BF16)
    bias_high = bias.astype(BF16)
    bias_low = (bias - bias_high.astype(F32)).astype(BF16)
    own_weights = jnp.concatenate(
        [input_gate_weight, bias_high[:, None], bias_low[:, None], w_eff], 1
    )
    piece_rows = ceil_to(row_count, pieces) // pieces
    padded = jnp.pad(own_weights, ((0, pieces * piece_rows - row_count), (0, 0)))
    mine = lax.dynamic_slice_in_dim(padded, (grp_at * seq_n + seq_at) * piece_rows, piece_rows, 0)
    got = spread(mine, "row")
    got = spread(got, "seq")
    got = spread(got, "grp")
    got = got.reshape(grp_n * seq_n, rows_n, piece_rows, -1)
    whole = jnp.swapaxes(got, 0, 1).reshape(rows_n, pieces * piece_rows, -1)[:, :row_count]
    whole = whole.reshape(4, hidden, -1)
    whole = jnp.pad(whole, ((0, 0), (0, hid - hidden), (0, 0))).reshape(4 * hid, -1)
    w_in = whole[:, : width_in + 2]
    w_rec = jnp.pad(whole[:, width_in + 2 :], ((0, 0), (0, hid - hidden)))
    w_in_t = jnp.pad(w_in.T, ((0, wide - width_in - 2), (0, 0)))
    w_rec_t = w_rec.T

    in_scale = in_mask.astype(F32) / KEEP_INPUT
    tok_time = jnp.swapaxes(tokens, 0, 1)
    dropped = (tok_time.astype(F32) * in_scale[None]).astype(BF16)
    dropped = jnp.concatenate(
        [
            dropped,
            jnp.ones((time_steps, seq_count, 2), BF16),
            jnp.zeros((time_steps, seq_count, wide - width_in - 2), BF16),
        ],
        2,
    )
    cot_time = jnp.pad(jnp.swapaxes(cotangent, 0, 1), ((0, 0), (0, 0), (0, hid - hidden)))

    group_hot = (groups[:, None] == jnp.arange(2)[None, :]).astype(F32)
    valid_count = jnp.clip(lengths, 0, time_steps).astype(F32)
    local_counts = jnp.sum(group_hot * valid_count[:, None], 0)
    counts = butterfly_sum(local_counts, ("grp", "seq"))
    group_ratio = jnp.sum(counts) / counts
    seq_ratio = jnp.sum(group_hot * group_ratio[None, :], 1)
    out_scale = jnp.pad(out_mask.astype(F32) / KEEP_OUTPUT, ((0, 0), (0, hid - hidden)))
    act_coef = 2.0 * ACTIVATION_COEF * seq_ratio[:, None] * out_scale * out_scale
    smooth_coef = jnp.broadcast_to(2.0 * TAR_BETA * seq_ratio[:, None], (seq_count, hid))
    length_wide = jnp.broadcast_to(lengths[:, None], (seq_count, hid))

    steps = block_steps(time_steps, 7)
    blocks = time_steps // steps

    def at_time(width, order=lambda b: b):
        return pl.BlockSpec((steps, seq_count, width), lambda b: (order(b), 0, 0))

    def fixed(*shape):
        return pl.BlockSpec(shape, lambda b: (0,) * len(shape))

    acts, cells, prev_low = pl.pallas_call(
        functools.partial(forward_kernel, hid),
        grid=(blocks,),
        in_specs=[at_time(wide), fixed(wide, 4 * hid), fixed(hid, 4 * hid)],
        out_specs=[at_time(4 * hid), at_time(hid), at_time(hid)],
        out_shape=[
            jax.ShapeDtypeStruct((time_steps, seq_count, 4 * hid), F32),
            jax.ShapeDtypeStruct((time_steps, seq_count, hid), F32),
            jax.ShapeDtypeStruct((time_steps, seq_count, hid), BF16),
        ],
        scratch_shapes=[
            pltpu.VMEM((steps * seq_count, 4 * hid), F32),
            pltpu.VMEM((seq_count, hid), F32),
            pltpu.VMEM((seq_count, hid), BF16),
        ],
        compiler_params=params(),
        name="forward",
    )(dropped, w_in_t, w_rec_t)

    def back(b):
        return blocks - 1 - b

    def before(b):
        return jnp.maximum(back(b) * steps - 1, 0)

    grads = pl.pallas_call(
        functools.partial(backward_kernel, hid),
        grid=(blocks,),
        in_specs=[
            at_time(4 * hid, back),
            at_time(hid, back),
            pl.BlockSpec((1, seq_count, hid), lambda b: (before(b), 0, 0)),
            pl.BlockSpec((1, seq_count, hid), lambda b: (before(b), 0, 3)),
            at_time(hid, back),
            fixed(seq_count, hid),
            fixed(seq_count, hid),
            fixed(seq_count, hid),
            fixed(seq_count, hid),
            fixed(4 * hid, hid),
        ],
        out_specs=at_time(4 * hid, back),
        out_shape=jax.ShapeDtypeStruct((time_steps, seq_count, 4 * hid), BF16),
        scratch_shapes=[pltpu.VMEM((seq_count, hid), F32)] * 3,
        compiler_params=params(),
        name="backward",
    )(
        acts,
        cells,
        cells,
        acts,
        cot_time,
        out_scale,
        act_coef,
        smooth_coef,
        length_wide,
        w_rec,
    )

    if row_count == hidden:
        own_rows = lax.dynamic_slice_in_dim(grads, row_at * hid, hid, 2)
    else:
        packed = grads.reshape(time_steps, seq_count, 4, hid)[..., :hidden]
        packed = packed.reshape(time_steps, seq_count, gates)
        own_rows = lax.dynamic_slice_in_dim(packed, row_at * row_count, row_count, 2)
        own_rows = jnp.pad(own_rows, ((0, 0), (0, 0), (0, -row_count % LANES)))
    own_wide = own_rows.shape[2]
    pick = jnp.broadcast_to((groups == 0).astype(BF16)[:, None], (seq_count, own_wide))
    part_in, part_rec = pl.pallas_call(
        weight_kernel,
        grid=(blocks,),
        in_specs=[
            at_time(own_wide),
            at_time(wide),
            at_time(hid),
            fixed(seq_count, own_wide),
        ],
        out_specs=[fixed(2, own_wide, wide), fixed(2, own_wide, hid)],
        out_shape=[
            jax.ShapeDtypeStruct((2, own_wide, wide), F32),
            jax.ShapeDtypeStruct((2, own_wide, hid), F32),
        ],
        compiler_params=params(),
        name="weights",
    )(own_rows, dropped, prev_low, pick)

    def split(block):
        total = jnp.concatenate(
            [block[0][:, : width_in + 1], block[1][:, :hidden] * w_scale], 1
        )
        return total

    def group_part(at):
        return split(
            (
                lax.dynamic_index_in_dim(part_in, at, 0, False)[:row_count],
                lax.dynamic_index_in_dim(part_rec, at, 0, False)[:row_count],
            )
        )

    other = flip(group_part(1 - grp_at).astype(BF16), "grp", 1)
    summed = group_part(grp_at) + other.astype(F32)
    columns = summed.shape[1]
    part_rows = ceil_to(row_count, seq_n) // seq_n
    summed = jnp.pad(summed, ((0, seq_n * part_rows - row_count), (0, 0)))
    sent = lax.all_to_all(
        summed.astype(BF16).reshape(seq_n, part_rows, columns), "seq", 0, 0, tiled=True
    )
    total = jnp.sum(sent.astype(F32), 0)
    total_low = total.astype(BF16)
    everyone = spread(total_low, "seq").reshape(seq_n * part_rows, columns)[:row_count]
    everyone = everyone.astype(F32)
    peer = flip(total_low, "grp", 1).astype(F32)
    self_dot = jnp.sum(total * total)
    cross_dot = jnp.sum(total * peer)
    mine_hot = (jnp.arange(2) == grp_at).astype(F32)
    local_gram = (
        mine_hot[:, None] * mine_hot[None, :] * self_dot
        + mine_hot[:, None] * (1.0 - mine_hot)[None, :] * cross_dot
    )
    gram = butterfly_sum(local_gram, ("grp", "seq", "row"))

    own_seqs = lax.dynamic_slice_in_dim(grads, row_at * share, share, 1)
    own_scale = lax.dynamic_slice_in_dim(in_scale, row_at * share, share, 0)
    input_time = jnp.einsum(
        "tsr,rk->tsk", own_seqs, w_in[:, :width_in], preferred_element_type=F32
    )
    input_grad = jnp.swapaxes(input_time * own_scale[None], 0, 1)
    return (
        input_grad,
        everyone[None, :, :width_in],
        everyone[None, :, width_in + 1 :],
        everyone[None, :, width_in],
        gram,
    )


def solution(mesh):
    return jax.shard_map(
        local,
        mesh=mesh,
        in_specs=(
            P(("grp", "seq"), None, None),
            P(("grp", "seq"), None),
            P(("grp", "seq"), None),
            P(("grp", "seq")),
            P(("grp", "seq")),
            P("row", None),
            P("row", None),
            P("row", None),
            P("row"),
            P(("grp", "seq"), None, None),
        ),
        out_specs=(
            P(("grp", "seq", "row"), None, None),
            P("grp", "row", None),
            P("grp", "row", None),
            P("grp", "row"),
            P(),
        ),
        check_vma=False,
    )
```

```python
import functools

import jax
import jax.numpy as jnp
from jax import lax
from jax.experimental import pallas as pl
from jax.experimental.pallas import tpu as pltpu
from jax.sharding import PartitionSpec as P

ACTIVATION_COEF = 2.0
TAR_BETA = 1.0
KEEP_INPUT = 0.75
KEEP_OUTPUT = 0.6
KEEP_WEIGHT = 0.5
LANES = 128
TILE = 256
VMEM_LIMIT = 58 << 20
BF16 = jnp.bfloat16
F32 = jnp.float32
OVER_ROWS = (((0,), (0,)), ((), ()))


def ceil_to(value, step):
    return -(-value // step) * step


def dot(left, right):
    return jnp.dot(left, right, preferred_element_type=F32)


def flip(block, axis, bit):
    count = lax.axis_size(axis)
    return lax.ppermute(block, axis, [(at, at ^ bit) for at in range(count)])


def butterfly_sum(block, axes):
    for axis in axes:
        count = lax.axis_size(axis)
        if count & (count - 1):
            block = lax.psum(block, axis)
            continue
        bit = 1
        while bit < count:
            block = block + flip(block, axis, bit)
            bit *= 2
    return block


def sigmoid(value):
    return 0.5 * jnp.tanh(0.5 * value) + 0.5


class Columns:
    def __init__(self, hidden):
        self.hidden = hidden
        self.full = hidden // LANES
        self.rest = hidden - self.full * LANES
        assert 0 < 4 * self.rest <= LANES
        self.total = 4 * hidden
        self.order = (self.full,) + tuple(range(self.full))

    def units(self, j):
        return j * LANES, min((j + 1) * LANES, self.hidden)

    def gates(self, j):
        return 4 * j * LANES, min(4 * (j + 1) * LANES, self.total)

    def gate(self, j, q):
        width = LANES if j < self.full else self.rest
        start = 4 * j * LANES + q * width
        return start, start + width

    def pack(self, gated):
        parts = []
        for j in range(self.full + 1):
            first, last = self.units(j)
            parts.append(gated[:, first:last].reshape((-1,) + gated.shape[2:]))
        return jnp.concatenate(parts, 0)

    def unpack_lanes(self, packed):
        parts = []
        for q in range(4):
            for j in range(self.full + 1):
                first, last = self.gate(j, q)
                parts.append(packed[..., first:last])
        return jnp.concatenate(parts, -1)


def drop_kernel(width, tok_ref, scale_ref, drop_ref):
    scale = scale_ref[...]
    for k in range(tok_ref.shape[0]):
        drop_ref[k, :, :width] = (tok_ref[k].astype(F32) * scale).astype(BF16)
        drop_ref[k, :, width:] = jnp.ones_like(drop_ref[k, :, width:])


def order_kernel(place_ref, *refs):
    *pieces, turned_ref, plain_ref, rows = refs
    wide = turned_ref.shape[0] - plain_ref.shape[1]
    hidden = turned_ref.shape[1]
    count = pieces[0].shape[0]
    step = rows.shape[0] // len(pieces)
    rows[...] = jnp.zeros_like(rows)
    unit = lax.broadcasted_iota(jnp.int32, (step, hidden), 1)
    line = lax.broadcasted_iota(jnp.int32, (step, hidden), 0)
    hot = []
    for at, piece in enumerate(pieces):
        rows[at * step : at * step + count] = piece[...]
        here = (unit == line + place_ref[at] * count) & (line < count)
        hot.append(here.astype(F32).astype(BF16))
    hot = jnp.concatenate(hot, 0)
    turned_ref[...] = lax.dot_general(
        rows[...], hot, OVER_ROWS, preferred_element_type=F32
    ).astype(BF16)
    plain_ref[...] = lax.dot_general(
        hot, rows[:, wide:], OVER_ROWS, preferred_element_type=F32
    ).astype(BF16)


def pack_kernel(cols, row_ref, *refs):
    turned, plain, (win_ref, rec_turned_ref, rec_ref) = refs[:4], refs[4:8], refs[8:]
    wide = win_ref.shape[0]
    for k in range(4):
        for q in range(4):

            @pl.when(row_ref[0] ^ k == q)
            def _():
                for j in range(cols.full + 1):
                    first, last = cols.units(j)
                    low, high = cols.gate(j, q)
                    win_ref[:, low:high] = turned[k][:wide, first:last]
                    rec_turned_ref[:, low:high] = turned[k][wide:, first:last]
                    rec_ref[low:high] = plain[k][first:last]


def forward_kernel(
    cols,
    sub,
    first_ref,
    second_ref,
    third_ref,
    win_ref,
    rec_ref,
    act_ref,
    cell_ref,
    prev_ref,
    even,
    odd,
    cell_s,
    low_s,
):
    seqs, width = first_ref.shape[1:]
    steps = act_ref.shape[0]
    hidden = cols.hidden

    @pl.when(pl.program_id(0) == 0)
    def _():
        cell_s[...] = jnp.zeros_like(cell_s)
        low_s[...] = jnp.zeros_like(low_s)
        even[...] = dot(first_ref[...].reshape(sub * seqs, width), win_ref[...])

    lane = lax.broadcasted_iota(jnp.int32, (1, 4 * cols.rest), 1)
    tanh_lane = (lane >= 2 * cols.rest) & (lane < 3 * cols.rest)
    rest_mul = jnp.where(tanh_lane, 1.0, 0.5)
    rest_add = jnp.where(tanh_lane, 0.0, 0.5)
    spans = [cols.units(j) for j in range(cols.full + 1)]
    cells = [cell_s[:, a:b] for a, b in spans]
    lows = [low_s[:, a:b] for a, b in spans]
    chunk = ceil_to(-(-cols.total // sub), TILE)
    for k in range(steps):
        u, v = divmod(k, sub)
        now, later = (even, odd) if u % 2 == 0 else (odd, even)
        start, stop = chunk * v, min(chunk * (v + 1), cols.total)
        if start < stop:
            rows = (second_ref, third_ref)[u][...].reshape(sub * seqs, width)
            later[:, start:stop] = dot(rows, win_ref[:, start:stop])
        for (a, b), low in zip(spans, lows):
            prev_ref[k, :, a:b] = low
        low = jnp.concatenate(lows, 1)
        lows = [None] * len(spans)
        for j in cols.order:
            first, last = cols.gates(j)
            pre = now[v * seqs : (v + 1) * seqs, first:last] + dot(low, rec_ref[:, first:last])
            if j < cols.full:
                gate_i, gate_f, gate_g, gate_o = (
                    pre[:, q * LANES : (q + 1) * LANES] for q in range(4)
                )
                gate_i, gate_f, gate_o = sigmoid(gate_i), sigmoid(gate_f), sigmoid(gate_o)
                gate_g = jnp.tanh(gate_g)
                for q, gate in enumerate((gate_i, gate_f, gate_g, gate_o)):
                    a, b = cols.gate(j, q)
                    act_ref[k, :, a:b] = gate
            else:
                act = rest_mul * jnp.tanh(rest_mul * pre) + rest_add
                act_ref[k, :, first:last] = act
                gate_i, gate_f, gate_g, gate_o = (
                    act[:, q * cols.rest : (q + 1) * cols.rest] for q in range(4)
                )
            a, b = spans[j]
            cells[j] = gate_f * cells[j] + gate_i * gate_g
            cell_ref[k, :, a:b] = cells[j]
            lows[j] = (gate_o * jnp.tanh(cells[j])).astype(BF16)
    for j, (a, b) in enumerate(spans):
        cell_s[:, a:b] = cells[j]
        low_s[:, a:b] = lows[j]


def backward_kernel(
    cols,
    own,
    row_ref,
    act_ref,
    cell_ref,
    before_ref,
    act_before_ref,
    cot_ref,
    scale_ref,
    coef_ref,
    smooth_ref,
    length_ref,
    rec_ref,
    grad_ref,
    *refs,
):
    own_ref = refs[0] if own else None
    cell_grad_s, recur_s, smooth_s = refs[-3:]
    steps = act_ref.shape[0]
    place = pl.program_id(0)
    block = pl.num_programs(0) - 1 - place

    @pl.when(place == 0)
    def _():
        cell_grad_s[...] = jnp.zeros_like(cell_grad_s)
        recur_s[...] = jnp.zeros_like(recur_s)
        smooth_s[...] = jnp.zeros_like(smooth_s)

    inner = (block > 0).astype(F32)
    spans = [cols.units(j) for j in range(cols.full + 1)]

    def gates_at(ref, k, j):
        if j < cols.full:
            return [ref[k, :, a:b] for a, b in (cols.gate(j, q) for q in range(4))]
        first, last = cols.gates(j)
        packed = ref[k, :, first:last]
        return [packed[:, q * cols.rest : (q + 1) * cols.rest] for q in range(4)]

    blocks = range(cols.full + 1)
    dcell = [cell_grad_s[:, a:b] for a, b in spans]
    recur = [recur_s[:, a:b] for a, b in spans]
    smooth_next = [smooth_s[:, a:b] for a, b in spans]
    gates = [gates_at(act_ref, steps - 1, j) for j in blocks]
    tanh_cell = [jnp.tanh(cell_ref[steps - 1, :, a:b]) for a, b in spans]
    hidden = [gates[j][3] * tanh_cell[j] for j in blocks]
    for k in range(steps - 1, -1, -1):
        parts = [None] * len(spans)
        for j in cols.order:
            a, b = spans[j]
            gate_i, gate_f, gate_g, gate_o = gates[j]
            if k > 0:
                cell_before = cell_ref[k - 1, :, a:b]
                gates[j] = gates_at(act_ref, k - 1, j)
            else:
                cell_before = before_ref[0, :, a:b] * inner
                gates[j] = gates_at(act_before_ref, 0, j)
            tanh_before = jnp.tanh(cell_before)
            hidden_before = gates[j][3] * tanh_before
            valid = length_ref[:, a:b] > block * steps + k
            smooth = smooth_ref[:, a:b] * (hidden[j] - hidden_before)
            if k == 0:
                smooth = smooth * inner
            smooth = jnp.where(valid, smooth, 0.0)
            direct = scale_ref[:, a:b] * cot_ref[k, :, a:b].astype(F32) + coef_ref[:, a:b] * hidden[j]
            direct = jnp.where(valid, direct, 0.0) + smooth - smooth_next[j]
            smooth_next[j] = smooth
            dhidden = direct + recur[j]
            total = dcell[j] + dhidden * (gate_o * (1.0 - tanh_cell[j] * tanh_cell[j]))
            grads = [
                (total * (gate_g * gate_i * (1.0 - gate_i))).astype(BF16),
                (total * (cell_before * gate_f * (1.0 - gate_f))).astype(BF16),
                (total * (gate_i * (1.0 - gate_g * gate_g))).astype(BF16),
                (dhidden * (tanh_cell[j] * gate_o * (1.0 - gate_o))).astype(BF16),
            ]
            parts[j] = jnp.concatenate(grads, 1)
            first, last = cols.gates(j)
            grad_ref[k, :, first:last] = parts[j]
            if own:
                mine = grads[3]
                for q in range(3):
                    mine = jnp.where(row_ref[0] == q, grads[q], mine)
                own_ref[k, :, a:b] = mine
            dcell[j] = total * gate_f
            tanh_cell[j] = tanh_before
            hidden[j] = hidden_before
        back = dot(jnp.concatenate(parts, 1), rec_ref[...])
        recur = [back[:, a:b] for a, b in spans]
    for j, (a, b) in enumerate(spans):
        cell_grad_s[:, a:b] = dcell[j]
        recur_s[:, a:b] = recur[j]
        smooth_s[:, a:b] = smooth_next[j]


def weight_kernel(grp_ref, rows_ref, drop_ref, prev_ref, pick_ref, keep_ref, send_ref, sums):
    steps, seqs, own = rows_ref.shape
    width = drop_ref.shape[2]
    place = pl.program_id(0)

    @pl.when(place == 0)
    def _():
        sums[...] = jnp.zeros_like(sums)

    grads = rows_ref[...]
    first = (grads * pick_ref[...][None]).reshape(steps * seqs, own)
    second = grads.reshape(steps * seqs, own) - first
    drop = drop_ref[...].reshape(steps * seqs, width)
    prev = prev_ref[...].reshape(steps * seqs, prev_ref.shape[2])
    for at, part in enumerate((first, second)):
        sums[at, :, :width] += lax.dot_general(part, drop, OVER_ROWS, preferred_element_type=F32)
        sums[at, :, width:] += lax.dot_general(part, prev, OVER_ROWS, preferred_element_type=F32)

    @pl.when(place == pl.num_programs(0) - 1)
    def _():
        keep_ref[...] = sums[grp_ref[0]]
        send_ref[...] = sums[1 - grp_ref[0]].astype(BF16)


def params():
    return pltpu.CompilerParams(
        dimension_semantics=("arbitrary",), vmem_limit_bytes=VMEM_LIMIT
    )


def fixed(*shape):
    return pl.BlockSpec(shape, lambda *_: (0,) * len(shape))


def gather_shards(own_weights, cols, wide, row_at, grp_at, seq_at):
    hidden, rows_n = cols.hidden, lax.axis_size("row")
    grp_n, seq_n = lax.axis_size("grp"), lax.axis_size("seq")
    count = own_weights.shape[0]
    pieces = grp_n * seq_n
    if rows_n != 4 or grp_n != 2 or seq_n != 4 or count != hidden or count % pieces:
        whole = lax.all_gather(own_weights, "row", axis=0, tiled=True)
        packed = cols.pack(whole.reshape(4, hidden, -1))
        return packed[:, :wide].T, packed[:, wide:].T, packed[:, wide:]
    size = count // pieces
    split = own_weights.reshape(pieces, size, -1)
    mine = lax.dynamic_index_in_dim(split, grp_at * seq_n + seq_at, 0, False)
    sets = [[split[at] for at in range(pieces)]]
    places = [jnp.arange(pieces, dtype=jnp.int32)]
    steps = jnp.arange(seq_n, dtype=jnp.int32)
    relative = jnp.concatenate(
        [(grp_at ^ at) * seq_n + (seq_at ^ steps) for at in range(grp_n)]
    )
    for k in range(1, rows_n):
        here = flip(mine, "row", k)
        by_one = flip(here, "seq", 1)
        by_two = flip(here, "seq", 2)
        by_three = (
            flip(by_one, "seq", 2) if k == 1 else flip(by_two, "seq", 1) if k == 2 else flip(here, "seq", 3)
        )
        four = jnp.stack([here, by_one, by_two, by_three])
        other = flip(four, "grp", 1)
        sets.append([here, by_one, by_two, by_three] + [other[at] for at in range(seq_n)])
        places.append(relative)
    turned, plain = [], []
    for arrays, place in zip(sets, places):
        one, two = pl.pallas_call(
            order_kernel,
            grid_spec=pltpu.PrefetchScalarGridSpec(
                num_scalar_prefetch=1,
                grid=(1,),
                in_specs=[fixed(*a.shape) for a in arrays],
                out_specs=[fixed(wide + hidden, hidden), fixed(hidden, hidden)],
                scratch_shapes=[pltpu.VMEM((pieces * ceil_to(size, 64), wide + hidden), BF16)],
            ),
            out_shape=[
                jax.ShapeDtypeStruct((wide + hidden, hidden), BF16),
                jax.ShapeDtypeStruct((hidden, hidden), BF16),
            ],
            compiler_params=params(),
            name="order",
        )(place, *arrays)
        turned.append(one)
        plain.append(two)
    return pl.pallas_call(
        functools.partial(pack_kernel, cols),
        grid_spec=pltpu.PrefetchScalarGridSpec(
            num_scalar_prefetch=1,
            grid=(1,),
            in_specs=[fixed(*a.shape) for a in turned + plain],
            out_specs=[
                fixed(wide, cols.total),
                fixed(hidden, cols.total),
                fixed(cols.total, hidden),
            ],
        ),
        out_shape=[
            jax.ShapeDtypeStruct((wide, cols.total), BF16),
            jax.ShapeDtypeStruct((hidden, cols.total), BF16),
            jax.ShapeDtypeStruct((cols.total, hidden), BF16),
        ],
        compiler_params=params(),
        name="pack",
    )(row_at[None], *turned, *plain)


def local(
    tokens,
    in_mask,
    out_mask,
    lengths,
    groups,
    input_gate_weight,
    w_recur,
    weight_mask,
    bias,
    cotangent,
):
    seq_count, time_steps, width_in = tokens.shape
    hidden = cotangent.shape[2]
    row_count = input_gate_weight.shape[0]
    row_at = lax.axis_index("row")
    grp_at = lax.axis_index("grp")
    seq_at = lax.axis_index("seq")
    rows_n, seq_n = lax.axis_size("row"), lax.axis_size("seq")
    cols = Columns(hidden)
    wide = ceil_to(width_in + 2, LANES)
    share = seq_count // rows_n

    w_scale = weight_mask.astype(F32) / KEEP_WEIGHT
    w_eff = (w_recur.astype(F32) * w_scale).astype(BF16)
    bias_high = bias.astype(BF16)
    bias_low = (bias - bias_high.astype(F32)).astype(BF16)
    own_weights = jnp.concatenate(
        [
            input_gate_weight,
            bias_high[:, None],
            bias_low[:, None],
            jnp.zeros((row_count, wide - width_in - 2), BF16),
            w_eff,
        ],
        1,
    )
    w_in, w_rec_turned, w_rec = gather_shards(own_weights, cols, wide, row_at, grp_at, seq_at)

    sub = max(s for s in range(1, 8) if time_steps % (2 * s) == 0)
    steps = 2 * sub
    blocks = time_steps // steps

    def at_time(width):
        return pl.BlockSpec((steps, seq_count, width), lambda b, *_: (b, 0, 0))

    in_scale = in_mask.astype(F32) / KEEP_INPUT
    dropped = pl.pallas_call(
        functools.partial(drop_kernel, width_in),
        grid=(blocks,),
        in_specs=[at_time(width_in), fixed(seq_count, width_in)],
        out_specs=at_time(wide),
        out_shape=jax.ShapeDtypeStruct((time_steps, seq_count, wide), BF16),
        compiler_params=params(),
        name="drop",
    )(jnp.swapaxes(tokens, 0, 1), in_scale)
    cot_time = jnp.swapaxes(cotangent, 0, 1)

    group_hot = (groups[:, None] == jnp.arange(2)[None, :]).astype(F32)
    valid_count = jnp.clip(lengths, 0, time_steps).astype(F32)
    local_counts = jnp.sum(group_hot * valid_count[:, None], 0)
    counts = butterfly_sum(local_counts, ("grp", "seq"))
    group_ratio = jnp.sum(counts) / counts
    seq_ratio = jnp.sum(group_hot * group_ratio[None, :], 1)
    out_scale = out_mask.astype(F32) / KEEP_OUTPUT
    act_coef = 2.0 * ACTIVATION_COEF * seq_ratio[:, None] * out_scale * out_scale
    smooth_coef = jnp.broadcast_to(2.0 * TAR_BETA * seq_ratio[:, None], (seq_count, hidden))
    length_wide = jnp.broadcast_to(lengths[:, None], (seq_count, hidden))

    acts, cells, prev_low = pl.pallas_call(
        functools.partial(forward_kernel, cols, sub),
        grid=(blocks,),
        in_specs=[
            fixed(sub, seq_count, wide),
            pl.BlockSpec((sub, seq_count, wide), lambda b: (2 * b + 1, 0, 0)),
            pl.BlockSpec(
                (sub, seq_count, wide), lambda b: (jnp.minimum(2 * b + 2, 2 * blocks - 1), 0, 0)
            ),
            fixed(wide, cols.total),
            fixed(hidden, cols.total),
        ],
        out_specs=[at_time(cols.total), at_time(hidden), at_time(hidden)],
        out_shape=[
            jax.ShapeDtypeStruct((time_steps, seq_count, cols.total), F32),
            jax.ShapeDtypeStruct((time_steps, seq_count, hidden), F32),
            jax.ShapeDtypeStruct((time_steps, seq_count, hidden), BF16),
        ],
        scratch_shapes=[
            pltpu.VMEM((sub * seq_count, cols.total), F32),
            pltpu.VMEM((sub * seq_count, cols.total), F32),
            pltpu.VMEM((seq_count, hidden), F32),
            pltpu.VMEM((seq_count, hidden), BF16),
        ],
        compiler_params=params(),
        name="forward",
    )(dropped, dropped, dropped, w_in, w_rec_turned)

    def back(b):
        return 2 * blocks - 1 - b

    def before(width):
        return pl.BlockSpec(
            (1, seq_count, width), lambda b, *_: (jnp.maximum(back(b) * sub - 1, 0), 0, 0)
        )

    def back_time(width):
        return pl.BlockSpec((sub, seq_count, width), lambda b, *_: (back(b), 0, 0))

    own = row_count == hidden
    grad_specs = [back_time(cols.total)] + [back_time(hidden)] * own
    grad_shapes = [cols.total] + [hidden] * own
    grads, *own_rows = pl.pallas_call(
        functools.partial(backward_kernel, cols, own),
        grid_spec=pltpu.PrefetchScalarGridSpec(
            num_scalar_prefetch=1,
            grid=(2 * blocks,),
            in_specs=[
                back_time(cols.total),
                back_time(hidden),
                before(hidden),
                before(cols.total),
                back_time(hidden),
                fixed(seq_count, hidden),
                fixed(seq_count, hidden),
                fixed(seq_count, hidden),
                fixed(seq_count, hidden),
                fixed(cols.total, hidden),
            ],
            out_specs=grad_specs,
            scratch_shapes=[pltpu.VMEM((seq_count, hidden), F32)] * 3,
        ),
        out_shape=[
            jax.ShapeDtypeStruct((time_steps, seq_count, width), BF16) for width in grad_shapes
        ],
        compiler_params=params(),
        name="backward",
    )(
        row_at[None],
        acts,
        cells,
        cells,
        acts,
        cot_time,
        out_scale,
        act_coef,
        smooth_coef,
        length_wide,
        w_rec,
    )

    if own:
        own_rows = own_rows[0]
    else:
        own_rows = lax.dynamic_slice_in_dim(
            cols.unpack_lanes(grads), row_at * row_count, row_count, 2
        )
    pick = jnp.broadcast_to((groups == 0).astype(BF16)[:, None], (seq_count, row_count))
    columns = wide + hidden
    keep, send = pl.pallas_call(
        weight_kernel,
        grid_spec=pltpu.PrefetchScalarGridSpec(
            num_scalar_prefetch=1,
            grid=(blocks,),
            in_specs=[
                at_time(row_count),
                at_time(wide),
                at_time(hidden),
                fixed(seq_count, row_count),
            ],
            out_specs=[fixed(row_count, columns)] * 2,
            scratch_shapes=[pltpu.VMEM((2, row_count, columns), F32)],
        ),
        out_shape=[
            jax.ShapeDtypeStruct((row_count, columns), F32),
            jax.ShapeDtypeStruct((row_count, columns), BF16),
        ],
        compiler_params=params(),
        name="weights",
    )(grp_at[None], own_rows, dropped, prev_low, pick)

    part_rows = ceil_to(row_count, seq_n) // seq_n
    spare = ((0, seq_n * part_rows - row_count), (0, 0))
    summed = jnp.pad(keep + flip(send, "grp", 1).astype(F32), spare)
    summed = summed.reshape(seq_n, part_rows, columns)
    summed_low = summed.astype(BF16)
    total = lax.dynamic_index_in_dim(summed, seq_at, 0, False)
    for bit in range(1, seq_n):
        piece = lax.dynamic_index_in_dim(summed_low, seq_at ^ bit, 0, False)
        total = total + flip(piece, "seq", bit).astype(F32)
    scale_part = jnp.pad(w_scale, spare).reshape(seq_n, part_rows, hidden)
    scale_part = lax.dynamic_index_in_dim(scale_part, seq_at, 0, False)
    total = jnp.concatenate(
        [total[:, : width_in + 1], total[:, wide:] * scale_part], 1
    )
    total_low = total.astype(BF16)
    peer = flip(total_low, "grp", 1).astype(F32)
    relative = [total_low] + [flip(total_low, "seq", bit) for bit in range(1, seq_n)]
    rows = []
    for at in range(seq_n):
        row = relative[at]
        for other in range(1, seq_n):
            row = jnp.where(seq_at == other, relative[at ^ other], row)
        rows.append(row)
    everyone = jnp.concatenate(rows, 0)[:row_count].astype(F32)

    self_dot = jnp.sum(total * total)
    cross_dot = jnp.sum(total * peer)
    mine_hot = (jnp.arange(2) == grp_at).astype(F32)
    local_gram = (
        mine_hot[:, None] * mine_hot[None, :] * self_dot
        + mine_hot[:, None] * (1.0 - mine_hot)[None, :] * cross_dot
    )
    gram = butterfly_sum(local_gram, ("grp", "seq", "row"))

    own_seqs = lax.dynamic_slice_in_dim(grads, row_at * share, share, 1)
    own_scale = lax.dynamic_slice_in_dim(in_scale, row_at * share, share, 0)
    input_time = jnp.einsum(
        "tsr,kr->tsk", own_seqs, w_in[:width_in], preferred_element_type=F32
    )
    input_grad = jnp.swapaxes(input_time * own_scale[None], 0, 1)
    return (
        input_grad,
        everyone[None, :, :width_in],
        everyone[None, :, width_in + 1 :],
        everyone[None, :, width_in],
        gram,
    )


def solution(mesh):
    return jax.shard_map(
        local,
        mesh=mesh,
        in_specs=(
            P(("grp", "seq"), None, None),
            P(("grp", "seq"), None),
            P(("grp", "seq"), None),
            P(("grp", "seq")),
            P(("grp", "seq")),
            P("row", None),
            P("row", None),
            P("row", None),
            P("row"),
            P(("grp", "seq"), None, None),
        ),
        out_specs=(
            P(("grp", "seq", "row"), None, None),
            P("grp", "row", None),
            P("grp", "row", None),
            P("grp", "row"),
            P(),
        ),
        check_vma=False,
    )
```

```python
import functools

import jax
import jax.numpy as jnp
from jax import lax
from jax.experimental import pallas as pl
from jax.experimental.pallas import tpu as pltpu
from jax.sharding import PartitionSpec as P

ACTIVATION_COEF = 2.0
TAR_BETA = 1.0
KEEP_INPUT = 0.75
KEEP_OUTPUT = 0.6
KEEP_WEIGHT = 0.5
LANES = 128
TILE = 256
VMEM_LIMIT = 58 << 20
BF16 = jnp.bfloat16
F32 = jnp.float32
OVER_ROWS = (((0,), (0,)), ((), ()))


def ceil_to(value, step):
    return -(-value // step) * step


def dot(left, right):
    return jnp.dot(left, right, preferred_element_type=F32)


def flip(block, axis, bit):
    count = lax.axis_size(axis)
    return lax.ppermute(block, axis, [(at, at ^ bit) for at in range(count)])


def exchange_sum(block, axis):
    count = lax.axis_size(axis)
    if count not in (2, 4):
        return lax.psum(block, axis)
    parts = [block] + [flip(block, axis, bit) for bit in range(1, count)]
    while len(parts) > 1:
        parts = [parts[at] + parts[at + 1] for at in range(0, len(parts), 2)]
    return parts[0]


def sigmoid(value):
    return 0.5 * jnp.tanh(0.5 * value) + 0.5


class Columns:
    def __init__(self, hidden):
        self.hidden = hidden
        self.full = hidden // LANES
        self.rest = hidden - self.full * LANES
        assert 0 < 4 * self.rest <= LANES
        self.total = 4 * hidden
        self.order = (self.full,) + tuple(range(self.full))

    def units(self, j):
        return j * LANES, min((j + 1) * LANES, self.hidden)

    def gates(self, j):
        return 4 * j * LANES, min(4 * (j + 1) * LANES, self.total)

    def gate(self, j, q):
        width = LANES if j < self.full else self.rest
        start = 4 * j * LANES + q * width
        return start, start + width

    def pack(self, gated):
        parts = []
        for j in range(self.full + 1):
            first, last = self.units(j)
            parts.append(gated[:, first:last].reshape((-1,) + gated.shape[2:]))
        return jnp.concatenate(parts, 0)

    def unpack_lanes(self, packed):
        parts = []
        for q in range(4):
            for j in range(self.full + 1):
                first, last = self.gate(j, q)
                parts.append(packed[..., first:last])
        return jnp.concatenate(parts, -1)


def drop_kernel(width, tok_ref, scale_ref, drop_ref):
    scale = scale_ref[...]
    for k in range(tok_ref.shape[0]):
        drop_ref[k, :, :width] = (tok_ref[k].astype(F32) * scale).astype(BF16)
        drop_ref[k, :, width:] = jnp.ones_like(drop_ref[k, :, width:])


def shard_kernel(plan, at_ref, in_ref, rec_ref, mask_ref, bias_ref, own_ref, *mine_ref):
    width = in_ref.shape[1]
    hidden = rec_ref.shape[1]
    bias = bias_ref[...]
    high = bias.astype(BF16)
    scale = mask_ref[...].astype(F32) / KEEP_WEIGHT
    own_ref[:, :width] = in_ref[...]
    own_ref[:, width : width + 1] = high
    own_ref[:, width + 1 : width + 2] = (bias - high.astype(F32)).astype(BF16)
    own_ref[:, plan.wide : plan.wide + hidden] = (rec_ref[...].astype(F32) * scale).astype(BF16)
    own_ref[:, plan.wide + hidden :] = jnp.zeros_like(own_ref[:, plan.wide + hidden :])
    for ref in mine_ref:
        ref[...] = own_ref[plan.window(at_ref[1], at_ref[2])]


class Plan:
    def __init__(self, hidden, wide):
        self.hidden = hidden
        self.wide = wide
        self.columns = ceil_to(wide + hidden, LANES)
        self.row_step = hidden // 4 // 16 * 16
        self.rows = hidden - 3 * self.row_step
        tiles = self.columns // LANES
        self.column_step = tiles // 2 * LANES
        self.cut = self.columns - self.column_step

    def window(self, seq_at, grp_at):
        return (
            pl.ds(pl.multiple_of(seq_at * self.row_step, 16), self.rows),
            pl.ds(pl.multiple_of(grp_at * self.column_step, LANES), self.cut),
        )


def forward_kernel(cols, plan, sub, pieced, at_ref, first_ref, second_ref, third_ref, *refs):
    count = 5 if pieced else 1
    sources = refs[:count]
    act_ref, cell_ref, prev_ref, w_ref, rec_ref, turned, even, odd, cell_s, low_s = refs[count:]
    seqs, width = first_ref.shape[1:]
    steps = act_ref.shape[0]
    hidden = cols.hidden

    def columns_of(rows_ref, start, stop, first, last):
        parts = []
        for j in range(cols.full + 1):
            unit, _ = cols.units(j)
            for q in range(4):
                low, high = cols.gate(j, q)
                if low >= start and high <= stop:
                    parts.append(rows_ref[q, unit : unit + high - low, first:last])
        return jnp.concatenate(parts, 0)

    def turned_dot(left, right):
        return lax.dot_general(left, right, (((1,), (1,)), ((), ())), preferred_element_type=F32)

    @pl.when(pl.program_id(0) == 0)
    def _():
        if pieced:
            row_at, seq_at, grp_at = at_ref[0], at_ref[1], at_ref[2]
            w_ref[row_at] = sources[0][...]
            for (m, k), (batch, index) in PIECE_AT.items():
                for gi in range(2):
                    window = plan.window(seq_at ^ m, grp_at ^ gi)
                    w_ref[(row_at ^ k,) + window] = sources[1 + 2 * gi + batch][index]
        else:
            w_ref[...] = sources[0][...]
        rec_ref[...] = w_ref[:, :, width : width + hidden]
        line = lax.broadcasted_iota(jnp.int32, (hidden, hidden), 0)
        same = line == lax.broadcasted_iota(jnp.int32, (hidden, hidden), 1)
        turned[...] = turned_dot(
            same.astype(F32).astype(BF16), columns_of(rec_ref, 0, cols.total, 0, hidden)
        ).astype(BF16)
        cell_s[...] = jnp.zeros_like(cell_s)
        low_s[...] = jnp.zeros_like(low_s)
        even[...] = turned_dot(
            first_ref[...].reshape(sub * seqs, width), columns_of(w_ref, 0, cols.total, 0, width)
        )

    lane = lax.broadcasted_iota(jnp.int32, (1, 4 * cols.rest), 1)
    tanh_lane = (lane >= 2 * cols.rest) & (lane < 3 * cols.rest)
    rest_mul = jnp.where(tanh_lane, 1.0, 0.5)
    rest_add = jnp.where(tanh_lane, 0.0, 0.5)
    spans = [cols.units(j) for j in range(cols.full + 1)]
    cells = [cell_s[:, a:b] for a, b in spans]
    lows = [low_s[:, a:b] for a, b in spans]
    chunk = ceil_to(-(-cols.total // sub), TILE)
    for k in range(steps):
        u, v = divmod(k, sub)
        now, later = (even, odd) if u % 2 == 0 else (odd, even)
        start, stop = chunk * v, min(chunk * (v + 1), cols.total)
        if start < stop:
            rows = (second_ref, third_ref)[u][...].reshape(sub * seqs, width)
            later[:, start:stop] = turned_dot(rows, columns_of(w_ref, start, stop, 0, width))
        for (a, b), low in zip(spans, lows):
            prev_ref[k, :, a:b] = low
        low = jnp.concatenate(lows, 1)
        lows = [None] * len(spans)
        for j in cols.order:
            first, last = cols.gates(j)
            pre = now[v * seqs : (v + 1) * seqs, first:last] + dot(low, turned[:, first:last])
            if j < cols.full:
                gate_i, gate_f, gate_g, gate_o = (
                    pre[:, q * LANES : (q + 1) * LANES] for q in range(4)
                )
                gate_i, gate_f, gate_o = sigmoid(gate_i), sigmoid(gate_f), sigmoid(gate_o)
                gate_g = jnp.tanh(gate_g)
                for q, gate in enumerate((gate_i, gate_f, gate_g, gate_o)):
                    a, b = cols.gate(j, q)
                    act_ref[k, :, a:b] = gate
            else:
                act = rest_mul * jnp.tanh(rest_mul * pre) + rest_add
                act_ref[k, :, first:last] = act
                gate_i, gate_f, gate_g, gate_o = (
                    act[:, q * cols.rest : (q + 1) * cols.rest] for q in range(4)
                )
            a, b = spans[j]
            cells[j] = gate_f * cells[j] + gate_i * gate_g
            cell_ref[k, :, a:b] = cells[j]
            lows[j] = (gate_o * jnp.tanh(cells[j])).astype(BF16)
    for j, (a, b) in enumerate(spans):
        cell_s[:, a:b] = cells[j]
        low_s[:, a:b] = lows[j]


def backward_kernel(
    cols,
    own,
    row_ref,
    act_ref,
    cell_ref,
    before_ref,
    act_before_ref,
    cot_ref,
    scale_ref,
    coef_ref,
    smooth_ref,
    length_ref,
    rec_ref,
    grad_ref,
    *refs,
):
    own_ref = refs[0] if own else None
    cell_grad_s, recur_s, smooth_s = refs[-3:]
    steps = act_ref.shape[0]
    place = pl.program_id(0)
    block = pl.num_programs(0) - 1 - place

    @pl.when(place == 0)
    def _():
        cell_grad_s[...] = jnp.zeros_like(cell_grad_s)
        recur_s[...] = jnp.zeros_like(recur_s)
        smooth_s[...] = jnp.zeros_like(smooth_s)

    inner = (block > 0).astype(F32)
    spans = [cols.units(j) for j in range(cols.full + 1)]

    def gates_at(ref, k, j):
        if j < cols.full:
            return [ref[k, :, a:b] for a, b in (cols.gate(j, q) for q in range(4))]
        first, last = cols.gates(j)
        packed = ref[k, :, first:last]
        return [packed[:, q * cols.rest : (q + 1) * cols.rest] for q in range(4)]

    blocks = range(cols.full + 1)
    rec = jnp.concatenate([rec_ref[q, a:b] for a, b in spans for q in range(4)], 0)
    dcell = [cell_grad_s[:, a:b] for a, b in spans]
    recur = [recur_s[:, a:b] for a, b in spans]
    smooth_next = [smooth_s[:, a:b] for a, b in spans]
    gates = [gates_at(act_ref, steps - 1, j) for j in blocks]
    tanh_cell = [jnp.tanh(cell_ref[steps - 1, :, a:b]) for a, b in spans]
    hidden = [gates[j][3] * tanh_cell[j] for j in blocks]
    for k in range(steps - 1, -1, -1):
        parts = [None] * len(spans)
        for j in cols.order:
            a, b = spans[j]
            gate_i, gate_f, gate_g, gate_o = gates[j]
            if k > 0:
                cell_before = cell_ref[k - 1, :, a:b]
                gates[j] = gates_at(act_ref, k - 1, j)
            else:
                cell_before = before_ref[0, :, a:b] * inner
                gates[j] = gates_at(act_before_ref, 0, j)
            tanh_before = jnp.tanh(cell_before)
            hidden_before = gates[j][3] * tanh_before
            valid = length_ref[:, a:b] > block * steps + k
            smooth = smooth_ref[:, a:b] * (hidden[j] - hidden_before)
            if k == 0:
                smooth = smooth * inner
            smooth = jnp.where(valid, smooth, 0.0)
            direct = scale_ref[:, a:b] * cot_ref[k, :, a:b].astype(F32) + coef_ref[:, a:b] * hidden[j]
            direct = jnp.where(valid, direct, 0.0) + smooth - smooth_next[j]
            smooth_next[j] = smooth
            dhidden = direct + recur[j]
            total = dcell[j] + dhidden * (gate_o * (1.0 - tanh_cell[j] * tanh_cell[j]))
            grads = [
                (total * (gate_g * gate_i * (1.0 - gate_i))).astype(BF16),
                (total * (cell_before * gate_f * (1.0 - gate_f))).astype(BF16),
                (total * (gate_i * (1.0 - gate_g * gate_g))).astype(BF16),
                (dhidden * (tanh_cell[j] * gate_o * (1.0 - gate_o))).astype(BF16),
            ]
            parts[j] = jnp.concatenate(grads, 1)
            first, last = cols.gates(j)
            grad_ref[k, :, first:last] = parts[j]
            if own:
                mine = grads[3]
                for q in range(3):
                    mine = jnp.where(row_ref[0] == q, grads[q], mine)
                own_ref[k, :, a:b] = mine
            dcell[j] = total * gate_f
            tanh_cell[j] = tanh_before
            hidden[j] = hidden_before
        back = dot(jnp.concatenate(parts, 1), rec)
        recur = [back[:, a:b] for a, b in spans]
    for j, (a, b) in enumerate(spans):
        cell_grad_s[:, a:b] = dcell[j]
        recur_s[:, a:b] = recur[j]
        smooth_s[:, a:b] = smooth_next[j]


def weight_kernel(grp_ref, rows_ref, drop_ref, prev_ref, pick_ref, scale_ref, keep_ref, send_ref, sums):
    steps, seqs, own = rows_ref.shape
    width = drop_ref.shape[2]
    place = pl.program_id(0)

    @pl.when(place == 0)
    def _():
        sums[...] = jnp.zeros_like(sums)

    grads = rows_ref[...]
    first = (grads * pick_ref[...][None]).reshape(steps * seqs, own)
    second = grads.reshape(steps * seqs, own) - first
    drop = drop_ref[...].reshape(steps * seqs, width)
    prev = prev_ref[...].reshape(steps * seqs, prev_ref.shape[2])
    for at, part in enumerate((first, second)):
        sums[at, :own, :width] += lax.dot_general(
            part, drop, OVER_ROWS, preferred_element_type=F32
        )
        sums[at, :own, width:] += lax.dot_general(
            part, prev, OVER_ROWS, preferred_element_type=F32
        )

    @pl.when(place == pl.num_programs(0) - 1)
    def _():
        rows = keep_ref.shape[1]
        for at in range(2):
            sums[at, :own, width:] = sums[at, :own, width:] * scale_ref[...]
        for part in range(keep_ref.shape[0]):
            span = slice(part * rows, (part + 1) * rows)
            keep_ref[part] = sums[grp_ref[0], span]
            send_ref[part] = sums[1 - grp_ref[0], span].astype(BF16)


def params():
    return pltpu.CompilerParams(
        dimension_semantics=("arbitrary",), vmem_limit_bytes=VMEM_LIMIT
    )


def fixed(*shape):
    return pl.BlockSpec(shape, lambda *_: (0,) * len(shape))


def gather_pieces(mine, counts, beside):
    hold = lax.optimization_barrier
    one, two, beside, counts = hold(
        (flip(mine, "row", 1), flip(mine, "row", 2), beside, counts + flip(counts, "grp", 1))
    )
    near = jnp.stack([one, two])
    near_one, near_two, three, *others = hold(
        [flip(near, "seq", 1), flip(near, "seq", 2), flip(two, "row", 1)]
        + [flip(counts, "seq", bit) for bit in range(1, 4)]
    )
    counts = (counts + others[0]) + (others[1] + others[2])
    early = jnp.concatenate([near, near_one, near_two, three[None]], 0)
    across, diag_one, diag_two, *last = hold(
        [flip(early, "grp", 1), flip(near_two[0], "seq", 1), flip(near_one[1], "seq", 2)]
        + [flip(three, "seq", bit) for bit in range(1, 4)]
    )
    late = jnp.stack([diag_one, diag_two] + last)
    return early, late, across, flip(late, "grp", 1), counts, beside


PIECE_AT = {
    (0, 1): (0, 0),
    (0, 2): (0, 1),
    (1, 1): (0, 2),
    (1, 2): (0, 3),
    (2, 1): (0, 4),
    (2, 2): (0, 5),
    (0, 3): (0, 6),
    (3, 1): (1, 0),
    (3, 2): (1, 1),
    (1, 3): (1, 2),
    (2, 3): (1, 3),
    (3, 3): (1, 4),
}


def local(
    tokens,
    in_mask,
    out_mask,
    lengths,
    groups,
    input_gate_weight,
    w_recur,
    weight_mask,
    bias,
    cotangent,
):
    seq_count, time_steps, width_in = tokens.shape
    hidden = cotangent.shape[2]
    row_count = input_gate_weight.shape[0]
    row_at = lax.axis_index("row")
    grp_at = lax.axis_index("grp")
    seq_at = lax.axis_index("seq")
    rows_n, seq_n = lax.axis_size("row"), lax.axis_size("seq")
    cols = Columns(hidden)
    wide = ceil_to(width_in + 2, LANES)
    share = seq_count // rows_n
    own = row_count == hidden
    pieced = own and rows_n == 4 and seq_n == 4 and lax.axis_size("grp") == 2

    w_scale = weight_mask.astype(F32) / KEEP_WEIGHT
    plan = Plan(hidden, wide)
    at = jnp.stack([row_at, seq_at, grp_at]).astype(jnp.int32)
    own_weights, *mine = pl.pallas_call(
        functools.partial(shard_kernel, plan),
        grid_spec=pltpu.PrefetchScalarGridSpec(
            num_scalar_prefetch=1,
            grid=(1,),
            in_specs=[
                fixed(row_count, width_in),
                fixed(row_count, hidden),
                fixed(row_count, hidden),
                fixed(row_count, 1),
            ],
            out_specs=[fixed(row_count, plan.columns)] + [fixed(plan.rows, plan.cut)] * pieced,
        ),
        out_shape=[jax.ShapeDtypeStruct((row_count, plan.columns), BF16)]
        + [jax.ShapeDtypeStruct((plan.rows, plan.cut), BF16)] * pieced,
        compiler_params=params(),
        name="shard",
    )(at, input_gate_weight, w_recur, weight_mask, bias[:, None])
    sub = max(s for s in range(1, 8) if time_steps % (2 * s) == 0)
    steps = 2 * sub
    blocks = time_steps // steps

    def at_time(width):
        return pl.BlockSpec((steps, seq_count, width), lambda b, *_: (b, 0, 0))

    in_scale = in_mask.astype(F32) / KEEP_INPUT
    dropped = pl.pallas_call(
        functools.partial(drop_kernel, width_in),
        grid=(blocks,),
        in_specs=[at_time(width_in), fixed(seq_count, width_in)],
        out_specs=at_time(wide),
        out_shape=jax.ShapeDtypeStruct((time_steps, seq_count, wide), BF16),
        compiler_params=params(),
        name="drop",
    )(jnp.swapaxes(tokens, 0, 1), in_scale)
    cot_time = jnp.swapaxes(cotangent, 0, 1)

    group_hot = (groups[:, None] == jnp.arange(2)[None, :]).astype(F32)
    valid_count = jnp.clip(lengths, 0, time_steps).astype(F32)
    counts = jnp.sum(group_hot * valid_count[:, None], 0)
    if pieced:
        *pieces, counts, dropped = gather_pieces(mine[0], counts, dropped)
        sources = [own_weights] + pieces
    else:
        counts = lax.psum(counts, ("grp", "seq"))
        whole = lax.all_gather(own_weights, "row", axis=0, tiled=True)
        sources = [whole.reshape(4, hidden, plan.columns)]
    group_ratio = jnp.sum(counts) / counts
    seq_ratio = jnp.sum(group_hot * group_ratio[None, :], 1)
    out_scale = out_mask.astype(F32) / KEEP_OUTPUT
    act_coef = 2.0 * ACTIVATION_COEF * seq_ratio[:, None] * out_scale * out_scale
    smooth_coef = jnp.broadcast_to(2.0 * TAR_BETA * seq_ratio[:, None], (seq_count, hidden))
    length_wide = jnp.broadcast_to(lengths[:, None], (seq_count, hidden))

    acts, cells, prev_low, weights, w_rec = pl.pallas_call(
        functools.partial(forward_kernel, cols, plan, sub, pieced),
        grid_spec=pltpu.PrefetchScalarGridSpec(
            num_scalar_prefetch=1,
            grid=(blocks,),
            in_specs=[
                fixed(sub, seq_count, wide),
                pl.BlockSpec((sub, seq_count, wide), lambda b, *_: (2 * b + 1, 0, 0)),
                pl.BlockSpec(
                    (sub, seq_count, wide),
                    lambda b, *_: (jnp.minimum(2 * b + 2, 2 * blocks - 1), 0, 0),
                ),
            ]
            + [fixed(*source.shape) for source in sources],
            out_specs=[
                at_time(cols.total),
                at_time(hidden),
                at_time(hidden),
                fixed(4, hidden, plan.columns),
                fixed(4, hidden, hidden),
            ],
            scratch_shapes=[
                pltpu.VMEM((hidden, cols.total), BF16),
                pltpu.VMEM((sub * seq_count, cols.total), F32),
                pltpu.VMEM((sub * seq_count, cols.total), F32),
                pltpu.VMEM((seq_count, hidden), F32),
                pltpu.VMEM((seq_count, hidden), BF16),
            ],
        ),
        out_shape=[
            jax.ShapeDtypeStruct((time_steps, seq_count, cols.total), F32),
            jax.ShapeDtypeStruct((time_steps, seq_count, hidden), F32),
            jax.ShapeDtypeStruct((time_steps, seq_count, hidden), BF16),
            jax.ShapeDtypeStruct((4, hidden, plan.columns), BF16),
            jax.ShapeDtypeStruct((4, hidden, hidden), BF16),
        ],
        compiler_params=params(),
        name="forward",
    )(at, dropped, dropped, dropped, *sources)

    def back(b):
        return 2 * blocks - 1 - b

    def before(width):
        return pl.BlockSpec(
            (1, seq_count, width), lambda b, *_: (jnp.maximum(back(b) * sub - 1, 0), 0, 0)
        )

    def back_time(width):
        return pl.BlockSpec((sub, seq_count, width), lambda b, *_: (back(b), 0, 0))

    grad_specs = [back_time(cols.total)] + [back_time(hidden)] * own
    grad_shapes = [cols.total] + [hidden] * own
    grads, *own_rows = pl.pallas_call(
        functools.partial(backward_kernel, cols, own),
        grid_spec=pltpu.PrefetchScalarGridSpec(
            num_scalar_prefetch=1,
            grid=(2 * blocks,),
            in_specs=[
                back_time(cols.total),
                back_time(hidden),
                before(hidden),
                before(cols.total),
                back_time(hidden),
                fixed(seq_count, hidden),
                fixed(seq_count, hidden),
                fixed(seq_count, hidden),
                fixed(seq_count, hidden),
                fixed(4, hidden, hidden),
            ],
            out_specs=grad_specs,
            scratch_shapes=[pltpu.VMEM((seq_count, hidden), F32)] * 3,
        ),
        out_shape=[
            jax.ShapeDtypeStruct((time_steps, seq_count, width), BF16) for width in grad_shapes
        ],
        compiler_params=params(),
        name="backward",
    )(
        row_at[None],
        acts,
        cells,
        cells,
        acts,
        cot_time,
        out_scale,
        act_coef,
        smooth_coef,
        length_wide,
        w_rec,
    )

    if own:
        own_rows = own_rows[0]
    else:
        own_rows = lax.dynamic_slice_in_dim(
            cols.unpack_lanes(grads), row_at * row_count, row_count, 2
        )
    pick = jnp.broadcast_to((groups == 0).astype(BF16)[:, None], (seq_count, row_count))
    columns = wide + hidden
    part_rows = ceil_to(-(-row_count // seq_n), 8)
    keep, send = pl.pallas_call(
        weight_kernel,
        grid_spec=pltpu.PrefetchScalarGridSpec(
            num_scalar_prefetch=1,
            grid=(blocks,),
            in_specs=[
                at_time(row_count),
                at_time(wide),
                at_time(hidden),
                fixed(seq_count, row_count),
                fixed(row_count, hidden),
            ],
            out_specs=[fixed(seq_n, part_rows, columns)] * 2,
            scratch_shapes=[pltpu.VMEM((2, seq_n * part_rows, columns), F32)],
        ),
        out_shape=[
            jax.ShapeDtypeStruct((seq_n, part_rows, columns), F32),
            jax.ShapeDtypeStruct((seq_n, part_rows, columns), BF16),
        ],
        compiler_params=params(),
        name="weights",
    )(grp_at[None], own_rows, dropped, prev_low, pick, w_scale)

    both = (keep + flip(send, "grp", 1).astype(F32)).astype(BF16)
    swapped = lax.all_to_all(both, "seq", 0, 0, tiled=True)

    own_seqs = lax.dynamic_slice_in_dim(grads, row_at * share, share, 1)
    own_scale = lax.dynamic_slice_in_dim(in_scale, row_at * share, share, 0)
    w_in = cols.pack(weights[:, :, :width_in])
    input_time = jnp.einsum("tsr,rk->tsk", own_seqs, w_in, preferred_element_type=F32)
    input_grad = jnp.swapaxes(input_time * own_scale[None], 0, 1)
    swapped, input_grad = lax.optimization_barrier((swapped, input_grad))

    total = jnp.sum(swapped.astype(F32), 0).astype(BF16)
    everyone = lax.all_to_all(
        jnp.broadcast_to(total[None], (seq_n, part_rows, columns)), "seq", 0, 0, tiled=True
    )
    peer = flip(total, "grp", 1)
    ours, theirs = (
        jnp.concatenate([part[:, : width_in + 1], part[:, wide:]], 1).astype(F32)
        for part in (total, peer)
    )
    first = jnp.where(grp_at == 0, ours, theirs)
    second = jnp.where(grp_at == 0, theirs, ours)
    dots = [jnp.sum(a * b) for a, b in ((first, first), (first, second), (second, second))]
    gram = jnp.stack([dots[0], dots[1], dots[1], dots[2]]).reshape(2, 2)
    gram = exchange_sum(exchange_sum(gram, "seq"), "row")
    everyone, gram = lax.optimization_barrier((everyone, gram))
    everyone = everyone.reshape(seq_n * part_rows, columns)[:row_count].astype(F32)

    return (
        input_grad,
        everyone[None, :, :width_in],
        everyone[None, :, wide:],
        everyone[None, :, width_in],
        gram,
    )


def solution(mesh):
    return jax.shard_map(
        local,
        mesh=mesh,
        in_specs=(
            P(("grp", "seq"), None, None),
            P(("grp", "seq"), None),
            P(("grp", "seq"), None),
            P(("grp", "seq")),
            P(("grp", "seq")),
            P("row", None),
            P("row", None),
            P("row", None),
            P("row"),
            P(("grp", "seq"), None, None),
        ),
        out_specs=(
            P(("grp", "seq", "row"), None, None),
            P("grp", "row", None),
            P("grp", "row", None),
            P("grp", "row"),
            P(),
        ),
        check_vma=False,
    )
```

```python
import functools

import jax
import jax.numpy as jnp
from jax import lax
from jax.experimental import pallas as pl
from jax.experimental.pallas import tpu as pltpu
from jax.sharding import PartitionSpec as P

ACTIVATION_COEF = 2.0
TAR_BETA = 1.0
KEEP_INPUT = 0.75
KEEP_OUTPUT = 0.6
KEEP_WEIGHT = 0.5
LANES = 128
TILE = 256
VMEM_LIMIT = 58 << 20
BF16 = jnp.bfloat16
F32 = jnp.float32
OVER_ROWS = (((0,), (0,)), ((), ()))


def ceil_to(value, step):
    return -(-value // step) * step


def dot(left, right):
    return jnp.dot(left, right, preferred_element_type=F32)


def flip(block, axis, bit):
    count = lax.axis_size(axis)
    return lax.ppermute(block, axis, [(at, at ^ bit) for at in range(count)])


def exchange_sum(block, axis):
    count = lax.axis_size(axis)
    if count not in (2, 4):
        return lax.psum(block, axis)
    parts = [block] + [flip(block, axis, bit) for bit in range(1, count)]
    while len(parts) > 1:
        parts = [parts[at] + parts[at + 1] for at in range(0, len(parts), 2)]
    return parts[0]


def sigmoid(value):
    return 0.5 * jnp.tanh(0.5 * value) + 0.5


class Columns:
    def __init__(self, hidden):
        self.hidden = hidden
        self.full = hidden // LANES
        self.rest = hidden - self.full * LANES
        assert 0 < 4 * self.rest <= LANES
        self.total = 4 * hidden
        self.order = (self.full,) + tuple(range(self.full))

    def units(self, j):
        return j * LANES, min((j + 1) * LANES, self.hidden)

    def gates(self, j):
        return 4 * j * LANES, min(4 * (j + 1) * LANES, self.total)

    def gate(self, j, q):
        width = LANES if j < self.full else self.rest
        start = 4 * j * LANES + q * width
        return start, start + width

    def pack(self, gated):
        parts = []
        for j in range(self.full + 1):
            first, last = self.units(j)
            parts.append(gated[:, first:last].reshape((-1,) + gated.shape[2:]))
        return jnp.concatenate(parts, 0)

    def unpack_lanes(self, packed):
        parts = []
        for q in range(4):
            for j in range(self.full + 1):
                first, last = self.gate(j, q)
                parts.append(packed[..., first:last])
        return jnp.concatenate(parts, -1)


def drop_kernel(width, tok_ref, scale_ref, drop_ref):
    scale = scale_ref[...]
    for k in range(tok_ref.shape[0]):
        drop_ref[k, :, :width] = (tok_ref[k].astype(F32) * scale).astype(BF16)
        drop_ref[k, :, width:] = jnp.ones_like(drop_ref[k, :, width:])


def turned_dot(left, right):
    return lax.dot_general(left, right, (((1,), (1,)), ((), ())), preferred_element_type=F32)


def identity(size):
    line = lax.broadcasted_iota(jnp.int32, (size, size), 0)
    same = line == lax.broadcasted_iota(jnp.int32, (size, size), 1)
    return same.astype(F32).astype(BF16)


def shard_kernel(plan, at_ref, in_ref, rec_ref, mask_ref, bias_ref, own_ref, *mine_ref):
    rows, width = in_ref.shape
    hidden = rec_ref.shape[1]
    bias = bias_ref[...]
    high = bias.astype(BF16)
    pair = jnp.concatenate([high, (bias - high.astype(F32)).astype(BF16)], 0)
    scale = mask_ref[...].astype(F32) / KEEP_WEIGHT
    own_ref[:, :width] = in_ref[...]
    own_ref[:, width : width + 2] = turned_dot(identity(rows), pair).astype(BF16)
    own_ref[:, plan.wide : plan.wide + hidden] = (rec_ref[...].astype(F32) * scale).astype(BF16)
    own_ref[:, plan.wide + hidden :] = jnp.zeros_like(own_ref[:, plan.wide + hidden :])
    for ref in mine_ref:
        ref[...] = own_ref[plan.window(at_ref[1], at_ref[2], 0, plan.rows)]


class Plan:
    def __init__(self, hidden, wide):
        self.wide = wide
        self.columns = ceil_to(wide + hidden, LANES)
        self.row_step = hidden // 32 * 16
        self.rows = hidden - self.row_step
        self.first = ceil_to(self.rows // 2, 16)
        self.column_step = self.columns // LANES // 2 * LANES
        self.cut = self.columns - self.column_step

    def window(self, seq_at, grp_at, start, count):
        half = (seq_at ^ (seq_at >> 1)) & 1
        return (
            pl.ds(pl.multiple_of(half * self.row_step + start, 16), count),
            pl.ds(pl.multiple_of(grp_at * self.column_step, LANES), self.cut),
        )

    def places(self):
        first, rest = self.first, self.rows - self.first
        return [
            (0, 1, 0, 0, self.rows),
            (0, 2, 0, 0, self.rows),
            (0, 1, 1, 0, first),
            (0, 2, 1, 0, first),
            (0, 1, 1, first, rest),
            (0, 2, 1, first, rest),
            (0, 3, 0, 0, self.rows),
            (1, 3, 1, 0, first),
            (1, 3, 1, first, rest),
        ]


def forward_kernel(cols, plan, sub, pieced, at_ref, first_ref, second_ref, third_ref, *refs):
    count = 5 if pieced else 1
    sources = refs[:count]
    act_ref, cell_ref, prev_ref, w_ref, rec_ref, turned, even, odd, cell_s, low_s = refs[count:]
    seqs, width = first_ref.shape[1:]
    steps = act_ref.shape[0]
    hidden = cols.hidden

    def columns_of(rows_ref, start, stop, first, last):
        parts = []
        for j in range(cols.full + 1):
            unit, _ = cols.units(j)
            for q in range(4):
                low, high = cols.gate(j, q)
                if low >= start and high <= stop:
                    parts.append(rows_ref[q, unit : unit + high - low, first:last])
        return jnp.concatenate(parts, 0)

    @pl.when(pl.program_id(0) == 0)
    def _():
        if pieced:
            row_at, seq_at, grp_at = at_ref[0], at_ref[1], at_ref[2]
            w_ref[row_at] = sources[0][...]
            for gi in range(2):
                line = [0, 0]
                for array, k, m, start, size in plan.places():
                    window = plan.window(seq_at ^ m, grp_at ^ gi, start, size)
                    piece = sources[1 + 2 * gi + array][line[array] : line[array] + size]
                    w_ref[(row_at ^ k,) + window] = piece
                    line[array] += size
        else:
            w_ref[...] = sources[0][...]
        rec_ref[...] = w_ref[:, :, width : width + hidden]
        turned[...] = turned_dot(
            identity(hidden), columns_of(rec_ref, 0, cols.total, 0, hidden)
        ).astype(BF16)
        cell_s[...] = jnp.zeros_like(cell_s)
        low_s[...] = jnp.zeros_like(low_s)
        even[...] = turned_dot(
            first_ref[...].reshape(sub * seqs, width), columns_of(w_ref, 0, cols.total, 0, width)
        )

    lane = lax.broadcasted_iota(jnp.int32, (1, 4 * cols.rest), 1)
    tanh_lane = (lane >= 2 * cols.rest) & (lane < 3 * cols.rest)
    rest_mul = jnp.where(tanh_lane, 1.0, 0.5)
    rest_add = jnp.where(tanh_lane, 0.0, 0.5)
    spans = [cols.units(j) for j in range(cols.full + 1)]
    cells = [cell_s[:, a:b] for a, b in spans]
    lows = [low_s[:, a:b] for a, b in spans]
    chunk = ceil_to(-(-cols.total // sub), TILE)
    for k in range(steps):
        u, v = divmod(k, sub)
        now, later = (even, odd) if u % 2 == 0 else (odd, even)
        start, stop = chunk * v, min(chunk * (v + 1), cols.total)
        if start < stop:
            rows = (second_ref, third_ref)[u][...].reshape(sub * seqs, width)
            later[:, start:stop] = turned_dot(rows, columns_of(w_ref, start, stop, 0, width))
        for (a, b), low in zip(spans, lows):
            prev_ref[k, :, a:b] = low
        low = jnp.concatenate(lows, 1)
        lows = [None] * len(spans)
        for j in cols.order:
            first, last = cols.gates(j)
            pre = now[v * seqs : (v + 1) * seqs, first:last] + dot(low, turned[:, first:last])
            if j < cols.full:
                gate_i, gate_f, gate_g, gate_o = (
                    pre[:, q * LANES : (q + 1) * LANES] for q in range(4)
                )
                gate_i, gate_f, gate_o = sigmoid(gate_i), sigmoid(gate_f), sigmoid(gate_o)
                gate_g = jnp.tanh(gate_g)
                for q, gate in enumerate((gate_i, gate_f, gate_g, gate_o)):
                    a, b = cols.gate(j, q)
                    act_ref[k, :, a:b] = gate
            else:
                act = rest_mul * jnp.tanh(rest_mul * pre) + rest_add
                act_ref[k, :, first:last] = act
                gate_i, gate_f, gate_g, gate_o = (
                    act[:, q * cols.rest : (q + 1) * cols.rest] for q in range(4)
                )
            a, b = spans[j]
            cells[j] = gate_f * cells[j] + gate_i * gate_g
            cell_ref[k, :, a:b] = cells[j]
            lows[j] = (gate_o * jnp.tanh(cells[j])).astype(BF16)
    for j, (a, b) in enumerate(spans):
        cell_s[:, a:b] = cells[j]
        low_s[:, a:b] = lows[j]


def backward_kernel(
    cols,
    own,
    row_ref,
    act_ref,
    cell_ref,
    before_ref,
    act_before_ref,
    cot_ref,
    scale_ref,
    coef_ref,
    smooth_ref,
    length_ref,
    rec_ref,
    grad_ref,
    *refs,
):
    own_ref = refs[0] if own else None
    cell_grad_s, recur_s, smooth_s = refs[-3:]
    steps = act_ref.shape[0]
    place = pl.program_id(0)
    block = pl.num_programs(0) - 1 - place

    @pl.when(place == 0)
    def _():
        cell_grad_s[...] = jnp.zeros_like(cell_grad_s)
        recur_s[...] = jnp.zeros_like(recur_s)
        smooth_s[...] = jnp.zeros_like(smooth_s)

    inner = (block > 0).astype(F32)
    spans = [cols.units(j) for j in range(cols.full + 1)]

    def gates_at(ref, k, j):
        if j < cols.full:
            return [ref[k, :, a:b] for a, b in (cols.gate(j, q) for q in range(4))]
        first, last = cols.gates(j)
        packed = ref[k, :, first:last]
        return [packed[:, q * cols.rest : (q + 1) * cols.rest] for q in range(4)]

    blocks = range(cols.full + 1)
    rec = jnp.concatenate([rec_ref[q, a:b] for a, b in spans for q in range(4)], 0)
    dcell = [cell_grad_s[:, a:b] for a, b in spans]
    recur = [recur_s[:, a:b] for a, b in spans]
    smooth_next = [smooth_s[:, a:b] for a, b in spans]
    gates = [gates_at(act_ref, steps - 1, j) for j in blocks]
    tanh_cell = [jnp.tanh(cell_ref[steps - 1, :, a:b]) for a, b in spans]
    hidden = [gates[j][3] * tanh_cell[j] for j in blocks]
    for k in range(steps - 1, -1, -1):
        parts = [None] * len(spans)
        for j in cols.order:
            a, b = spans[j]
            gate_i, gate_f, gate_g, gate_o = gates[j]
            if k > 0:
                cell_before = cell_ref[k - 1, :, a:b]
                gates[j] = gates_at(act_ref, k - 1, j)
            else:
                cell_before = before_ref[0, :, a:b] * inner
                gates[j] = gates_at(act_before_ref, 0, j)
            tanh_before = jnp.tanh(cell_before)
            hidden_before = gates[j][3] * tanh_before
            valid = length_ref[:, a:b] > block * steps + k
            smooth = smooth_ref[:, a:b] * (hidden[j] - hidden_before)
            if k == 0:
                smooth = smooth * inner
            smooth = jnp.where(valid, smooth, 0.0)
            direct = scale_ref[:, a:b] * cot_ref[k, :, a:b].astype(F32) + coef_ref[:, a:b] * hidden[j]
            direct = jnp.where(valid, direct, 0.0) + smooth - smooth_next[j]
            smooth_next[j] = smooth
            dhidden = direct + recur[j]
            total = dcell[j] + dhidden * (gate_o * (1.0 - tanh_cell[j] * tanh_cell[j]))
            grads = [
                (total * (gate_g * gate_i * (1.0 - gate_i))).astype(BF16),
                (total * (cell_before * gate_f * (1.0 - gate_f))).astype(BF16),
                (total * (gate_i * (1.0 - gate_g * gate_g))).astype(BF16),
                (dhidden * (tanh_cell[j] * gate_o * (1.0 - gate_o))).astype(BF16),
            ]
            parts[j] = jnp.concatenate(grads, 1)
            first, last = cols.gates(j)
            grad_ref[k, :, first:last] = parts[j]
            if own:
                mine = grads[3]
                for q in range(3):
                    mine = jnp.where(row_ref[0] == q, grads[q], mine)
                own_ref[k, :, a:b] = mine
            dcell[j] = total * gate_f
            tanh_cell[j] = tanh_before
            hidden[j] = hidden_before
        back = dot(jnp.concatenate(parts, 1), rec)
        recur = [back[:, a:b] for a, b in spans]
    for j, (a, b) in enumerate(spans):
        cell_grad_s[:, a:b] = dcell[j]
        recur_s[:, a:b] = recur[j]
        smooth_s[:, a:b] = smooth_next[j]


def weight_kernel(data_n, grp_ref, rows_ref, pick_ref, *refs):
    data, scale, (keep_ref, send_ref, sums) = refs[:data_n], refs[data_n:-3], refs[-3:]
    steps, seqs, own = rows_ref.shape
    place = pl.program_id(0)

    @pl.when(place == 0)
    def _():
        sums[...] = jnp.zeros_like(sums)

    grads = rows_ref[...]
    first = (grads * pick_ref[...][None]).reshape(steps * seqs, own)
    second = grads.reshape(steps * seqs, own) - first
    start = 0
    for ref in data:
        width = ref.shape[2]
        values = ref[...].reshape(steps * seqs, width)
        for at, part in enumerate((first, second)):
            sums[at, :own, start : start + width] += lax.dot_general(
                part, values, OVER_ROWS, preferred_element_type=F32
            )
        start += width

    @pl.when(place == pl.num_programs(0) - 1)
    def _():
        rows = keep_ref.shape[1]
        for ref in scale:
            for at in range(2):
                part = (at, slice(0, own), slice(start - width, start))
                sums[part] = sums[part] * ref[...]
        for part in range(keep_ref.shape[0]):
            span = slice(part * rows, (part + 1) * rows)
            keep_ref[part] = sums[grp_ref[0], span]
            send_ref[part] = sums[1 - grp_ref[0], span].astype(BF16)


def params():
    return pltpu.CompilerParams(
        dimension_semantics=("arbitrary",), vmem_limit_bytes=VMEM_LIMIT
    )


def fixed(*shape):
    return pl.BlockSpec(shape, lambda *_: (0,) * len(shape))


def gather_pieces(plan, mine, counts, beside):
    hold = lax.optimization_barrier
    cut = plan.cut
    one, two, beside, counts = hold(
        (flip(mine, "row", 1), flip(mine, "row", 2), beside, counts + flip(counts, "grp", 1))
    )
    near = jnp.stack([one, two])
    near_x, near_y, three, counts = hold(
        (
            flip(near[:, : plan.first], "seq", 1),
            flip(near[:, plan.first :], "seq", 2),
            flip(two, "row", 1),
            counts + flip(counts, "seq", 1),
        )
    )
    early = jnp.concatenate([part.reshape(-1, cut) for part in (near, near_x, near_y, three)], 0)
    last_x, last_y, early_other, counts = hold(
        (
            flip(three[: plan.first], "seq", 1),
            flip(three[plan.first :], "seq", 2),
            flip(early, "grp", 1),
            counts + flip(counts, "seq", 2),
        )
    )
    late = jnp.concatenate([last_x, last_y], 0)
    return early, late, early_other, flip(late, "grp", 1), counts, beside


def local(
    tokens,
    in_mask,
    out_mask,
    lengths,
    groups,
    input_gate_weight,
    w_recur,
    weight_mask,
    bias,
    cotangent,
):
    seq_count, time_steps, width_in = tokens.shape
    hidden = cotangent.shape[2]
    row_count = input_gate_weight.shape[0]
    row_at = lax.axis_index("row")
    grp_at = lax.axis_index("grp")
    seq_at = lax.axis_index("seq")
    rows_n, seq_n = lax.axis_size("row"), lax.axis_size("seq")
    cols = Columns(hidden)
    wide = ceil_to(width_in + 2, LANES)
    share = seq_count // rows_n
    own = row_count == hidden
    pieced = own and rows_n == 4 and seq_n == 4 and lax.axis_size("grp") == 2

    w_scale = weight_mask.astype(F32) / KEEP_WEIGHT
    plan = Plan(hidden, wide)
    at = jnp.stack([row_at, seq_at, grp_at]).astype(jnp.int32)
    own_weights, *mine = pl.pallas_call(
        functools.partial(shard_kernel, plan),
        grid_spec=pltpu.PrefetchScalarGridSpec(
            num_scalar_prefetch=1,
            grid=(1,),
            in_specs=[
                fixed(row_count, width_in),
                fixed(row_count, hidden),
                fixed(row_count, hidden),
                fixed(1, row_count),
            ],
            out_specs=[fixed(row_count, plan.columns)] + [fixed(plan.rows, plan.cut)] * pieced,
        ),
        out_shape=[jax.ShapeDtypeStruct((row_count, plan.columns), BF16)]
        + [jax.ShapeDtypeStruct((plan.rows, plan.cut), BF16)] * pieced,
        compiler_params=params(),
        name="shard",
    )(at, input_gate_weight, w_recur, weight_mask, bias[None])
    sub = max(s for s in range(1, 8) if time_steps % (2 * s) == 0)
    steps = 2 * sub
    blocks = time_steps // steps

    def at_time(width):
        return pl.BlockSpec((steps, seq_count, width), lambda b, *_: (b, 0, 0))

    in_scale = in_mask.astype(F32) / KEEP_INPUT
    dropped = pl.pallas_call(
        functools.partial(drop_kernel, width_in),
        grid=(blocks,),
        in_specs=[at_time(width_in), fixed(seq_count, width_in)],
        out_specs=at_time(wide),
        out_shape=jax.ShapeDtypeStruct((time_steps, seq_count, wide), BF16),
        compiler_params=params(),
        name="drop",
    )(jnp.swapaxes(tokens, 0, 1), in_scale)
    cot_time = jnp.swapaxes(cotangent, 0, 1)

    group_hot = (groups[:, None] == jnp.arange(2)[None, :]).astype(F32)
    valid_count = jnp.clip(lengths, 0, time_steps).astype(F32)
    counts = jnp.sum(group_hot * valid_count[:, None], 0)
    if pieced:
        *pieces, counts, dropped = gather_pieces(plan, mine[0], counts, dropped)
        sources = [own_weights] + pieces
    else:
        counts = lax.psum(counts, ("grp", "seq"))
        whole = lax.all_gather(own_weights, "row", axis=0, tiled=True)
        sources = [whole.reshape(4, hidden, plan.columns)]
    group_ratio = jnp.sum(counts) / counts
    seq_ratio = jnp.sum(group_hot * group_ratio[None, :], 1)
    out_scale = out_mask.astype(F32) / KEEP_OUTPUT
    act_coef = 2.0 * ACTIVATION_COEF * seq_ratio[:, None] * out_scale * out_scale
    smooth_coef = jnp.broadcast_to(2.0 * TAR_BETA * seq_ratio[:, None], (seq_count, hidden))
    length_wide = jnp.broadcast_to(lengths[:, None], (seq_count, hidden))

    acts, cells, prev_low, weights, w_rec = pl.pallas_call(
        functools.partial(forward_kernel, cols, plan, sub, pieced),
        grid_spec=pltpu.PrefetchScalarGridSpec(
            num_scalar_prefetch=1,
            grid=(blocks,),
            in_specs=[
                fixed(sub, seq_count, wide),
                pl.BlockSpec((sub, seq_count, wide), lambda b, *_: (2 * b + 1, 0, 0)),
                pl.BlockSpec(
                    (sub, seq_count, wide),
                    lambda b, *_: (jnp.minimum(2 * b + 2, 2 * blocks - 1), 0, 0),
                ),
            ]
            + [fixed(*source.shape) for source in sources],
            out_specs=[
                at_time(cols.total),
                at_time(hidden),
                at_time(hidden),
                fixed(4, hidden, plan.columns),
                fixed(4, hidden, hidden),
            ],
            scratch_shapes=[
                pltpu.VMEM((hidden, cols.total), BF16),
                pltpu.VMEM((sub * seq_count, cols.total), F32),
                pltpu.VMEM((sub * seq_count, cols.total), F32),
                pltpu.VMEM((seq_count, hidden), F32),
                pltpu.VMEM((seq_count, hidden), BF16),
            ],
        ),
        out_shape=[
            jax.ShapeDtypeStruct((time_steps, seq_count, cols.total), F32),
            jax.ShapeDtypeStruct((time_steps, seq_count, hidden), F32),
            jax.ShapeDtypeStruct((time_steps, seq_count, hidden), BF16),
            jax.ShapeDtypeStruct((4, hidden, plan.columns), BF16),
            jax.ShapeDtypeStruct((4, hidden, hidden), BF16),
        ],
        compiler_params=params(),
        name="forward",
    )(at, dropped, dropped, dropped, *sources)

    def back(b):
        return 2 * blocks - 1 - b

    def before(width):
        return pl.BlockSpec(
            (1, seq_count, width), lambda b, *_: (jnp.maximum(back(b) * sub - 1, 0), 0, 0)
        )

    def back_time(width):
        return pl.BlockSpec((sub, seq_count, width), lambda b, *_: (back(b), 0, 0))

    grad_specs = [back_time(cols.total)] + [back_time(hidden)] * own
    grad_shapes = [cols.total] + [hidden] * own
    grads, *own_rows = pl.pallas_call(
        functools.partial(backward_kernel, cols, own),
        grid_spec=pltpu.PrefetchScalarGridSpec(
            num_scalar_prefetch=1,
            grid=(2 * blocks,),
            in_specs=[
                back_time(cols.total),
                back_time(hidden),
                before(hidden),
                before(cols.total),
                back_time(hidden),
                fixed(seq_count, hidden),
                fixed(seq_count, hidden),
                fixed(seq_count, hidden),
                fixed(seq_count, hidden),
                fixed(4, hidden, hidden),
            ],
            out_specs=grad_specs,
            scratch_shapes=[pltpu.VMEM((seq_count, hidden), F32)] * 3,
        ),
        out_shape=[
            jax.ShapeDtypeStruct((time_steps, seq_count, width), BF16) for width in grad_shapes
        ],
        compiler_params=params(),
        name="backward",
    )(
        row_at[None],
        acts,
        cells,
        cells,
        acts,
        cot_time,
        out_scale,
        act_coef,
        smooth_coef,
        length_wide,
        w_rec,
    )

    if own:
        own_rows = own_rows[0]
    else:
        own_rows = lax.dynamic_slice_in_dim(
            cols.unpack_lanes(grads), row_at * row_count, row_count, 2
        )
    pick = jnp.broadcast_to((groups == 0).astype(BF16)[:, None], (seq_count, row_count))
    part_rows = ceil_to(-(-row_count // seq_n), 8)
    def weight_sums(rows, data, specs, scale):
        columns = sum(spec.block_shape[2] for spec in specs)
        return pl.pallas_call(
            functools.partial(weight_kernel, len(data)),
            grid_spec=pltpu.PrefetchScalarGridSpec(
                num_scalar_prefetch=1,
                grid=(blocks,),
                in_specs=[at_time(row_count), fixed(seq_count, row_count)]
                + specs
                + [fixed(*part.shape) for part in scale],
                out_specs=[fixed(seq_n, part_rows, columns)] * 2,
                scratch_shapes=[pltpu.VMEM((2, seq_n * part_rows, columns), F32)],
            ),
            out_shape=[
                jax.ShapeDtypeStruct((seq_n, part_rows, columns), F32),
                jax.ShapeDtypeStruct((seq_n, part_rows, columns), BF16),
            ],
            compiler_params=params(),
            name="weights",
        )(grp_at[None], rows, pick, *data, *scale)

    hold = lax.optimization_barrier
    keep, send = weight_sums(
        own_rows, [dropped, prev_low], [at_time(wide), at_time(hidden)], [w_scale]
    )
    block = (keep + flip(send, "grp", 1).astype(F32)).astype(BF16)
    swapped = lax.all_to_all(block, "seq", 0, 0, tiled=True)

    own_seqs = lax.dynamic_slice_in_dim(grads, row_at * share, share, 1)
    own_scale = lax.dynamic_slice_in_dim(in_scale, row_at * share, share, 0)
    w_in = cols.pack(weights[:, :, :width_in])
    input_time = jnp.einsum("tsr,rk->tsk", own_seqs, w_in, preferred_element_type=F32)
    input_grad = jnp.swapaxes(input_time * own_scale[None], 0, 1)
    swapped, input_grad = hold((swapped, input_grad))

    total = jnp.sum(swapped.astype(F32), 0).astype(BF16)
    copies = jnp.broadcast_to(total[None], (seq_n,) + total.shape)
    parts = lax.all_to_all(copies, "seq", 0, 0, tiled=True)
    peer = flip(total, "grp", 1)
    ours, theirs = (
        jnp.concatenate([part[:, : width_in + 1], part[:, wide:]], 1).astype(F32)
        for part in (total, peer)
    )
    first = jnp.where(grp_at == 0, ours, theirs)
    second = jnp.where(grp_at == 0, theirs, ours)
    dots = [jnp.sum(a * b) for a, b in ((first, first), (first, second), (second, second))]
    gram = jnp.stack([dots[0], dots[1], dots[1], dots[2]]).reshape(2, 2)
    gram = exchange_sum(exchange_sum(gram, "row"), "seq")
    parts, gram = hold((parts, gram))
    everyone = parts.reshape(seq_n * part_rows, wide + hidden)[:row_count].astype(F32)
    return (
        input_grad,
        everyone[None, :, :width_in],
        everyone[None, :, wide:],
        everyone[None, :, width_in],
        gram,
    )


def solution(mesh):
    return jax.shard_map(
        local,
        mesh=mesh,
        in_specs=(
            P(("grp", "seq"), None, None),
            P(("grp", "seq"), None),
            P(("grp", "seq"), None),
            P(("grp", "seq")),
            P(("grp", "seq")),
            P("row", None),
            P("row", None),
            P("row", None),
            P("row"),
            P(("grp", "seq"), None, None),
        ),
        out_specs=(
            P(("grp", "seq", "row"), None, None),
            P("grp", "row", None),
            P("grp", "row", None),
            P("grp", "row"),
            P(),
        ),
        check_vma=False,
    )
```

```python
import functools

import jax
import jax.numpy as jnp
from jax import lax
from jax.experimental import pallas as pl
from jax.experimental.pallas import tpu as pltpu
from jax.sharding import PartitionSpec as P

ACTIVATION_COEF = 2.0
TAR_BETA = 1.0
KEEP_INPUT = 0.75
KEEP_OUTPUT = 0.6
KEEP_WEIGHT = 0.5
LANES = 128
TILE = 256
BF16 = jnp.bfloat16
F32 = jnp.float32
OVER_ROWS = (((0,), (0,)), ((), ()))


def ceil_to(value, step):
    return -(-value // step) * step


def dot(left, right):
    return jnp.dot(left, right, preferred_element_type=F32)


def flip(block, axis, bit):
    count = lax.axis_size(axis)
    return lax.ppermute(block, axis, [(at, at ^ bit) for at in range(count)])


def exchange_sum(block, axis):
    count = lax.axis_size(axis)
    if count not in (2, 4):
        return lax.psum(block, axis)
    parts = [block] + [flip(block, axis, bit) for bit in range(1, count)]
    while len(parts) > 1:
        parts = [parts[at] + parts[at + 1] for at in range(0, len(parts), 2)]
    return parts[0]


def sigmoid(value):
    return 0.5 * jnp.tanh(0.5 * value) + 0.5


class Columns:
    def __init__(self, hidden):
        self.hidden = hidden
        self.full = hidden // LANES
        self.rest = hidden - self.full * LANES
        assert 0 < 4 * self.rest <= LANES
        self.total = 4 * hidden
        self.order = (self.full,) + tuple(range(self.full))

    def units(self, j):
        return j * LANES, min((j + 1) * LANES, self.hidden)

    def gates(self, j):
        return 4 * j * LANES, min(4 * (j + 1) * LANES, self.total)

    def gate(self, j, q):
        width = LANES if j < self.full else self.rest
        start = 4 * j * LANES + q * width
        return start, start + width

    def pack(self, gated):
        parts = []
        for j in range(self.full + 1):
            first, last = self.units(j)
            parts.append(gated[:, first:last].reshape((-1,) + gated.shape[2:]))
        return jnp.concatenate(parts, 0)

    def unpack_lanes(self, packed):
        parts = []
        for q in range(4):
            for j in range(self.full + 1):
                first, last = self.gate(j, q)
                parts.append(packed[..., first:last])
        return jnp.concatenate(parts, -1)


def drop_kernel(width, tok_ref, mask_ref, drop_ref):
    scale = mask_ref[...].astype(F32) * (1.0 / KEEP_INPUT)
    for k in range(tok_ref.shape[0]):
        drop_ref[k, :, :width] = (tok_ref[k].astype(F32) * scale).astype(BF16)
        drop_ref[k, :, width:] = jnp.ones_like(drop_ref[k, :, width:])


def turned_dot(left, right):
    return lax.dot_general(left, right, (((1,), (1,)), ((), ())), preferred_element_type=F32)


def identity(size):
    line = lax.broadcasted_iota(jnp.int32, (size, size), 0)
    same = line == lax.broadcasted_iota(jnp.int32, (size, size), 1)
    return same.astype(F32).astype(BF16)


def shard_kernel(plan, at_ref, in_ref, rec_ref, mask_ref, bias_ref, own_ref, *mine_ref):
    rows, width = in_ref.shape
    hidden = rec_ref.shape[1]
    bias = bias_ref[...]
    high = bias.astype(BF16)
    pair = jnp.concatenate([high, (bias - high.astype(F32)).astype(BF16)], 0)
    scale = mask_ref[...].astype(F32) / KEEP_WEIGHT
    own_ref[:, :width] = in_ref[...]
    own_ref[:, width : width + 2] = turned_dot(identity(rows), pair).astype(BF16)
    own_ref[:, plan.wide : plan.wide + hidden] = (rec_ref[...].astype(F32) * scale).astype(BF16)
    own_ref[:, plan.wide + hidden :] = jnp.zeros_like(own_ref[:, plan.wide + hidden :])
    for ref in mine_ref:
        ref[...] = own_ref[plan.window(at_ref[1], at_ref[2], 0, plan.rows)]


class Plan:
    def __init__(self, hidden, wide):
        self.wide = wide
        self.columns = ceil_to(wide + hidden, LANES)
        self.row_step = hidden // 32 * 16
        self.rows = hidden - self.row_step
        self.first = ceil_to(self.rows // 2, 16)
        self.column_step = self.columns // LANES // 2 * LANES
        self.cut = self.columns - self.column_step

    def window(self, seq_at, grp_at, start, count):
        half = (seq_at ^ (seq_at >> 1)) & 1
        return (
            pl.ds(pl.multiple_of(half * self.row_step + start, 16), count),
            pl.ds(pl.multiple_of(grp_at * self.column_step, LANES), self.cut),
        )

    def places(self):
        first, rest = self.first, self.rows - self.first
        return [
            (0, 1, 0, 0, self.rows),
            (0, 2, 0, 0, self.rows),
            (0, 1, 1, 0, first),
            (0, 2, 1, 0, first),
            (0, 1, 1, first, rest),
            (0, 2, 1, first, rest),
            (0, 3, 0, 0, self.rows),
            (1, 3, 1, 0, first),
            (1, 3, 1, first, rest),
        ]


def forward_kernel(cols, plan, sub, pieced, at_ref, first_ref, second_ref, third_ref, *refs):
    count = 5 if pieced else 1
    sources = refs[:count]
    act_ref, cell_ref, prev_ref, w_out, rec_out, w_ref, turned, even, odd, cell_s, low_s, sems = refs[
        count:
    ]
    seqs, width = first_ref.shape[1:]
    steps = act_ref.shape[0]
    hidden = cols.hidden

    def columns_of(rows_ref, start, stop, first, last):
        parts = []
        for j in range(cols.full + 1):
            unit, _ = cols.units(j)
            for q in range(4):
                low, high = cols.gate(j, q)
                if low >= start and high <= stop:
                    parts.append(rows_ref[q, unit : unit + high - low, first:last])
        return jnp.concatenate(parts, 0)

    copies = [
        pltpu.make_async_copy(w_ref.at[:, :, :width], w_out, sems.at[0]),
        pltpu.make_async_copy(w_ref.at[:, :, width:], rec_out, sems.at[1]),
    ]

    @pl.when(pl.program_id(0) == 0)
    def _():
        if pieced:
            row_at, seq_at, grp_at = at_ref[0], at_ref[1], at_ref[2]
            w_ref[row_at] = sources[0][...]
            for gi in range(2):
                line = [0, 0]
                for array, k, m, start, size in plan.places():
                    window = plan.window(seq_at ^ m, grp_at ^ gi, start, size)
                    piece = sources[1 + 2 * gi + array][line[array] : line[array] + size]
                    w_ref[(row_at ^ k,) + window] = piece
                    line[array] += size
        else:
            w_ref[...] = sources[0][...]
        for copy in copies:
            copy.start()
        turned[...] = turned_dot(
            identity(hidden), columns_of(w_ref, 0, cols.total, width, width + hidden)
        ).astype(BF16)
        cell_s[...] = jnp.zeros_like(cell_s)
        low_s[...] = jnp.zeros_like(low_s)
        even[...] = turned_dot(
            first_ref[...].reshape(sub * seqs, width), columns_of(w_ref, 0, cols.total, 0, width)
        )

    lane = lax.broadcasted_iota(jnp.int32, (1, 4 * cols.rest), 1)
    tanh_lane = (lane >= 2 * cols.rest) & (lane < 3 * cols.rest)
    rest_mul = jnp.where(tanh_lane, 1.0, 0.5)
    rest_add = jnp.where(tanh_lane, 0.0, 0.5)
    spans = [cols.units(j) for j in range(cols.full + 1)]
    cells = [cell_s[:, a:b] for a, b in spans]
    lows = [low_s[:, a:b] for a, b in spans]
    chunk = ceil_to(-(-cols.total // sub), TILE)
    for k in range(steps):
        u, v = divmod(k, sub)
        now, later = (even, odd) if u % 2 == 0 else (odd, even)
        start, stop = chunk * v, min(chunk * (v + 1), cols.total)
        if start < stop:
            rows = (second_ref, third_ref)[u][...].reshape(sub * seqs, width)
            later[:, start:stop] = turned_dot(rows, columns_of(w_ref, start, stop, 0, width))
        for (a, b), low in zip(spans, lows):
            prev_ref[k, :, a:b] = low
        low = jnp.concatenate(lows, 1)
        lows = [None] * len(spans)
        for j in cols.order:
            first, last = cols.gates(j)
            pre = now[v * seqs : (v + 1) * seqs, first:last] + dot(low, turned[:, first:last])
            if j < cols.full:
                gate_i, gate_f, gate_g, gate_o = (
                    pre[:, q * LANES : (q + 1) * LANES] for q in range(4)
                )
                gate_i, gate_f, gate_o = sigmoid(gate_i), sigmoid(gate_f), sigmoid(gate_o)
                gate_g = jnp.tanh(gate_g)
                for q, gate in enumerate((gate_i, gate_f, gate_g, gate_o)):
                    a, b = cols.gate(j, q)
                    act_ref[k, :, a:b] = gate
            else:
                act = rest_mul * jnp.tanh(rest_mul * pre) + rest_add
                act_ref[k, :, first:last] = act
                gate_i, gate_f, gate_g, gate_o = (
                    act[:, q * cols.rest : (q + 1) * cols.rest] for q in range(4)
                )
            a, b = spans[j]
            cells[j] = gate_f * cells[j] + gate_i * gate_g
            cell_ref[k, :, a:b] = cells[j]
            lows[j] = (gate_o * jnp.tanh(cells[j])).astype(BF16)
    for j, (a, b) in enumerate(spans):
        cell_s[:, a:b] = cells[j]
        low_s[:, a:b] = lows[j]

    @pl.when(pl.program_id(0) == pl.num_programs(0) - 1)
    def _():
        for copy in copies:
            copy.wait()


def backward_kernel(
    cols,
    own,
    at_ref,
    act_ref,
    cell_ref,
    before_ref,
    act_before_ref,
    cot_ref,
    mask_ref,
    ratio_ref,
    length_row_ref,
    rec_ref,
    *refs,
):
    grad_ref = refs[6 if own else 0]
    if own:
        drop_ref, prev_ref, drop_end_ref, prev_end_ref, group_ref, weight_mask_ref = refs[:6]
        keep_ref, send_ref = refs[7:9]
        own_s, sides, pick, sums = refs[9:13]
    dcell_s, recur_s, smooth_s, tanh_s, scale_s, coef_s, smooth_coef_s, length_s = refs[-8:]
    steps, seqs, _ = act_ref.shape
    hidden_n = cols.hidden
    place = pl.program_id(0)
    block = pl.num_programs(0) - 1 - place
    spans = [cols.units(j) for j in range(cols.full + 1)]

    @pl.when(place == 0)
    def _():
        dcell_s[...] = jnp.zeros_like(dcell_s)
        recur_s[...] = jnp.zeros_like(recur_s)
        smooth_s[...] = jnp.zeros_like(smooth_s)
        tanh_s[...] = jnp.tanh(cell_ref[steps - 1])
        ratio = column_of(ratio_ref[...])
        length_s[...] = column_of(length_row_ref[...])
        smooth_coef_s[...] = 2.0 * TAR_BETA * ratio
        scale_s[...] = mask_ref[...].astype(F32) * (1.0 / KEEP_OUTPUT)
        for a, b in spans:
            scale = scale_s[:, a:b]
            coef_s[:, a:b] = 2.0 * ACTIVATION_COEF * ratio[:, : b - a] * scale * scale
        if own:
            sums[...] = jnp.zeros_like(sums)
            sides[...] = jnp.zeros_like(sides)
            first = (group_ref[...] == 0.0).astype(F32).astype(BF16)
            for k in range(steps):
                pick[:, k * seqs : (k + 1) * seqs] = first

    inner = (block > 0).astype(F32)
    rec = jnp.concatenate([rec_ref[q, a:b, :hidden_n] for a, b in spans for q in range(4)], 0)
    jobs = []
    if own:
        width = drop_ref.shape[2]
        for kind, count in enumerate((width, hidden_n)):
            for start in range(0, count, TILE):
                jobs += [(kind, start, min(start + TILE, count), q) for q in range(2)]

    def weight_job(n, data):
        kind, start, stop, q = jobs[n]
        values = data[kind][...].reshape(steps * seqs, data[kind].shape[2])[:, start:stop]
        base = kind * width
        sums[q, :hidden_n, base + start : base + stop] += dot(sides[q], values)

    def gates_at(k, j):
        if j < cols.full:
            return [act_ref[k, :, a:b] for a, b in (cols.gate(j, q) for q in range(4))]
        first, last = cols.gates(j)
        packed = act_ref[k, :, first:last]
        return [packed[:, q * cols.rest : (q + 1) * cols.rest] for q in range(4)]

    for k in range(steps - 1, -1, -1):
        late = steps - 1 - k
        for n in range(late * len(jobs) // steps, (late + 1) * len(jobs) // steps):
            weight_job(n, (drop_ref, prev_ref))
        for j in cols.order:
            a, b = spans[j]
            gate_i, gate_f, gate_g, gate_o = gates_at(k, j)
            tanh_cell = tanh_s[:, a:b]
            hidden = gate_o * tanh_cell
            low, high = cols.gate(j, 3)
            if k > 0:
                cell_before = cell_ref[k - 1, :, a:b]
                out_before = act_ref[k - 1, :, low:high]
            else:
                cell_before = before_ref[0, :, a:b] * inner
                out_before = act_before_ref[0, :, low:high]
            tanh_before = jnp.tanh(cell_before)
            tanh_s[:, a:b] = tanh_before
            valid = length_s[:, : b - a] > (block * steps + k).astype(F32)
            smooth = smooth_coef_s[:, : b - a] * (hidden - out_before * tanh_before)
            if k == 0:
                smooth = smooth * inner
            smooth = jnp.where(valid, smooth, 0.0)
            direct = scale_s[:, a:b] * cot_ref[k, :, a:b].astype(F32) + coef_s[:, a:b] * hidden
            direct = jnp.where(valid, direct, 0.0) + smooth - smooth_s[:, a:b]
            smooth_s[:, a:b] = smooth
            dhidden = direct + recur_s[:, a:b]
            total = dcell_s[:, a:b] + dhidden * (gate_o * (1.0 - tanh_cell * tanh_cell))
            dcell_s[:, a:b] = total * gate_f
            grads = [
                (total * (gate_g * gate_i * (1.0 - gate_i))).astype(BF16),
                (total * (cell_before * gate_f * (1.0 - gate_f))).astype(BF16),
                (total * (gate_i * (1.0 - gate_g * gate_g))).astype(BF16),
                (dhidden * (tanh_cell * gate_o * (1.0 - gate_o))).astype(BF16),
            ]
            first, last = cols.gates(j)
            grad_ref[k, :, first:last] = jnp.concatenate(grads, 1)
            if own:
                mine = grads[3]
                for q in range(3):
                    mine = jnp.where(at_ref[0] == q, grads[q], mine)
                own_s[k * seqs : (k + 1) * seqs, a:b] = mine
        recur_s[...] = dot(grad_ref[k], rec)
    if own:
        turned = own_s[...].T
        first = turned * pick[...]
        sides[0] = first
        sides[1] = turned - first

        @pl.when(block == 0)
        def _():
            for n in range(len(jobs)):
                weight_job(n, (drop_end_ref, prev_end_ref))
            scale = weight_mask_ref[...].astype(F32) * (1.0 / KEEP_WEIGHT)
            for q in range(2):
                sums[q, :hidden_n, width:] = sums[q, :hidden_n, width:] * scale
            hand_out(at_ref[2], sums, keep_ref, send_ref)


def hand_out(grp_at, sums, keep_ref, send_ref):
    rows = keep_ref.shape[1]
    for part in range(keep_ref.shape[0]):
        span = slice(part * rows, (part + 1) * rows)
        keep_ref[part] = sums[grp_at, span]
        send_ref[part] = sums[1 - grp_at, span].astype(BF16)


def weight_kernel(grp_ref, rows_ref, group_ref, drop_ref, prev_ref, mask_ref, keep_ref, send_ref, sums, pick):
    steps, seqs, own = rows_ref.shape
    place = pl.program_id(0)

    @pl.when(place == 0)
    def _():
        sums[...] = jnp.zeros_like(sums)
        one = (column_of(group_ref[...]) == 0.0).astype(F32).astype(BF16)
        for at in range(0, own, LANES):
            width = min(LANES, own - at)
            pick[:, at : at + width] = one[:, :width]

    grads = rows_ref[...]
    first = (grads * pick[...][None]).reshape(steps * seqs, own)
    second = grads.reshape(steps * seqs, own) - first
    start = 0
    for ref in (drop_ref, prev_ref):
        width = ref.shape[2]
        values = ref[...].reshape(steps * seqs, width)
        for at, part in enumerate((first, second)):
            sums[at, :own, start : start + width] += lax.dot_general(
                part, values, OVER_ROWS, preferred_element_type=F32
            )
        start += width

    @pl.when(place == pl.num_programs(0) - 1)
    def _():
        scale = mask_ref[...].astype(F32) * (1.0 / KEEP_WEIGHT)
        for at in range(2):
            part = (at, slice(0, own), slice(start - width, start))
            sums[part] = sums[part] * scale
        hand_out(grp_ref[0], sums, keep_ref, send_ref)


def params(megabytes):
    return pltpu.CompilerParams(
        dimension_semantics=("arbitrary",), vmem_limit_bytes=megabytes << 20
    )


def fixed(*shape):
    return pl.BlockSpec(shape, lambda *_: (0,) * len(shape), pipeline_mode=pl.Buffered(1))


def column_of(row):
    return jnp.broadcast_to(row, (LANES, row.shape[1])).T


def gather_pieces(plan, mine, counts, beside):
    hold = lax.optimization_barrier
    cut = plan.cut
    one, two, beside, counts = hold(
        (flip(mine, "row", 1), flip(mine, "row", 2), beside, counts + flip(counts, "grp", 1))
    )
    near = jnp.stack([one, two])
    near_x, near_y, three, counts = hold(
        (
            flip(near[:, : plan.first], "seq", 1),
            flip(near[:, plan.first :], "seq", 2),
            flip(two, "row", 1),
            counts + flip(counts, "seq", 1),
        )
    )
    early = jnp.concatenate([part.reshape(-1, cut) for part in (near, near_x, near_y, three)], 0)
    last_x, last_y, early_other, counts = hold(
        (
            flip(three[: plan.first], "seq", 1),
            flip(three[plan.first :], "seq", 2),
            flip(early, "grp", 1),
            counts + flip(counts, "seq", 2),
        )
    )
    late = jnp.concatenate([last_x, last_y], 0)
    return early, late, early_other, flip(late, "grp", 1), counts, beside


def local(
    tokens,
    in_mask,
    out_mask,
    lengths,
    groups,
    input_gate_weight,
    w_recur,
    weight_mask,
    bias,
    cotangent,
):
    seq_count, time_steps, width_in = tokens.shape
    hidden = cotangent.shape[2]
    row_count = input_gate_weight.shape[0]
    row_at = lax.axis_index("row")
    grp_at = lax.axis_index("grp")
    seq_at = lax.axis_index("seq")
    rows_n, seq_n = lax.axis_size("row"), lax.axis_size("seq")
    cols = Columns(hidden)
    wide = ceil_to(width_in + 2, LANES)
    share = seq_count // rows_n
    own = row_count == hidden
    pieced = own and rows_n == 4 and seq_n == 4 and lax.axis_size("grp") == 2

    plan = Plan(hidden, wide)
    at = jnp.stack([row_at, seq_at, grp_at]).astype(jnp.int32)
    own_weights, *mine = pl.pallas_call(
        functools.partial(shard_kernel, plan),
        grid_spec=pltpu.PrefetchScalarGridSpec(
            num_scalar_prefetch=1,
            grid=(1,),
            in_specs=[
                fixed(row_count, width_in),
                fixed(row_count, hidden),
                fixed(row_count, hidden),
                fixed(1, row_count),
            ],
            out_specs=[fixed(row_count, plan.columns)] + [fixed(plan.rows, plan.cut)] * pieced,
        ),
        out_shape=[jax.ShapeDtypeStruct((row_count, plan.columns), BF16)]
        + [jax.ShapeDtypeStruct((plan.rows, plan.cut), BF16)] * pieced,
        compiler_params=params(58),
        name="shard",
    )(at, input_gate_weight, w_recur, weight_mask, bias[None])
    sub = max(s for s in range(1, 8) if time_steps % (2 * s) == 0)
    steps = 2 * sub
    blocks = time_steps // steps

    def at_time(width):
        return pl.BlockSpec((steps, seq_count, width), lambda b, *_: (b, 0, 0))

    dropped = pl.pallas_call(
        functools.partial(drop_kernel, width_in),
        grid=(blocks,),
        in_specs=[at_time(width_in), fixed(seq_count, width_in)],
        out_specs=at_time(wide),
        out_shape=jax.ShapeDtypeStruct((time_steps, seq_count, wide), BF16),
        compiler_params=params(58),
        name="drop",
    )(jnp.swapaxes(tokens, 0, 1), in_mask)
    cot_time = jnp.swapaxes(cotangent, 0, 1)

    group_hot = (groups[:, None] == jnp.arange(2)[None, :]).astype(F32)
    valid_count = jnp.clip(lengths, 0, time_steps).astype(F32)
    counts = jnp.sum(group_hot * valid_count[:, None], 0)
    if pieced:
        *pieces, counts, dropped = gather_pieces(plan, mine[0], counts, dropped)
        sources = [own_weights] + pieces
    else:
        counts = lax.psum(counts, ("grp", "seq"))
        whole = lax.all_gather(own_weights, "row", axis=0, tiled=True)
        sources = [whole.reshape(4, hidden, plan.columns)]
    group_ratio = jnp.sum(counts) / counts
    seq_ratio = jnp.sum(group_hot * group_ratio[None, :], 1)

    acts, cells, prev_low, weights, w_rec = pl.pallas_call(
        functools.partial(forward_kernel, cols, plan, sub, pieced),
        grid_spec=pltpu.PrefetchScalarGridSpec(
            num_scalar_prefetch=1,
            grid=(blocks,),
            in_specs=[
                fixed(sub, seq_count, wide),
                pl.BlockSpec((sub, seq_count, wide), lambda b, *_: (2 * b + 1, 0, 0)),
                pl.BlockSpec(
                    (sub, seq_count, wide),
                    lambda b, *_: (jnp.minimum(2 * b + 2, 2 * blocks - 1), 0, 0),
                ),
            ]
            + [fixed(*source.shape) for source in sources],
            out_specs=[
                at_time(cols.total),
                at_time(hidden),
                at_time(hidden),
                pl.BlockSpec(memory_space=pl.ANY),
                pl.BlockSpec(memory_space=pl.ANY),
            ],
            scratch_shapes=[
                pltpu.VMEM((4, hidden, plan.columns), BF16),
                pltpu.VMEM((hidden, cols.total), BF16),
                pltpu.VMEM((sub * seq_count, cols.total), F32),
                pltpu.VMEM((sub * seq_count, cols.total), F32),
                pltpu.VMEM((seq_count, hidden), F32),
                pltpu.VMEM((seq_count, hidden), BF16),
                pltpu.SemaphoreType.DMA((2,)),
            ],
        ),
        out_shape=[
            jax.ShapeDtypeStruct((time_steps, seq_count, cols.total), F32),
            jax.ShapeDtypeStruct((time_steps, seq_count, hidden), F32),
            jax.ShapeDtypeStruct((time_steps, seq_count, hidden), BF16),
            jax.ShapeDtypeStruct((4, hidden, wide), BF16),
            jax.ShapeDtypeStruct((4, hidden, plan.columns - wide), BF16),
        ],
        compiler_params=params(58),
        name="forward",
    )(at, dropped, dropped, dropped, *sources)

    def back(b):
        return blocks - 1 - b

    def before(width):
        return pl.BlockSpec(
            (1, seq_count, width), lambda b, *_: (jnp.maximum(back(b) * steps - 1, 0), 0, 0)
        )

    def back_time(width):
        return pl.BlockSpec((steps, seq_count, width), lambda b, *_: (back(b), 0, 0))

    def later_time(width):
        return pl.BlockSpec(
            (steps, seq_count, width), lambda b, *_: (jnp.minimum(back(b) + 1, blocks - 1), 0, 0)
        )

    part_rows = ceil_to(-(-row_count // seq_n), 8)
    columns = wide + hidden
    group_row = groups.astype(F32)[None]
    sum_specs = [fixed(seq_n, part_rows, columns)] * 2
    sum_shapes = [
        jax.ShapeDtypeStruct((seq_n, part_rows, columns), F32),
        jax.ShapeDtypeStruct((seq_n, part_rows, columns), BF16),
    ]
    sum_scratch = pltpu.VMEM((2, seq_n * part_rows, columns), F32)
    per_unit = pltpu.VMEM((seq_count, hidden), F32)
    own_specs, own_arrays, own_scratch = [], [], []
    if own:
        own_specs = [
            later_time(wide),
            later_time(hidden),
            fixed(steps, seq_count, wide),
            fixed(steps, seq_count, hidden),
            fixed(1, seq_count),
            fixed(row_count, hidden),
        ]
        own_arrays = [dropped, prev_low, dropped, prev_low, group_row, weight_mask]
        own_scratch = [
            pltpu.VMEM((steps * seq_count, hidden), BF16),
            pltpu.VMEM((2, hidden, steps * seq_count), BF16),
            pltpu.VMEM((1, steps * seq_count), BF16),
            sum_scratch,
        ]
    grads, *sums = pl.pallas_call(
        functools.partial(backward_kernel, cols, own),
        grid_spec=pltpu.PrefetchScalarGridSpec(
            num_scalar_prefetch=1,
            grid=(blocks,),
            in_specs=[
                back_time(cols.total),
                back_time(hidden),
                before(hidden),
                before(cols.total),
                back_time(hidden),
                fixed(seq_count, hidden),
                fixed(1, seq_count),
                fixed(1, seq_count),
                fixed(4, hidden, plan.columns - wide),
            ]
            + own_specs,
            out_specs=[back_time(cols.total)] + sum_specs * own,
            scratch_shapes=own_scratch
            + [per_unit] * 6
            + [pltpu.VMEM((seq_count, LANES), F32)] * 2,
        ),
        out_shape=[jax.ShapeDtypeStruct((time_steps, seq_count, cols.total), BF16)]
        + sum_shapes * own,
        compiler_params=params(58),
        name="backward",
    )(
        at,
        acts,
        cells,
        cells,
        acts,
        cot_time,
        out_mask,
        seq_ratio[None],
        lengths.astype(F32)[None],
        w_rec,
        *own_arrays,
    )

    if not own:
        own_rows = lax.dynamic_slice_in_dim(
            cols.unpack_lanes(grads), row_at * row_count, row_count, 2
        )
        sums = pl.pallas_call(
            weight_kernel,
            grid_spec=pltpu.PrefetchScalarGridSpec(
                num_scalar_prefetch=1,
                grid=(blocks,),
                in_specs=[
                    at_time(row_count),
                    fixed(1, seq_count),
                    at_time(wide),
                    at_time(hidden),
                    fixed(row_count, hidden),
                ],
                out_specs=sum_specs,
                scratch_shapes=[sum_scratch, pltpu.VMEM((seq_count, row_count), BF16)],
            ),
            out_shape=sum_shapes,
            compiler_params=params(58),
            name="weights",
        )(grp_at[None], own_rows, group_row, dropped, prev_low, weight_mask)
    keep, send = sums

    hold = lax.optimization_barrier
    block = (keep + flip(send, "grp", 1).astype(F32)).astype(BF16)
    swapped = lax.all_to_all(block, "seq", 0, 0, tiled=True)

    own_seqs = lax.dynamic_slice_in_dim(grads, row_at * share, share, 1)
    own_scale = lax.dynamic_slice_in_dim(in_mask, row_at * share, share, 0).astype(F32) / KEEP_INPUT
    w_in = cols.pack(weights[:, :, :width_in])
    input_time = jnp.einsum("tsr,rk->tsk", own_seqs, w_in, preferred_element_type=F32)
    input_grad = jnp.swapaxes(input_time * own_scale[None], 0, 1)
    swapped, input_grad = hold((swapped, input_grad))

    total = jnp.sum(swapped.astype(F32), 0).astype(BF16)
    copies = jnp.broadcast_to(total[None], (seq_n,) + total.shape)
    parts = lax.all_to_all(copies, "seq", 0, 0, tiled=True)
    peer = flip(total, "grp", 1)
    ours, theirs = (
        jnp.concatenate([part[:, : width_in + 1], part[:, wide:]], 1).astype(F32)
        for part in (total, peer)
    )
    first = jnp.where(grp_at == 0, ours, theirs)
    second = jnp.where(grp_at == 0, theirs, ours)
    dots = [jnp.sum(a * b) for a, b in ((first, first), (first, second), (second, second))]
    gram = jnp.stack([dots[0], dots[1], dots[1], dots[2]]).reshape(2, 2)
    gram = exchange_sum(exchange_sum(gram, "row"), "seq")
    parts, gram = hold((parts, gram))
    everyone = parts.reshape(seq_n * part_rows, wide + hidden)[:row_count].astype(F32)
    return (
        input_grad,
        everyone[None, :, :width_in],
        everyone[None, :, wide:],
        everyone[None, :, width_in],
        gram,
    )


def solution(mesh):
    return jax.shard_map(
        local,
        mesh=mesh,
        in_specs=(
            P(("grp", "seq"), None, None),
            P(("grp", "seq"), None),
            P(("grp", "seq"), None),
            P(("grp", "seq")),
            P(("grp", "seq")),
            P("row", None),
            P("row", None),
            P("row", None),
            P("row"),
            P(("grp", "seq"), None, None),
        ),
        out_specs=(
            P(("grp", "seq", "row"), None, None),
            P("grp", "row", None),
            P("grp", "row", None),
            P("grp", "row"),
            P(),
        ),
        check_vma=False,
    )
```

```python
import functools

import jax
import jax.numpy as jnp
from jax import lax
from jax.experimental import pallas as pl
from jax.experimental.pallas import tpu as pltpu
from jax.sharding import PartitionSpec as P

ACTIVATION_COEF = 2.0
TAR_BETA = 1.0
KEEP_INPUT = 0.75
KEEP_OUTPUT = 0.6
KEEP_WEIGHT = 0.5
LANES = 128
TILE = 256
BF16 = jnp.bfloat16
F32 = jnp.float32
OVER_ROWS = (((0,), (0,)), ((), ()))


def ceil_to(value, step):
    return -(-value // step) * step


def dot(left, right):
    return jnp.dot(left, right, preferred_element_type=F32)


def flip(block, axis, bit):
    count = lax.axis_size(axis)
    return lax.ppermute(block, axis, [(at, at ^ bit) for at in range(count)])


def exchange_sum(block, axis):
    count = lax.axis_size(axis)
    if count not in (2, 4):
        return lax.psum(block, axis)
    parts = [block] + [flip(block, axis, bit) for bit in range(1, count)]
    while len(parts) > 1:
        parts = [parts[at] + parts[at + 1] for at in range(0, len(parts), 2)]
    return parts[0]


def sigmoid(value):
    return 0.5 * jnp.tanh(0.5 * value) + 0.5


class Columns:
    def __init__(self, hidden):
        self.hidden = hidden
        self.full = hidden // LANES
        self.rest = hidden - self.full * LANES
        assert 0 < 4 * self.rest <= LANES
        self.total = 4 * hidden
        self.order = (self.full,) + tuple(range(self.full))

    def units(self, j):
        return j * LANES, min((j + 1) * LANES, self.hidden)

    def gates(self, j):
        return 4 * j * LANES, min(4 * (j + 1) * LANES, self.total)

    def gate(self, j, q):
        width = LANES if j < self.full else self.rest
        start = 4 * j * LANES + q * width
        return start, start + width

    def pack(self, gated):
        parts = []
        for j in range(self.full + 1):
            first, last = self.units(j)
            parts.append(gated[:, first:last].reshape((-1,) + gated.shape[2:]))
        return jnp.concatenate(parts, 0)

    def unpack_lanes(self, packed):
        parts = []
        for q in range(4):
            for j in range(self.full + 1):
                first, last = self.gate(j, q)
                parts.append(packed[..., first:last])
        return jnp.concatenate(parts, -1)


def drop_kernel(width, tok_ref, mask_ref, drop_ref):
    scale = mask_ref[...].astype(F32) * (1.0 / KEEP_INPUT)
    for k in range(tok_ref.shape[0]):
        drop_ref[k, :, :width] = (tok_ref[k].astype(F32) * scale).astype(BF16)
        drop_ref[k, :, width:] = jnp.ones_like(drop_ref[k, :, width:])


def turned_dot(left, right):
    return lax.dot_general(left, right, (((1,), (1,)), ((), ())), preferred_element_type=F32)


def identity(size):
    line = lax.broadcasted_iota(jnp.int32, (size, size), 0)
    same = line == lax.broadcasted_iota(jnp.int32, (size, size), 1)
    return same.astype(F32).astype(BF16)


def shard_kernel(plan, at_ref, in_ref, rec_ref, mask_ref, bias_ref, own_ref, *mine_ref):
    rows, width = in_ref.shape
    hidden = rec_ref.shape[1]
    bias = bias_ref[...]
    high = bias.astype(BF16)
    pair = jnp.concatenate([high, (bias - high.astype(F32)).astype(BF16)], 0)
    scale = mask_ref[...].astype(F32) / KEEP_WEIGHT
    own_ref[:, :width] = in_ref[...]
    own_ref[:, width : width + 2] = turned_dot(identity(rows), pair).astype(BF16)
    own_ref[:, plan.wide : plan.wide + hidden] = (rec_ref[...].astype(F32) * scale).astype(BF16)
    own_ref[:, plan.wide + hidden :] = jnp.zeros_like(own_ref[:, plan.wide + hidden :])
    for ref in mine_ref:
        ref[...] = own_ref[plan.window(at_ref[1], at_ref[2], 0, plan.rows)]


class Plan:
    def __init__(self, hidden, wide):
        self.wide = wide
        self.columns = ceil_to(wide + hidden, LANES)
        self.row_step = hidden // 32 * 16
        self.rows = hidden - self.row_step
        self.first = ceil_to(self.rows // 2, 16)
        self.column_step = self.columns // LANES // 2 * LANES
        self.cut = self.columns - self.column_step

    def window(self, seq_at, grp_at, start, count):
        half = (seq_at ^ (seq_at >> 1)) & 1
        return (
            pl.ds(pl.multiple_of(half * self.row_step + start, 16), count),
            pl.ds(pl.multiple_of(grp_at * self.column_step, LANES), self.cut),
        )

    def places(self):
        first, rest = self.first, self.rows - self.first
        return [
            (0, 1, 0, 0, self.rows),
            (0, 2, 0, 0, self.rows),
            (0, 1, 1, 0, first),
            (0, 2, 1, 0, first),
            (0, 1, 1, first, rest),
            (0, 2, 1, first, rest),
            (0, 3, 0, 0, self.rows),
            (1, 3, 1, 0, first),
            (1, 3, 1, first, rest),
        ]


def forward_kernel(cols, plan, sub, pieced, at_ref, first_ref, second_ref, third_ref, *refs):
    count = 5 if pieced else 1
    sources = refs[:count]
    act_ref, cell_ref, prev_ref, w_out, rec_out, w_ref, turned, even, odd, cell_s, low_s, sems = refs[
        count:
    ]
    seqs, width = first_ref.shape[1:]
    steps = act_ref.shape[0]
    hidden = cols.hidden

    def columns_of(rows_ref, start, stop, first, last):
        parts = []
        for j in range(cols.full + 1):
            unit, _ = cols.units(j)
            for q in range(4):
                low, high = cols.gate(j, q)
                if low >= start and high <= stop:
                    parts.append(rows_ref[q, unit : unit + high - low, first:last])
        return jnp.concatenate(parts, 0)

    copies = [
        pltpu.make_async_copy(w_ref.at[:, :, :width], w_out, sems.at[0]),
        pltpu.make_async_copy(w_ref.at[:, :, width:], rec_out, sems.at[1]),
    ]

    @pl.when(pl.program_id(0) == 0)
    def _():
        if pieced:
            row_at, seq_at, grp_at = at_ref[0], at_ref[1], at_ref[2]
            w_ref[row_at] = sources[0][...]
            for gi in range(2):
                line = [0, 0]
                for array, k, m, start, size in plan.places():
                    window = plan.window(seq_at ^ m, grp_at ^ gi, start, size)
                    piece = sources[1 + 2 * gi + array][line[array] : line[array] + size]
                    w_ref[(row_at ^ k,) + window] = piece
                    line[array] += size
        else:
            w_ref[...] = sources[0][...]
        for copy in copies:
            copy.start()
        turned[...] = turned_dot(
            identity(hidden), columns_of(w_ref, 0, cols.total, width, width + hidden)
        ).astype(BF16)
        cell_s[...] = jnp.zeros_like(cell_s)
        low_s[...] = jnp.zeros_like(low_s)
        even[...] = turned_dot(
            first_ref[...].reshape(sub * seqs, width), columns_of(w_ref, 0, cols.total, 0, width)
        )

    lane = lax.broadcasted_iota(jnp.int32, (1, 4 * cols.rest), 1)
    tanh_lane = (lane >= 2 * cols.rest) & (lane < 3 * cols.rest)
    rest_mul = jnp.where(tanh_lane, 1.0, 0.5)
    rest_add = jnp.where(tanh_lane, 0.0, 0.5)
    spans = [cols.units(j) for j in range(cols.full + 1)]
    cells = [cell_s[:, a:b] for a, b in spans]
    lows = [low_s[:, a:b] for a, b in spans]
    chunk = ceil_to(-(-cols.total // sub), TILE)
    for k in range(steps):
        u, v = divmod(k, sub)
        now, later = (even, odd) if u % 2 == 0 else (odd, even)
        start, stop = chunk * v, min(chunk * (v + 1), cols.total)
        if start < stop:
            rows = (second_ref, third_ref)[u][...].reshape(sub * seqs, width)
            later[:, start:stop] = turned_dot(rows, columns_of(w_ref, start, stop, 0, width))
        for (a, b), low in zip(spans, lows):
            prev_ref[k, :, a:b] = low
        low = jnp.concatenate(lows, 1)
        lows = [None] * len(spans)
        for j in cols.order:
            first, last = cols.gates(j)
            pre = now[v * seqs : (v + 1) * seqs, first:last] + dot(low, turned[:, first:last])
            if j < cols.full:
                gate_i, gate_f, gate_g, gate_o = (
                    pre[:, q * LANES : (q + 1) * LANES] for q in range(4)
                )
                gate_i, gate_f, gate_o = sigmoid(gate_i), sigmoid(gate_f), sigmoid(gate_o)
                gate_g = jnp.tanh(gate_g)
                for q, gate in enumerate((gate_i, gate_f, gate_g, gate_o)):
                    a, b = cols.gate(j, q)
                    act_ref[k, :, a:b] = gate
            else:
                act = rest_mul * jnp.tanh(rest_mul * pre) + rest_add
                act_ref[k, :, first:last] = act
                gate_i, gate_f, gate_g, gate_o = (
                    act[:, q * cols.rest : (q + 1) * cols.rest] for q in range(4)
                )
            a, b = spans[j]
            cells[j] = gate_f * cells[j] + gate_i * gate_g
            cell_ref[k, :, a:b] = cells[j]
            lows[j] = (gate_o * jnp.tanh(cells[j])).astype(BF16)
    for j, (a, b) in enumerate(spans):
        cell_s[:, a:b] = cells[j]
        low_s[:, a:b] = lows[j]

    @pl.when(pl.program_id(0) == pl.num_programs(0) - 1)
    def _():
        for copy in copies:
            copy.wait()


def backward_kernel(
    cols,
    own,
    at_ref,
    act_ref,
    cell_ref,
    before_ref,
    act_before_ref,
    cot_ref,
    mask_ref,
    ratio_ref,
    length_row_ref,
    rec_ref,
    *refs,
):
    grad_ref = refs[6 if own else 0]
    if own:
        drop_ref, prev_ref, drop_end_ref, prev_end_ref, group_ref, weight_mask_ref = refs[:6]
        keep_ref, send_ref = refs[7:9]
        own_s, sides, pick, sums = refs[9:13]
    dcell_s, recur_s, smooth_s, tanh_s, scale_s, coef_s, smooth_coef_s, length_s = refs[-8:]
    steps, seqs, _ = act_ref.shape
    hidden_n = cols.hidden
    place = pl.program_id(0)
    block = pl.num_programs(0) - 1 - place
    spans = [cols.units(j) for j in range(cols.full + 1)]

    @pl.when(place == 0)
    def _():
        dcell_s[...] = jnp.zeros_like(dcell_s)
        recur_s[...] = jnp.zeros_like(recur_s)
        smooth_s[...] = jnp.zeros_like(smooth_s)
        tanh_s[...] = jnp.tanh(cell_ref[steps - 1])
        ratio = column_of(ratio_ref[...])
        length_s[...] = column_of(length_row_ref[...])
        smooth_coef_s[...] = 2.0 * TAR_BETA * ratio
        scale_s[...] = mask_ref[...].astype(F32) * (1.0 / KEEP_OUTPUT)
        for a, b in spans:
            scale = scale_s[:, a:b]
            coef_s[:, a:b] = 2.0 * ACTIVATION_COEF * ratio[:, : b - a] * scale * scale
        if own:
            sums[...] = jnp.zeros_like(sums)
            sides[...] = jnp.zeros_like(sides)
            first = (group_ref[...] == 0.0).astype(F32).astype(BF16)
            for k in range(steps):
                pick[:, k * seqs : (k + 1) * seqs] = first

    inner = (block > 0).astype(F32)
    rec = jnp.concatenate([rec_ref[q, a:b, :hidden_n] for a, b in spans for q in range(4)], 0)
    jobs = []
    if own:
        width = drop_ref.shape[2]
        for kind, count in enumerate((width, hidden_n)):
            for start in range(0, count, TILE):
                jobs += [(kind, start, min(start + TILE, count), q) for q in range(2)]

    def weight_job(n, data):
        kind, start, stop, q = jobs[n]
        values = data[kind][...].reshape(steps * seqs, data[kind].shape[2])[:, start:stop]
        base = kind * width
        sums[q, :hidden_n, base + start : base + stop] += dot(sides[q], values)

    def gates_at(k, j):
        if j < cols.full:
            return [act_ref[k, :, a:b] for a, b in (cols.gate(j, q) for q in range(4))]
        first, last = cols.gates(j)
        packed = act_ref[k, :, first:last]
        return [packed[:, q * cols.rest : (q + 1) * cols.rest] for q in range(4)]

    for k in range(steps - 1, -1, -1):
        late = steps - 1 - k
        for n in range(late * len(jobs) // steps, (late + 1) * len(jobs) // steps):
            weight_job(n, (drop_ref, prev_ref))
        for j in cols.order:
            a, b = spans[j]
            gate_i, gate_f, gate_g, gate_o = gates_at(k, j)
            tanh_cell = tanh_s[:, a:b]
            hidden = gate_o * tanh_cell
            low, high = cols.gate(j, 3)
            if k > 0:
                cell_before = cell_ref[k - 1, :, a:b]
                out_before = act_ref[k - 1, :, low:high]
            else:
                cell_before = before_ref[0, :, a:b] * inner
                out_before = act_before_ref[0, :, low:high]
            tanh_before = jnp.tanh(cell_before)
            tanh_s[:, a:b] = tanh_before
            valid = length_s[:, : b - a] > (block * steps + k).astype(F32)
            smooth = smooth_coef_s[:, : b - a] * (hidden - out_before * tanh_before)
            if k == 0:
                smooth = smooth * inner
            smooth = jnp.where(valid, smooth, 0.0)
            direct = scale_s[:, a:b] * cot_ref[k, :, a:b].astype(F32) + coef_s[:, a:b] * hidden
            direct = jnp.where(valid, direct, 0.0) + smooth - smooth_s[:, a:b]
            smooth_s[:, a:b] = smooth
            dhidden = direct + recur_s[:, a:b]
            total = dcell_s[:, a:b] + dhidden * (gate_o * (1.0 - tanh_cell * tanh_cell))
            dcell_s[:, a:b] = total * gate_f
            grads = [
                (total * (gate_g * gate_i * (1.0 - gate_i))).astype(BF16),
                (total * (cell_before * gate_f * (1.0 - gate_f))).astype(BF16),
                (total * (gate_i * (1.0 - gate_g * gate_g))).astype(BF16),
                (dhidden * (tanh_cell * gate_o * (1.0 - gate_o))).astype(BF16),
            ]
            first, last = cols.gates(j)
            grad_ref[k, :, first:last] = jnp.concatenate(grads, 1)
            if own:
                mine = grads[3]
                for q in range(3):
                    mine = jnp.where(at_ref[0] == q, grads[q], mine)
                own_s[k * seqs : (k + 1) * seqs, a:b] = mine
        recur_s[...] = dot(grad_ref[k], rec)
    if own:
        turned = own_s[...].T
        first = turned * pick[...]
        sides[0] = first
        sides[1] = turned - first

        @pl.when(block == 0)
        def _():
            for n in range(len(jobs)):
                weight_job(n, (drop_end_ref, prev_end_ref))
            scale = weight_mask_ref[...].astype(F32) * (1.0 / KEEP_WEIGHT)
            for q in range(2):
                sums[q, :hidden_n, width:] = sums[q, :hidden_n, width:] * scale
            hand_out(at_ref[2], sums, keep_ref, send_ref)


def hand_out(grp_at, sums, keep_ref, send_ref):
    rows = keep_ref.shape[1]
    for part in range(keep_ref.shape[0]):
        span = slice(part * rows, (part + 1) * rows)
        keep_ref[part] = sums[grp_at, span]
        send_ref[part] = sums[1 - grp_at, span].astype(BF16)


def weight_kernel(grp_ref, rows_ref, group_ref, drop_ref, prev_ref, mask_ref, keep_ref, send_ref, sums, pick):
    steps, seqs, own = rows_ref.shape
    place = pl.program_id(0)

    @pl.when(place == 0)
    def _():
        sums[...] = jnp.zeros_like(sums)
        one = (column_of(group_ref[...]) == 0.0).astype(F32).astype(BF16)
        for at in range(0, own, LANES):
            width = min(LANES, own - at)
            pick[:, at : at + width] = one[:, :width]

    grads = rows_ref[...]
    first = (grads * pick[...][None]).reshape(steps * seqs, own)
    second = grads.reshape(steps * seqs, own) - first
    start = 0
    for ref in (drop_ref, prev_ref):
        width = ref.shape[2]
        values = ref[...].reshape(steps * seqs, width)
        for at, part in enumerate((first, second)):
            sums[at, :own, start : start + width] += lax.dot_general(
                part, values, OVER_ROWS, preferred_element_type=F32
            )
        start += width

    @pl.when(place == pl.num_programs(0) - 1)
    def _():
        scale = mask_ref[...].astype(F32) * (1.0 / KEEP_WEIGHT)
        for at in range(2):
            part = (at, slice(0, own), slice(start - width, start))
            sums[part] = sums[part] * scale
        hand_out(grp_ref[0], sums, keep_ref, send_ref)


def params(megabytes):
    return pltpu.CompilerParams(
        dimension_semantics=("arbitrary",), vmem_limit_bytes=megabytes << 20
    )


def fixed(*shape):
    return pl.BlockSpec(shape, lambda *_: (0,) * len(shape), pipeline_mode=pl.Buffered(1))


def column_of(row):
    return jnp.broadcast_to(row, (LANES, row.shape[1])).T


def gather_pieces(plan, mine, counts, beside):
    hold = lax.optimization_barrier
    cut = plan.cut
    one, two, beside, counts = hold(
        (flip(mine, "row", 1), flip(mine, "row", 2), beside, counts + flip(counts, "grp", 1))
    )
    near = jnp.stack([one, two])
    near_x, near_y, three, counts = hold(
        (
            flip(near[:, : plan.first], "seq", 1),
            flip(near[:, plan.first :], "seq", 2),
            flip(two, "row", 1),
            counts + flip(counts, "seq", 1),
        )
    )
    early = jnp.concatenate([part.reshape(-1, cut) for part in (near, near_x, near_y, three)], 0)
    last_x, last_y, early_other, counts = hold(
        (
            flip(three[: plan.first], "seq", 1),
            flip(three[plan.first :], "seq", 2),
            flip(early, "grp", 1),
            counts + flip(counts, "seq", 2),
        )
    )
    late = jnp.concatenate([last_x, last_y], 0)
    return early, late, early_other, flip(late, "grp", 1), counts, beside


def local(
    tokens,
    in_mask,
    out_mask,
    lengths,
    groups,
    input_gate_weight,
    w_recur,
    weight_mask,
    bias,
    cotangent,
):
    seq_count, time_steps, width_in = tokens.shape
    hidden = cotangent.shape[2]
    row_count = input_gate_weight.shape[0]
    row_at = lax.axis_index("row")
    grp_at = lax.axis_index("grp")
    seq_at = lax.axis_index("seq")
    rows_n, seq_n = lax.axis_size("row"), lax.axis_size("seq")
    cols = Columns(hidden)
    wide = ceil_to(width_in + 2, LANES)
    share = seq_count // rows_n
    own = row_count == hidden
    pieced = own and rows_n == 4 and seq_n == 4 and lax.axis_size("grp") == 2

    plan = Plan(hidden, wide)
    at = jnp.stack([row_at, seq_at, grp_at]).astype(jnp.int32)
    own_weights, *mine = pl.pallas_call(
        functools.partial(shard_kernel, plan),
        grid_spec=pltpu.PrefetchScalarGridSpec(
            num_scalar_prefetch=1,
            grid=(1,),
            in_specs=[
                fixed(row_count, width_in),
                fixed(row_count, hidden),
                fixed(row_count, hidden),
                fixed(1, row_count),
            ],
            out_specs=[fixed(row_count, plan.columns)] + [fixed(plan.rows, plan.cut)] * pieced,
        ),
        out_shape=[jax.ShapeDtypeStruct((row_count, plan.columns), BF16)]
        + [jax.ShapeDtypeStruct((plan.rows, plan.cut), BF16)] * pieced,
        compiler_params=params(58),
        name="shard",
    )(at, input_gate_weight, w_recur, weight_mask, bias[None])
    sub = max(s for s in range(1, 8) if time_steps % (2 * s) == 0)
    steps = 2 * sub
    blocks = time_steps // steps

    def at_time(width):
        return pl.BlockSpec((steps, seq_count, width), lambda b, *_: (b, 0, 0))

    dropped = pl.pallas_call(
        functools.partial(drop_kernel, width_in),
        grid=(blocks,),
        in_specs=[at_time(width_in), fixed(seq_count, width_in)],
        out_specs=at_time(wide),
        out_shape=jax.ShapeDtypeStruct((time_steps, seq_count, wide), BF16),
        compiler_params=params(58),
        name="drop",
    )(jnp.swapaxes(tokens, 0, 1), in_mask)
    cot_time = jnp.swapaxes(cotangent, 0, 1)

    group_hot = (groups[:, None] == jnp.arange(2)[None, :]).astype(F32)
    valid_count = jnp.clip(lengths, 0, time_steps).astype(F32)
    counts = jnp.sum(group_hot * valid_count[:, None], 0)
    if pieced:
        *pieces, counts, dropped = gather_pieces(plan, mine[0], counts, dropped)
        sources = [own_weights] + pieces
    else:
        counts = lax.psum(counts, ("grp", "seq"))
        whole = lax.all_gather(own_weights, "row", axis=0, tiled=True)
        sources = [whole.reshape(4, hidden, plan.columns)]
    group_ratio = jnp.sum(counts) / counts
    seq_ratio = jnp.sum(group_hot * group_ratio[None, :], 1)

    acts, cells, prev_low, weights, w_rec = pl.pallas_call(
        functools.partial(forward_kernel, cols, plan, sub, pieced),
        grid_spec=pltpu.PrefetchScalarGridSpec(
            num_scalar_prefetch=1,
            grid=(blocks,),
            in_specs=[
                fixed(sub, seq_count, wide),
                pl.BlockSpec((sub, seq_count, wide), lambda b, *_: (2 * b + 1, 0, 0)),
                pl.BlockSpec(
                    (sub, seq_count, wide),
                    lambda b, *_: (jnp.minimum(2 * b + 2, 2 * blocks - 1), 0, 0),
                ),
            ]
            + [fixed(*source.shape) for source in sources],
            out_specs=[
                at_time(cols.total),
                at_time(hidden),
                at_time(hidden),
                pl.BlockSpec(memory_space=pl.ANY),
                pl.BlockSpec(memory_space=pl.ANY),
            ],
            scratch_shapes=[
                pltpu.VMEM((4, hidden, plan.columns), BF16),
                pltpu.VMEM((hidden, cols.total), BF16),
                pltpu.VMEM((sub * seq_count, cols.total), F32),
                pltpu.VMEM((sub * seq_count, cols.total), F32),
                pltpu.VMEM((seq_count, hidden), F32),
                pltpu.VMEM((seq_count, hidden), BF16),
                pltpu.SemaphoreType.DMA((2,)),
            ],
        ),
        out_shape=[
            jax.ShapeDtypeStruct((time_steps, seq_count, cols.total), F32),
            jax.ShapeDtypeStruct((time_steps, seq_count, hidden), F32),
            jax.ShapeDtypeStruct((time_steps, seq_count, hidden), BF16),
            jax.ShapeDtypeStruct((4, hidden, wide), BF16),
            jax.ShapeDtypeStruct((4, hidden, plan.columns - wide), BF16),
        ],
        compiler_params=params(58),
        name="forward",
    )(at, dropped, dropped, dropped, *sources)

    back_steps = sub
    back_blocks = time_steps // back_steps

    def back(b):
        return back_blocks - 1 - b

    def before(width):
        return pl.BlockSpec(
            (1, seq_count, width), lambda b, *_: (jnp.maximum(back(b) * back_steps - 1, 0), 0, 0)
        )

    def back_time(width):
        return pl.BlockSpec((back_steps, seq_count, width), lambda b, *_: (back(b), 0, 0))

    def later_time(width):
        return pl.BlockSpec(
            (back_steps, seq_count, width),
            lambda b, *_: (jnp.minimum(back(b) + 1, back_blocks - 1), 0, 0),
        )

    part_rows = ceil_to(-(-row_count // seq_n), 8)
    columns = wide + hidden
    group_row = groups.astype(F32)[None]
    sum_specs = [fixed(seq_n, part_rows, columns)] * 2
    sum_shapes = [
        jax.ShapeDtypeStruct((seq_n, part_rows, columns), F32),
        jax.ShapeDtypeStruct((seq_n, part_rows, columns), BF16),
    ]
    sum_scratch = pltpu.VMEM((2, seq_n * part_rows, columns), F32)
    per_unit = pltpu.VMEM((seq_count, hidden), F32)
    own_specs, own_arrays, own_scratch = [], [], []
    if own:
        own_specs = [
            later_time(wide),
            later_time(hidden),
            fixed(back_steps, seq_count, wide),
            fixed(back_steps, seq_count, hidden),
            fixed(1, seq_count),
            fixed(row_count, hidden),
        ]
        own_arrays = [dropped, prev_low, dropped, prev_low, group_row, weight_mask]
        own_scratch = [
            pltpu.VMEM((back_steps * seq_count, hidden), BF16),
            pltpu.VMEM((2, hidden, back_steps * seq_count), BF16),
            pltpu.VMEM((1, back_steps * seq_count), BF16),
            sum_scratch,
        ]
    grads, *sums = pl.pallas_call(
        functools.partial(backward_kernel, cols, own),
        grid_spec=pltpu.PrefetchScalarGridSpec(
            num_scalar_prefetch=1,
            grid=(back_blocks,),
            in_specs=[
                back_time(cols.total),
                back_time(hidden),
                before(hidden),
                before(cols.total),
                back_time(hidden),
                fixed(seq_count, hidden),
                fixed(1, seq_count),
                fixed(1, seq_count),
                fixed(4, hidden, plan.columns - wide),
            ]
            + own_specs,
            out_specs=[back_time(cols.total)] + sum_specs * own,
            scratch_shapes=own_scratch
            + [per_unit] * 6
            + [pltpu.VMEM((seq_count, LANES), F32)] * 2,
        ),
        out_shape=[jax.ShapeDtypeStruct((time_steps, seq_count, cols.total), BF16)]
        + sum_shapes * own,
        compiler_params=params(58),
        name="backward",
    )(
        at,
        acts,
        cells,
        cells,
        acts,
        cot_time,
        out_mask,
        seq_ratio[None],
        lengths.astype(F32)[None],
        w_rec,
        *own_arrays,
    )

    if not own:
        own_rows = lax.dynamic_slice_in_dim(
            cols.unpack_lanes(grads), row_at * row_count, row_count, 2
        )
        sums = pl.pallas_call(
            weight_kernel,
            grid_spec=pltpu.PrefetchScalarGridSpec(
                num_scalar_prefetch=1,
                grid=(blocks,),
                in_specs=[
                    at_time(row_count),
                    fixed(1, seq_count),
                    at_time(wide),
                    at_time(hidden),
                    fixed(row_count, hidden),
                ],
                out_specs=sum_specs,
                scratch_shapes=[sum_scratch, pltpu.VMEM((seq_count, row_count), BF16)],
            ),
            out_shape=sum_shapes,
            compiler_params=params(58),
            name="weights",
        )(grp_at[None], own_rows, group_row, dropped, prev_low, weight_mask)
    keep, send = sums

    hold = lax.optimization_barrier
    block = (keep + flip(send, "grp", 1).astype(F32)).astype(BF16)
    swapped = lax.all_to_all(block, "seq", 0, 0, tiled=True)

    own_seqs = lax.dynamic_slice_in_dim(grads, row_at * share, share, 1)
    own_scale = lax.dynamic_slice_in_dim(in_mask, row_at * share, share, 0).astype(F32) / KEEP_INPUT
    w_in = cols.pack(weights[:, :, :width_in])
    input_time = jnp.einsum("tsr,rk->tsk", own_seqs, w_in, preferred_element_type=F32)
    input_grad = jnp.swapaxes(input_time * own_scale[None], 0, 1)
    swapped, input_grad = hold((swapped, input_grad))

    total = jnp.sum(swapped.astype(F32), 0).astype(BF16)
    copies = jnp.broadcast_to(total[None], (seq_n,) + total.shape)
    parts = lax.all_to_all(copies, "seq", 0, 0, tiled=True)
    peer = flip(total, "grp", 1)
    ours, theirs = (
        jnp.concatenate([part[:, : width_in + 1], part[:, wide:]], 1).astype(F32)
        for part in (total, peer)
    )
    first = jnp.where(grp_at == 0, ours, theirs)
    second = jnp.where(grp_at == 0, theirs, ours)
    dots = [jnp.sum(a * b) for a, b in ((first, first), (first, second), (second, second))]
    gram = jnp.stack([dots[0], dots[1], dots[1], dots[2]]).reshape(2, 2)
    gram = exchange_sum(exchange_sum(gram, "row"), "seq")
    parts, gram = hold((parts, gram))
    everyone = parts.reshape(seq_n * part_rows, wide + hidden)[:row_count].astype(F32)
    return (
        input_grad,
        everyone[None, :, :width_in],
        everyone[None, :, wide:],
        everyone[None, :, width_in],
        gram,
    )


def solution(mesh):
    return jax.shard_map(
        local,
        mesh=mesh,
        in_specs=(
            P(("grp", "seq"), None, None),
            P(("grp", "seq"), None),
            P(("grp", "seq"), None),
            P(("grp", "seq")),
            P(("grp", "seq")),
            P("row", None),
            P("row", None),
            P("row", None),
            P("row"),
            P(("grp", "seq"), None, None),
        ),
        out_specs=(
            P(("grp", "seq", "row"), None, None),
            P("grp", "row", None),
            P("grp", "row", None),
            P("grp", "row"),
            P(),
        ),
        check_vma=False,
    )
```

```python
import functools

import jax
import jax.numpy as jnp
from jax import lax
from jax.experimental import pallas as pl
from jax.experimental.pallas import tpu as pltpu
from jax.sharding import PartitionSpec as P

ACTIVATION_COEF = 2.0
TAR_BETA = 1.0
KEEP_INPUT = 0.75
KEEP_OUTPUT = 0.6
KEEP_WEIGHT = 0.5
LANES = 128
TILE = 256
BF16 = jnp.bfloat16
F32 = jnp.float32
OVER_ROWS = (((0,), (0,)), ((), ()))


def ceil_to(value, step):
    return -(-value // step) * step


def dot(left, right):
    return jnp.dot(left, right, preferred_element_type=F32)


def flip(block, axis, bit):
    count = lax.axis_size(axis)
    return lax.ppermute(block, axis, [(at, at ^ bit) for at in range(count)])


def exchange_sum(block, axis):
    count = lax.axis_size(axis)
    if count not in (2, 4):
        return lax.psum(block, axis)
    parts = [block] + [flip(block, axis, bit) for bit in range(1, count)]
    while len(parts) > 1:
        parts = [parts[at] + parts[at + 1] for at in range(0, len(parts), 2)]
    return parts[0]


def sigmoid(value):
    return 0.5 * jnp.tanh(0.5 * value) + 0.5


class Columns:
    def __init__(self, hidden):
        self.hidden = hidden
        self.full = hidden // LANES
        self.rest = hidden - self.full * LANES
        assert 0 < 4 * self.rest <= LANES
        self.total = 4 * hidden
        self.order = (self.full,) + tuple(range(self.full))

    def units(self, j):
        return j * LANES, min((j + 1) * LANES, self.hidden)

    def gates(self, j):
        return 4 * j * LANES, min(4 * (j + 1) * LANES, self.total)

    def gate(self, j, q):
        width = LANES if j < self.full else self.rest
        start = 4 * j * LANES + q * width
        return start, start + width

    def pack(self, gated):
        parts = []
        for j in range(self.full + 1):
            first, last = self.units(j)
            parts.append(gated[:, first:last].reshape((-1,) + gated.shape[2:]))
        return jnp.concatenate(parts, 0)

    def unpack_lanes(self, packed):
        parts = []
        for q in range(4):
            for j in range(self.full + 1):
                first, last = self.gate(j, q)
                parts.append(packed[..., first:last])
        return jnp.concatenate(parts, -1)


def drop_kernel(width, tok_ref, mask_ref, drop_ref):
    scale = mask_ref[...].astype(F32) * (1.0 / KEEP_INPUT)
    for k in range(tok_ref.shape[0]):
        drop_ref[k, :, :width] = (tok_ref[k].astype(F32) * scale).astype(BF16)
        drop_ref[k, :, width:] = jnp.ones_like(drop_ref[k, :, width:])


def turned_dot(left, right):
    return lax.dot_general(left, right, (((1,), (1,)), ((), ())), preferred_element_type=F32)


def identity(size):
    line = lax.broadcasted_iota(jnp.int32, (size, size), 0)
    same = line == lax.broadcasted_iota(jnp.int32, (size, size), 1)
    return same.astype(F32).astype(BF16)


def shard_kernel(plan, at_ref, in_ref, rec_ref, mask_ref, bias_ref, own_ref, *mine_ref):
    rows, width = in_ref.shape
    hidden = rec_ref.shape[1]
    bias = bias_ref[...]
    high = bias.astype(BF16)
    pair = jnp.concatenate([high, (bias - high.astype(F32)).astype(BF16)], 0)
    scale = mask_ref[...].astype(F32) / KEEP_WEIGHT
    own_ref[:, :width] = in_ref[...]
    own_ref[:, width : width + 2] = turned_dot(identity(rows), pair).astype(BF16)
    own_ref[:, plan.wide : plan.wide + hidden] = (rec_ref[...].astype(F32) * scale).astype(BF16)
    own_ref[:, plan.wide + hidden :] = jnp.zeros_like(own_ref[:, plan.wide + hidden :])
    for ref in mine_ref:
        ref[...] = own_ref[plan.window(at_ref[1], at_ref[2], 0, plan.rows)]


class Plan:
    def __init__(self, hidden, wide):
        self.wide = wide
        self.columns = ceil_to(wide + hidden, LANES)
        self.row_step = hidden // 32 * 16
        self.rows = hidden - self.row_step
        self.first = ceil_to(self.rows // 2, 16)
        self.column_step = self.columns // LANES // 2 * LANES
        self.cut = self.columns - self.column_step

    def window(self, seq_at, grp_at, start, count):
        half = (seq_at ^ (seq_at >> 1)) & 1
        return (
            pl.ds(pl.multiple_of(half * self.row_step + start, 16), count),
            pl.ds(pl.multiple_of(grp_at * self.column_step, LANES), self.cut),
        )

    def places(self):
        first, rest = self.first, self.rows - self.first
        return [
            (0, 1, 0, 0, self.rows),
            (0, 2, 0, 0, self.rows),
            (0, 1, 1, 0, first),
            (0, 2, 1, 0, first),
            (0, 1, 1, first, rest),
            (0, 2, 1, first, rest),
            (0, 3, 0, 0, self.rows),
            (1, 3, 1, 0, first),
            (1, 3, 1, first, rest),
        ]


def forward_kernel(cols, plan, sub, pieced, at_ref, first_ref, second_ref, third_ref, *refs):
    count = 5 if pieced else 1
    sources = refs[:count]
    act_ref, cell_ref, prev_ref, w_out, rec_out, w_ref, turned, even, odd, cell_s, low_s, sems = refs[
        count:
    ]
    seqs, width = first_ref.shape[1:]
    steps = act_ref.shape[0]
    hidden = cols.hidden

    def columns_of(rows_ref, start, stop, first, last):
        parts = []
        for j in range(cols.full + 1):
            unit, _ = cols.units(j)
            for q in range(4):
                low, high = cols.gate(j, q)
                if low >= start and high <= stop:
                    parts.append(rows_ref[q, unit : unit + high - low, first:last])
        return jnp.concatenate(parts, 0)

    copies = [
        pltpu.make_async_copy(w_ref.at[:, :, :width], w_out, sems.at[0]),
        pltpu.make_async_copy(w_ref.at[:, :, width:], rec_out, sems.at[1]),
    ]

    @pl.when(pl.program_id(0) == 0)
    def _():
        if pieced:
            row_at, seq_at, grp_at = at_ref[0], at_ref[1], at_ref[2]
            w_ref[row_at] = sources[0][...]
            for gi in range(2):
                line = [0, 0]
                for array, k, m, start, size in plan.places():
                    window = plan.window(seq_at ^ m, grp_at ^ gi, start, size)
                    piece = sources[1 + 2 * gi + array][line[array] : line[array] + size]
                    w_ref[(row_at ^ k,) + window] = piece
                    line[array] += size
        else:
            w_ref[...] = sources[0][...]
        for copy in copies:
            copy.start()
        turned[...] = turned_dot(
            identity(hidden), columns_of(w_ref, 0, cols.total, width, width + hidden)
        ).astype(BF16)
        cell_s[...] = jnp.zeros_like(cell_s)
        low_s[...] = jnp.zeros_like(low_s)
        even[...] = turned_dot(
            first_ref[...].reshape(sub * seqs, width), columns_of(w_ref, 0, cols.total, 0, width)
        )

    lane = lax.broadcasted_iota(jnp.int32, (1, 4 * cols.rest), 1)
    tanh_lane = (lane >= 2 * cols.rest) & (lane < 3 * cols.rest)
    rest_mul = jnp.where(tanh_lane, 1.0, 0.5)
    rest_add = jnp.where(tanh_lane, 0.0, 0.5)
    spans = [cols.units(j) for j in range(cols.full + 1)]
    cells = [cell_s[:, a:b] for a, b in spans]
    lows = [low_s[:, a:b] for a, b in spans]
    chunk = ceil_to(-(-cols.total // sub), TILE)
    for k in range(steps):
        u, v = divmod(k, sub)
        now, later = (even, odd) if u % 2 == 0 else (odd, even)
        start, stop = chunk * v, min(chunk * (v + 1), cols.total)
        if start < stop:
            rows = (second_ref, third_ref)[u][...].reshape(sub * seqs, width)
            later[:, start:stop] = turned_dot(rows, columns_of(w_ref, start, stop, 0, width))
        for (a, b), low in zip(spans, lows):
            prev_ref[k, :, a:b] = low
        low = jnp.concatenate(lows, 1)
        lows = [None] * len(spans)
        for j in cols.order:
            first, last = cols.gates(j)
            pre = now[v * seqs : (v + 1) * seqs, first:last] + dot(low, turned[:, first:last])
            if j < cols.full:
                gate_i, gate_f, gate_g, gate_o = (
                    pre[:, q * LANES : (q + 1) * LANES] for q in range(4)
                )
                gate_i, gate_f, gate_o = sigmoid(gate_i), sigmoid(gate_f), sigmoid(gate_o)
                gate_g = jnp.tanh(gate_g)
                for q, gate in enumerate((gate_i, gate_f, gate_g, gate_o)):
                    a, b = cols.gate(j, q)
                    act_ref[k, :, a:b] = gate
            else:
                act = rest_mul * jnp.tanh(rest_mul * pre) + rest_add
                act_ref[k, :, first:last] = act
                gate_i, gate_f, gate_g, gate_o = (
                    act[:, q * cols.rest : (q + 1) * cols.rest] for q in range(4)
                )
            a, b = spans[j]
            cells[j] = gate_f * cells[j] + gate_i * gate_g
            cell_ref[k, :, a:b] = cells[j]
            lows[j] = (gate_o * jnp.tanh(cells[j])).astype(BF16)
    for j, (a, b) in enumerate(spans):
        cell_s[:, a:b] = cells[j]
        low_s[:, a:b] = lows[j]

    @pl.when(pl.program_id(0) == pl.num_programs(0) - 1)
    def _():
        for copy in copies:
            copy.wait()


def backward_kernel(
    cols,
    own,
    at_ref,
    act_ref,
    cell_ref,
    before_ref,
    act_before_ref,
    cot_ref,
    mask_ref,
    ratio_ref,
    length_row_ref,
    rec_ref,
    *refs,
):
    grad_ref = refs[6 if own else 0]
    if own:
        drop_ref, prev_ref, drop_end_ref, prev_end_ref, group_ref, weight_mask_ref = refs[:6]
        keep_ref, send_ref = refs[7:9]
        own_s, sides, pick, sums = refs[9:13]
    dcell_s, recur_s, smooth_s, tanh_s, scale_s, coef_s, smooth_coef_s, length_s = refs[-8:]
    steps, seqs, _ = act_ref.shape
    hidden_n = cols.hidden
    place = pl.program_id(0)
    block = pl.num_programs(0) - 1 - place
    spans = [cols.units(j) for j in range(cols.full + 1)]

    @pl.when(place == 0)
    def _():
        dcell_s[...] = jnp.zeros_like(dcell_s)
        recur_s[...] = jnp.zeros_like(recur_s)
        smooth_s[...] = jnp.zeros_like(smooth_s)
        tanh_s[...] = jnp.tanh(cell_ref[steps - 1])
        ratio = column_of(ratio_ref[...])
        length_s[...] = column_of(length_row_ref[...])
        smooth_coef_s[...] = 2.0 * TAR_BETA * ratio
        scale_s[...] = mask_ref[...].astype(F32) * (1.0 / KEEP_OUTPUT)
        for a, b in spans:
            scale = scale_s[:, a:b]
            coef_s[:, a:b] = 2.0 * ACTIVATION_COEF * ratio[:, : b - a] * scale * scale
        if own:
            sums[...] = jnp.zeros_like(sums)
            sides[...] = jnp.zeros_like(sides)
            first = (group_ref[...] == 0.0).astype(F32).astype(BF16)
            for k in range(steps):
                pick[:, k * seqs : (k + 1) * seqs] = first

    inner = (block > 0).astype(F32)
    rec = jnp.concatenate([rec_ref[q, a:b, :hidden_n] for a, b in spans for q in range(4)], 0)
    jobs = []
    if own:
        width = drop_ref.shape[2]
        for kind, count in enumerate((width, hidden_n)):
            for start in range(0, count, TILE):
                jobs += [(kind, start, min(start + TILE, count), q) for q in range(2)]

    def weight_job(n, data):
        kind, start, stop, q = jobs[n]
        values = data[kind][...].reshape(steps * seqs, data[kind].shape[2])[:, start:stop]
        base = kind * width
        sums[q, :hidden_n, base + start : base + stop] += dot(sides[q], values)

    def gates_at(k, j):
        if j < cols.full:
            return [act_ref[k, :, a:b] for a, b in (cols.gate(j, q) for q in range(4))]
        first, last = cols.gates(j)
        packed = act_ref[k, :, first:last]
        return [packed[:, q * cols.rest : (q + 1) * cols.rest] for q in range(4)]

    for k in range(steps - 1, -1, -1):
        late = steps - 1 - k
        for n in range(late * len(jobs) // steps, (late + 1) * len(jobs) // steps):
            weight_job(n, (drop_ref, prev_ref))
        for j in cols.order:
            a, b = spans[j]
            gate_i, gate_f, gate_g, gate_o = gates_at(k, j)
            tanh_cell = tanh_s[:, a:b]
            hidden = gate_o * tanh_cell
            low, high = cols.gate(j, 3)
            if k > 0:
                cell_before = cell_ref[k - 1, :, a:b]
                out_before = act_ref[k - 1, :, low:high]
            else:
                cell_before = before_ref[0, :, a:b] * inner
                out_before = act_before_ref[0, :, low:high]
            tanh_before = jnp.tanh(cell_before)
            tanh_s[:, a:b] = tanh_before
            valid = length_s[:, : b - a] > (block * steps + k).astype(F32)
            smooth = smooth_coef_s[:, : b - a] * (hidden - out_before * tanh_before)
            if k == 0:
                smooth = smooth * inner
            smooth = jnp.where(valid, smooth, 0.0)
            direct = scale_s[:, a:b] * cot_ref[k, :, a:b].astype(F32) + coef_s[:, a:b] * hidden
            direct = jnp.where(valid, direct, 0.0) + smooth - smooth_s[:, a:b]
            smooth_s[:, a:b] = smooth
            dhidden = direct + recur_s[:, a:b]
            total = dcell_s[:, a:b] + dhidden * (gate_o * (1.0 - tanh_cell * tanh_cell))
            dcell_s[:, a:b] = total * gate_f
            grads = [
                (total * (gate_g * gate_i * (1.0 - gate_i))).astype(BF16),
                (total * (cell_before * gate_f * (1.0 - gate_f))).astype(BF16),
                (total * (gate_i * (1.0 - gate_g * gate_g))).astype(BF16),
                (dhidden * (tanh_cell * gate_o * (1.0 - gate_o))).astype(BF16),
            ]
            first, last = cols.gates(j)
            grad_ref[k, :, first:last] = jnp.concatenate(grads, 1)
            if own:
                mine = grads[3]
                for q in range(3):
                    mine = jnp.where(at_ref[0] == q, grads[q], mine)
                own_s[k * seqs : (k + 1) * seqs, a:b] = mine
        recur_s[...] = dot(grad_ref[k], rec)
    if own:
        turned = own_s[...].T
        first = turned * pick[...]
        sides[0] = first
        sides[1] = turned - first

        @pl.when(block == 0)
        def _():
            for n in range(len(jobs)):
                weight_job(n, (drop_end_ref, prev_end_ref))
            scale = weight_mask_ref[...].astype(F32) * (1.0 / KEEP_WEIGHT)
            for q in range(2):
                sums[q, :hidden_n, width:] = sums[q, :hidden_n, width:] * scale
            hand_out(at_ref[2], sums, keep_ref, send_ref)


def hand_out(grp_at, sums, keep_ref, send_ref):
    rows = keep_ref.shape[1]
    for part in range(keep_ref.shape[0]):
        span = slice(part * rows, (part + 1) * rows)
        keep_ref[part] = sums[grp_at, span]
        send_ref[part] = sums[1 - grp_at, span].astype(BF16)


def weight_kernel(grp_ref, rows_ref, group_ref, drop_ref, prev_ref, mask_ref, keep_ref, send_ref, sums, pick):
    steps, seqs, own = rows_ref.shape
    place = pl.program_id(0)

    @pl.when(place == 0)
    def _():
        sums[...] = jnp.zeros_like(sums)
        one = (column_of(group_ref[...]) == 0.0).astype(F32).astype(BF16)
        for at in range(0, own, LANES):
            width = min(LANES, own - at)
            pick[:, at : at + width] = one[:, :width]

    grads = rows_ref[...]
    first = (grads * pick[...][None]).reshape(steps * seqs, own)
    second = grads.reshape(steps * seqs, own) - first
    start = 0
    for ref in (drop_ref, prev_ref):
        width = ref.shape[2]
        values = ref[...].reshape(steps * seqs, width)
        for at, part in enumerate((first, second)):
            sums[at, :own, start : start + width] += lax.dot_general(
                part, values, OVER_ROWS, preferred_element_type=F32
            )
        start += width

    @pl.when(place == pl.num_programs(0) - 1)
    def _():
        scale = mask_ref[...].astype(F32) * (1.0 / KEEP_WEIGHT)
        for at in range(2):
            part = (at, slice(0, own), slice(start - width, start))
            sums[part] = sums[part] * scale
        hand_out(grp_ref[0], sums, keep_ref, send_ref)


def params(megabytes):
    return pltpu.CompilerParams(
        dimension_semantics=("arbitrary",), vmem_limit_bytes=megabytes << 20
    )


def fixed(*shape):
    return pl.BlockSpec(shape, lambda *_: (0,) * len(shape), pipeline_mode=pl.Buffered(1))


def column_of(row):
    return jnp.broadcast_to(row, (LANES, row.shape[1])).T


def gather_pieces(plan, mine, counts, beside):
    hold = lax.optimization_barrier
    cut = plan.cut
    one, two, beside, counts = hold(
        (flip(mine, "row", 1), flip(mine, "row", 2), beside, counts + flip(counts, "grp", 1))
    )
    near = jnp.stack([one, two])
    near_x, near_y, three, counts = hold(
        (
            flip(near[:, : plan.first], "seq", 1),
            flip(near[:, plan.first :], "seq", 2),
            flip(two, "row", 1),
            counts + flip(counts, "seq", 1),
        )
    )
    early = jnp.concatenate([part.reshape(-1, cut) for part in (near, near_x, near_y, three)], 0)
    last_x, last_y, early_other, counts = hold(
        (
            flip(three[: plan.first], "seq", 1),
            flip(three[plan.first :], "seq", 2),
            flip(early, "grp", 1),
            counts + flip(counts, "seq", 2),
        )
    )
    late = jnp.concatenate([last_x, last_y], 0)
    return early, late, early_other, flip(late, "grp", 1), counts, beside


def local(
    tokens,
    in_mask,
    out_mask,
    lengths,
    groups,
    input_gate_weight,
    w_recur,
    weight_mask,
    bias,
    cotangent,
):
    seq_count, time_steps, width_in = tokens.shape
    hidden = cotangent.shape[2]
    row_count = input_gate_weight.shape[0]
    row_at = lax.axis_index("row")
    grp_at = lax.axis_index("grp")
    seq_at = lax.axis_index("seq")
    rows_n, seq_n = lax.axis_size("row"), lax.axis_size("seq")
    cols = Columns(hidden)
    wide = ceil_to(width_in + 2, LANES)
    share = seq_count // rows_n
    own = row_count == hidden
    pieced = own and rows_n == 4 and seq_n == 4 and lax.axis_size("grp") == 2

    plan = Plan(hidden, wide)
    at = jnp.stack([row_at, seq_at, grp_at]).astype(jnp.int32)
    own_weights, *mine = pl.pallas_call(
        functools.partial(shard_kernel, plan),
        grid_spec=pltpu.PrefetchScalarGridSpec(
            num_scalar_prefetch=1,
            grid=(1,),
            in_specs=[
                fixed(row_count, width_in),
                fixed(row_count, hidden),
                fixed(row_count, hidden),
                fixed(1, row_count),
            ],
            out_specs=[fixed(row_count, plan.columns)] + [fixed(plan.rows, plan.cut)] * pieced,
        ),
        out_shape=[jax.ShapeDtypeStruct((row_count, plan.columns), BF16)]
        + [jax.ShapeDtypeStruct((plan.rows, plan.cut), BF16)] * pieced,
        compiler_params=params(58),
        name="shard",
    )(at, input_gate_weight, w_recur, weight_mask, bias[None])
    sub = max(s for s in range(1, 8) if time_steps % (2 * s) == 0)
    steps = 2 * sub
    blocks = time_steps // steps

    def at_time(width):
        return pl.BlockSpec((steps, seq_count, width), lambda b, *_: (b, 0, 0))

    dropped = pl.pallas_call(
        functools.partial(drop_kernel, width_in),
        grid=(blocks,),
        in_specs=[at_time(width_in), fixed(seq_count, width_in)],
        out_specs=at_time(wide),
        out_shape=jax.ShapeDtypeStruct((time_steps, seq_count, wide), BF16),
        compiler_params=params(58),
        name="drop",
    )(jnp.swapaxes(tokens, 0, 1), in_mask)
    cot_time = jnp.swapaxes(cotangent, 0, 1)

    group_hot = (groups[:, None] == jnp.arange(2)[None, :]).astype(F32)
    valid_count = jnp.clip(lengths, 0, time_steps).astype(F32)
    counts = jnp.sum(group_hot * valid_count[:, None], 0)
    if pieced:
        *pieces, counts, dropped = gather_pieces(plan, mine[0], counts, dropped)
        sources = [own_weights] + pieces
    else:
        counts = lax.psum(counts, ("grp", "seq"))
        whole = lax.all_gather(own_weights, "row", axis=0, tiled=True)
        sources = [whole.reshape(4, hidden, plan.columns)]
    group_ratio = jnp.sum(counts) / counts
    seq_ratio = jnp.sum(group_hot * group_ratio[None, :], 1)

    acts, cells, prev_low, weights, w_rec = pl.pallas_call(
        functools.partial(forward_kernel, cols, plan, sub, pieced),
        grid_spec=pltpu.PrefetchScalarGridSpec(
            num_scalar_prefetch=1,
            grid=(blocks,),
            in_specs=[
                fixed(sub, seq_count, wide),
                pl.BlockSpec((sub, seq_count, wide), lambda b, *_: (2 * b + 1, 0, 0)),
                pl.BlockSpec(
                    (sub, seq_count, wide),
                    lambda b, *_: (jnp.minimum(2 * b + 2, 2 * blocks - 1), 0, 0),
                ),
            ]
            + [fixed(*source.shape) for source in sources],
            out_specs=[
                at_time(cols.total),
                at_time(hidden),
                at_time(hidden),
                pl.BlockSpec(memory_space=pl.ANY),
                pl.BlockSpec(memory_space=pl.ANY),
            ],
            scratch_shapes=[
                pltpu.VMEM((4, hidden, plan.columns), BF16),
                pltpu.VMEM((hidden, cols.total), BF16),
                pltpu.VMEM((sub * seq_count, cols.total), F32),
                pltpu.VMEM((sub * seq_count, cols.total), F32),
                pltpu.VMEM((seq_count, hidden), F32),
                pltpu.VMEM((seq_count, hidden), BF16),
                pltpu.SemaphoreType.DMA((2,)),
            ],
        ),
        out_shape=[
            jax.ShapeDtypeStruct((time_steps, seq_count, cols.total), F32),
            jax.ShapeDtypeStruct((time_steps, seq_count, hidden), F32),
            jax.ShapeDtypeStruct((time_steps, seq_count, hidden), BF16),
            jax.ShapeDtypeStruct((4, hidden, wide), BF16),
            jax.ShapeDtypeStruct((4, hidden, plan.columns - wide), BF16),
        ],
        compiler_params=params(58),
        name="forward",
    )(at, dropped, dropped, dropped, *sources)

    back_steps = sub
    back_blocks = time_steps // back_steps

    def back(b):
        return back_blocks - 1 - b

    def before(width):
        return pl.BlockSpec(
            (1, seq_count, width), lambda b, *_: (jnp.maximum(back(b) * back_steps - 1, 0), 0, 0)
        )

    def back_time(width):
        return pl.BlockSpec((back_steps, seq_count, width), lambda b, *_: (back(b), 0, 0))

    def later_time(width):
        return pl.BlockSpec(
            (back_steps, seq_count, width),
            lambda b, *_: (jnp.minimum(back(b) + 1, back_blocks - 1), 0, 0),
        )

    part_rows = ceil_to(-(-row_count // seq_n), 8)
    columns = wide + hidden
    group_row = groups.astype(F32)[None]
    sum_specs = [fixed(seq_n, part_rows, columns)] * 2
    sum_shapes = [
        jax.ShapeDtypeStruct((seq_n, part_rows, columns), F32),
        jax.ShapeDtypeStruct((seq_n, part_rows, columns), BF16),
    ]
    sum_scratch = pltpu.VMEM((2, seq_n * part_rows, columns), F32)
    per_unit = pltpu.VMEM((seq_count, hidden), F32)
    own_specs, own_arrays, own_scratch = [], [], []
    if own:
        own_specs = [
            later_time(wide),
            later_time(hidden),
            fixed(back_steps, seq_count, wide),
            fixed(back_steps, seq_count, hidden),
            fixed(1, seq_count),
            fixed(row_count, hidden),
        ]
        own_arrays = [dropped, prev_low, dropped, prev_low, group_row, weight_mask]
        own_scratch = [
            pltpu.VMEM((back_steps * seq_count, hidden), BF16),
            pltpu.VMEM((2, hidden, back_steps * seq_count), BF16),
            pltpu.VMEM((1, back_steps * seq_count), BF16),
            sum_scratch,
        ]
    grads, *sums = pl.pallas_call(
        functools.partial(backward_kernel, cols, own),
        grid_spec=pltpu.PrefetchScalarGridSpec(
            num_scalar_prefetch=1,
            grid=(back_blocks,),
            in_specs=[
                back_time(cols.total),
                back_time(hidden),
                before(hidden),
                before(cols.total),
                back_time(hidden),
                fixed(seq_count, hidden),
                fixed(1, seq_count),
                fixed(1, seq_count),
                fixed(4, hidden, plan.columns - wide),
            ]
            + own_specs,
            out_specs=[back_time(cols.total)] + sum_specs * own,
            scratch_shapes=own_scratch
            + [per_unit] * 6
            + [pltpu.VMEM((seq_count, LANES), F32)] * 2,
        ),
        out_shape=[jax.ShapeDtypeStruct((time_steps, seq_count, cols.total), BF16)]
        + sum_shapes * own,
        compiler_params=params(58),
        name="backward",
    )(
        at,
        acts,
        cells,
        cells,
        acts,
        cot_time,
        out_mask,
        seq_ratio[None],
        lengths.astype(F32)[None],
        w_rec,
        *own_arrays,
    )

    if not own:
        own_rows = lax.dynamic_slice_in_dim(
            cols.unpack_lanes(grads), row_at * row_count, row_count, 2
        )
        sums = pl.pallas_call(
            weight_kernel,
            grid_spec=pltpu.PrefetchScalarGridSpec(
                num_scalar_prefetch=1,
                grid=(blocks,),
                in_specs=[
                    at_time(row_count),
                    fixed(1, seq_count),
                    at_time(wide),
                    at_time(hidden),
                    fixed(row_count, hidden),
                ],
                out_specs=sum_specs,
                scratch_shapes=[sum_scratch, pltpu.VMEM((seq_count, row_count), BF16)],
            ),
            out_shape=sum_shapes,
            compiler_params=params(58),
            name="weights",
        )(grp_at[None], own_rows, group_row, dropped, prev_low, weight_mask)
    keep, send = sums

    hold = lax.optimization_barrier
    block = (keep + flip(send, "grp", 1).astype(F32)).astype(BF16)
    swapped = lax.all_to_all(block, "seq", 0, 0, tiled=True)

    own_seqs = lax.dynamic_slice_in_dim(grads, row_at * share, share, 1)
    own_scale = lax.dynamic_slice_in_dim(in_mask, row_at * share, share, 0).astype(F32) / KEEP_INPUT
    w_in = cols.pack(weights[:, :, :width_in])
    input_time = jnp.einsum("tsr,rk->tsk", own_seqs, w_in, preferred_element_type=F32)
    input_grad = jnp.swapaxes(input_time * own_scale[None], 0, 1)
    swapped, input_grad = hold((swapped, input_grad))

    total = jnp.sum(swapped.astype(F32), 0).astype(BF16)
    copies = jnp.broadcast_to(total[None], (seq_n,) + total.shape)
    parts = lax.all_to_all(copies, "seq", 0, 0, tiled=True)
    peer = flip(total, "grp", 1)
    ours, theirs = (
        jnp.concatenate([part[:, : width_in + 1], part[:, wide:]], 1).astype(F32)
        for part in (total, peer)
    )
    first = jnp.where(grp_at == 0, ours, theirs)
    second = jnp.where(grp_at == 0, theirs, ours)
    dots = [jnp.sum(a * b) for a, b in ((first, first), (first, second), (second, second))]
    gram = jnp.stack([dots[0], dots[1], dots[1], dots[2]]).reshape(2, 2)
    gram = exchange_sum(gram, "row")
    first, *rest = [flip(gram, "seq", bit) for bit in range(1, seq_n)]
    parts, first = hold((parts, first))
    gram = (gram + first) + (rest[0] + rest[1])
    everyone = parts.reshape(seq_n * part_rows, wide + hidden)[:row_count].astype(F32)
    return (
        input_grad,
        everyone[None, :, :width_in],
        everyone[None, :, wide:],
        everyone[None, :, width_in],
        gram,
    )


def solution(mesh):
    return jax.shard_map(
        local,
        mesh=mesh,
        in_specs=(
            P(("grp", "seq"), None, None),
            P(("grp", "seq"), None),
            P(("grp", "seq"), None),
            P(("grp", "seq")),
            P(("grp", "seq")),
            P("row", None),
            P("row", None),
            P("row", None),
            P("row"),
            P(("grp", "seq"), None, None),
        ),
        out_specs=(
            P(("grp", "seq", "row"), None, None),
            P("grp", "row", None),
            P("grp", "row", None),
            P("grp", "row"),
            P(),
        ),
        check_vma=False,
    )
```

```python
import functools

import jax
import jax.numpy as jnp
from jax import lax
from jax.experimental import pallas as pl
from jax.experimental.pallas import tpu as pltpu
from jax.sharding import PartitionSpec as P

ACTIVATION_COEF = 2.0
TAR_BETA = 1.0
KEEP_INPUT = 0.75
KEEP_OUTPUT = 0.6
KEEP_WEIGHT = 0.5
LANES = 128
TILE = 256
BF16 = jnp.bfloat16
F32 = jnp.float32
OVER_ROWS = (((0,), (0,)), ((), ()))


def ceil_to(value, step):
    return -(-value // step) * step


def dot(left, right):
    return jnp.dot(left, right, preferred_element_type=F32)


def flip(block, axis, bit):
    count = lax.axis_size(axis)
    return lax.ppermute(block, axis, [(at, at ^ bit) for at in range(count)])


def exchange_sum(block, axis):
    count = lax.axis_size(axis)
    if count not in (2, 4):
        return lax.psum(block, axis)
    parts = [block] + [flip(block, axis, bit) for bit in range(1, count)]
    while len(parts) > 1:
        parts = [parts[at] + parts[at + 1] for at in range(0, len(parts), 2)]
    return parts[0]


def sigmoid(value):
    return 0.5 * jnp.tanh(0.5 * value) + 0.5


class Columns:
    def __init__(self, hidden):
        self.hidden = hidden
        self.full = hidden // LANES
        self.rest = hidden - self.full * LANES
        assert 0 < 4 * self.rest <= LANES
        self.total = 4 * hidden
        self.order = (self.full,) + tuple(range(self.full))

    def units(self, j):
        return j * LANES, min((j + 1) * LANES, self.hidden)

    def gates(self, j):
        return 4 * j * LANES, min(4 * (j + 1) * LANES, self.total)

    def gate(self, j, q):
        width = LANES if j < self.full else self.rest
        start = 4 * j * LANES + q * width
        return start, start + width

    def pack(self, gated):
        parts = []
        for j in range(self.full + 1):
            first, last = self.units(j)
            parts.append(gated[:, first:last].reshape((-1,) + gated.shape[2:]))
        return jnp.concatenate(parts, 0)

    def unpack_lanes(self, packed):
        parts = []
        for q in range(4):
            for j in range(self.full + 1):
                first, last = self.gate(j, q)
                parts.append(packed[..., first:last])
        return jnp.concatenate(parts, -1)


def drop_kernel(width, tok_ref, mask_ref, drop_ref):
    scale = mask_ref[...].astype(F32) * (1.0 / KEEP_INPUT)
    for k in range(tok_ref.shape[0]):
        drop_ref[k, :, :width] = (tok_ref[k].astype(F32) * scale).astype(BF16)
        drop_ref[k, :, width:] = jnp.ones_like(drop_ref[k, :, width:])


def turned_dot(left, right):
    return lax.dot_general(left, right, (((1,), (1,)), ((), ())), preferred_element_type=F32)


def identity(size):
    line = lax.broadcasted_iota(jnp.int32, (size, size), 0)
    same = line == lax.broadcasted_iota(jnp.int32, (size, size), 1)
    return same.astype(F32).astype(BF16)


def shard_kernel(plan, at_ref, in_ref, rec_ref, mask_ref, bias_ref, own_ref, *mine_ref):
    rows, width = in_ref.shape
    hidden = rec_ref.shape[1]
    bias = bias_ref[...]
    high = bias.astype(BF16)
    pair = jnp.concatenate([high, (bias - high.astype(F32)).astype(BF16)], 0)
    scale = mask_ref[...].astype(F32) / KEEP_WEIGHT
    own_ref[:, :width] = in_ref[...]
    own_ref[:, width : width + 2] = turned_dot(identity(rows), pair).astype(BF16)
    own_ref[:, plan.wide : plan.wide + hidden] = (rec_ref[...].astype(F32) * scale).astype(BF16)
    own_ref[:, plan.wide + hidden :] = jnp.zeros_like(own_ref[:, plan.wide + hidden :])
    for ref in mine_ref:
        ref[...] = own_ref[plan.window(at_ref[1], at_ref[2], 0, plan.rows)]


class Plan:
    def __init__(self, hidden, wide):
        self.wide = wide
        self.columns = ceil_to(wide + hidden, LANES)
        self.row_step = hidden // 32 * 16
        self.rows = hidden - self.row_step
        self.first = ceil_to(self.rows // 2, 16)
        self.column_step = self.columns // LANES // 2 * LANES
        self.cut = self.columns - self.column_step

    def window(self, seq_at, grp_at, start, count):
        half = (seq_at ^ (seq_at >> 1)) & 1
        return (
            pl.ds(pl.multiple_of(half * self.row_step + start, 16), count),
            pl.ds(pl.multiple_of(grp_at * self.column_step, LANES), self.cut),
        )

    def places(self):
        first, rest = self.first, self.rows - self.first
        return [
            (0, 1, 0, 0, self.rows),
            (0, 2, 0, 0, self.rows),
            (0, 1, 1, 0, first),
            (0, 2, 1, 0, first),
            (0, 1, 1, first, rest),
            (0, 2, 1, first, rest),
            (0, 3, 0, 0, self.rows),
            (1, 3, 1, 0, first),
            (1, 3, 1, first, rest),
        ]


def forward_kernel(cols, plan, sub, pieced, at_ref, first_ref, second_ref, third_ref, *refs):
    count = 5 if pieced else 1
    sources = refs[:count]
    act_ref, cell_ref, prev_ref, w_out, rec_out, w_ref, turned, even, odd, cell_s, low_s, sems = refs[
        count:
    ]
    seqs, width = first_ref.shape[1:]
    steps = act_ref.shape[0]
    hidden = cols.hidden

    def columns_of(rows_ref, start, stop, first, last):
        parts = []
        for j in range(cols.full + 1):
            unit, _ = cols.units(j)
            for q in range(4):
                low, high = cols.gate(j, q)
                if low >= start and high <= stop:
                    parts.append(rows_ref[q, unit : unit + high - low, first:last])
        return jnp.concatenate(parts, 0)

    copies = [
        pltpu.make_async_copy(w_ref.at[:, :, :width], w_out, sems.at[0]),
        pltpu.make_async_copy(w_ref.at[:, :, width:], rec_out, sems.at[1]),
    ]

    @pl.when(pl.program_id(0) == 0)
    def _():
        if pieced:
            row_at, seq_at, grp_at = at_ref[0], at_ref[1], at_ref[2]
            w_ref[row_at] = sources[0][...]
            for gi in range(2):
                line = [0, 0]
                for array, k, m, start, size in plan.places():
                    window = plan.window(seq_at ^ m, grp_at ^ gi, start, size)
                    piece = sources[1 + 2 * gi + array][line[array] : line[array] + size]
                    w_ref[(row_at ^ k,) + window] = piece
                    line[array] += size
        else:
            w_ref[...] = sources[0][...]
        for copy in copies:
            copy.start()
        turned[...] = turned_dot(
            identity(hidden), columns_of(w_ref, 0, cols.total, width, width + hidden)
        ).astype(BF16)
        cell_s[...] = jnp.zeros_like(cell_s)
        low_s[...] = jnp.zeros_like(low_s)
        even[...] = turned_dot(
            first_ref[...].reshape(sub * seqs, width), columns_of(w_ref, 0, cols.total, 0, width)
        )

    lane = lax.broadcasted_iota(jnp.int32, (1, 4 * cols.rest), 1)
    tanh_lane = (lane >= 2 * cols.rest) & (lane < 3 * cols.rest)
    rest_mul = jnp.where(tanh_lane, 1.0, 0.5)
    rest_add = jnp.where(tanh_lane, 0.0, 0.5)
    spans = [cols.units(j) for j in range(cols.full + 1)]
    cells = [cell_s[:, a:b] for a, b in spans]
    lows = [low_s[:, a:b] for a, b in spans]
    chunk = ceil_to(-(-cols.total // sub), TILE)
    for k in range(steps):
        u, v = divmod(k, sub)
        now, later = (even, odd) if u % 2 == 0 else (odd, even)
        start, stop = chunk * v, min(chunk * (v + 1), cols.total)
        if start < stop:
            rows = (second_ref, third_ref)[u][...].reshape(sub * seqs, width)
            later[:, start:stop] = turned_dot(rows, columns_of(w_ref, start, stop, 0, width))
        for (a, b), low in zip(spans, lows):
            prev_ref[k, :, a:b] = low
        low = jnp.concatenate(lows, 1)
        lows = [None] * len(spans)
        for j in cols.order:
            first, last = cols.gates(j)
            pre = now[v * seqs : (v + 1) * seqs, first:last] + dot(low, turned[:, first:last])
            if j < cols.full:
                gate_i, gate_f, gate_g, gate_o = (
                    pre[:, q * LANES : (q + 1) * LANES] for q in range(4)
                )
                gate_i, gate_f, gate_o = sigmoid(gate_i), sigmoid(gate_f), sigmoid(gate_o)
                gate_g = jnp.tanh(gate_g)
                for q, gate in enumerate((gate_i, gate_f, gate_g, gate_o)):
                    a, b = cols.gate(j, q)
                    act_ref[k, :, a:b] = gate
            else:
                act = rest_mul * jnp.tanh(rest_mul * pre) + rest_add
                act_ref[k, :, first:last] = act
                gate_i, gate_f, gate_g, gate_o = (
                    act[:, q * cols.rest : (q + 1) * cols.rest] for q in range(4)
                )
            a, b = spans[j]
            cells[j] = gate_f * cells[j] + gate_i * gate_g
            cell_ref[k, :, a:b] = cells[j]
            lows[j] = (gate_o * jnp.tanh(cells[j])).astype(BF16)
    for j, (a, b) in enumerate(spans):
        cell_s[:, a:b] = cells[j]
        low_s[:, a:b] = lows[j]

    @pl.when(pl.program_id(0) == pl.num_programs(0) - 1)
    def _():
        for copy in copies:
            copy.wait()


def backward_kernel(
    cols,
    own,
    at_ref,
    act_ref,
    cell_ref,
    before_ref,
    act_before_ref,
    cot_ref,
    mask_ref,
    ratio_ref,
    length_row_ref,
    rec_ref,
    *refs,
):
    grad_ref = refs[6 if own else 0]
    if own:
        drop_ref, prev_ref, drop_end_ref, prev_end_ref, group_ref, weight_mask_ref = refs[:6]
        keep_ref, send_ref = refs[7:9]
        own_s, sides, pick, sums = refs[9:13]
    dcell_s, recur_s, smooth_s, tanh_s, scale_s, coef_s, smooth_coef_s, length_s = refs[-8:]
    steps, seqs, _ = act_ref.shape
    hidden_n = cols.hidden
    place = pl.program_id(0)
    block = pl.num_programs(0) - 1 - place
    spans = [cols.units(j) for j in range(cols.full + 1)]

    @pl.when(place == 0)
    def _():
        dcell_s[...] = jnp.zeros_like(dcell_s)
        recur_s[...] = jnp.zeros_like(recur_s)
        smooth_s[...] = jnp.zeros_like(smooth_s)
        tanh_s[...] = jnp.tanh(cell_ref[steps - 1])
        ratio = column_of(ratio_ref[...])
        length_s[...] = column_of(length_row_ref[...])
        smooth_coef_s[...] = 2.0 * TAR_BETA * ratio
        scale_s[...] = mask_ref[...].astype(F32) * (1.0 / KEEP_OUTPUT)
        for a, b in spans:
            scale = scale_s[:, a:b]
            coef_s[:, a:b] = 2.0 * ACTIVATION_COEF * ratio[:, : b - a] * scale * scale
        if own:
            sums[...] = jnp.zeros_like(sums)
            sides[...] = jnp.zeros_like(sides)
            first = (group_ref[...] == 0.0).astype(F32).astype(BF16)
            for k in range(steps):
                pick[:, k * seqs : (k + 1) * seqs] = first

    inner = (block > 0).astype(F32)
    rec = jnp.concatenate([rec_ref[q, a:b, :hidden_n] for a, b in spans for q in range(4)], 0)
    jobs = []
    if own:
        width = drop_ref.shape[2]
        for kind, count in enumerate((width, hidden_n)):
            for start in range(0, count, TILE):
                jobs += [(kind, start, min(start + TILE, count), q) for q in range(2)]

    def weight_job(n, data):
        kind, start, stop, q = jobs[n]
        values = data[kind][...].reshape(steps * seqs, data[kind].shape[2])[:, start:stop]
        base = kind * width
        sums[q, :hidden_n, base + start : base + stop] += dot(sides[q], values)

    def gates_at(k, j):
        if j < cols.full:
            return [act_ref[k, :, a:b] for a, b in (cols.gate(j, q) for q in range(4))]
        first, last = cols.gates(j)
        packed = act_ref[k, :, first:last]
        return [packed[:, q * cols.rest : (q + 1) * cols.rest] for q in range(4)]

    for k in range(steps - 1, -1, -1):
        late = steps - 1 - k
        for n in range(late * len(jobs) // steps, (late + 1) * len(jobs) // steps):
            weight_job(n, (drop_ref, prev_ref))
        for j in cols.order:
            a, b = spans[j]
            gate_i, gate_f, gate_g, gate_o = gates_at(k, j)
            tanh_cell = tanh_s[:, a:b]
            hidden = gate_o * tanh_cell
            low, high = cols.gate(j, 3)
            if k > 0:
                cell_before = cell_ref[k - 1, :, a:b]
                out_before = act_ref[k - 1, :, low:high]
            else:
                cell_before = before_ref[0, :, a:b] * inner
                out_before = act_before_ref[0, :, low:high]
            tanh_before = jnp.tanh(cell_before)
            tanh_s[:, a:b] = tanh_before
            valid = length_s[:, : b - a] > (block * steps + k).astype(F32)
            smooth = smooth_coef_s[:, : b - a] * (hidden - out_before * tanh_before)
            if k == 0:
                smooth = smooth * inner
            smooth = jnp.where(valid, smooth, 0.0)
            direct = scale_s[:, a:b] * cot_ref[k, :, a:b].astype(F32) + coef_s[:, a:b] * hidden
            direct = jnp.where(valid, direct, 0.0) + smooth - smooth_s[:, a:b]
            smooth_s[:, a:b] = smooth
            dhidden = direct + recur_s[:, a:b]
            total = dcell_s[:, a:b] + dhidden * (gate_o * (1.0 - tanh_cell * tanh_cell))
            dcell_s[:, a:b] = total * gate_f
            grads = [
                (total * (gate_g * gate_i * (1.0 - gate_i))).astype(BF16),
                (total * (cell_before * gate_f * (1.0 - gate_f))).astype(BF16),
                (total * (gate_i * (1.0 - gate_g * gate_g))).astype(BF16),
                (dhidden * (tanh_cell * gate_o * (1.0 - gate_o))).astype(BF16),
            ]
            first, last = cols.gates(j)
            grad_ref[k, :, first:last] = jnp.concatenate(grads, 1)
            if own:
                mine = grads[3]
                for q in range(3):
                    mine = jnp.where(at_ref[0] == q, grads[q], mine)
                own_s[k * seqs : (k + 1) * seqs, a:b] = mine
        recur_s[...] = dot(grad_ref[k], rec)
    if own:
        turned = own_s[...].T
        first = turned * pick[...]
        sides[0] = first
        sides[1] = turned - first

        @pl.when(block == 0)
        def _():
            for n in range(len(jobs)):
                weight_job(n, (drop_end_ref, prev_end_ref))
            scale = weight_mask_ref[...].astype(F32) * (1.0 / KEEP_WEIGHT)
            for q in range(2):
                sums[q, :hidden_n, width:] = sums[q, :hidden_n, width:] * scale
            hand_out(at_ref[2], sums, keep_ref, send_ref)


def hand_out(grp_at, sums, keep_ref, send_ref):
    rows = keep_ref.shape[1]
    for part in range(keep_ref.shape[0]):
        span = slice(part * rows, (part + 1) * rows)
        keep_ref[part] = sums[grp_at, span]
        send_ref[part] = sums[1 - grp_at, span].astype(BF16)


def weight_kernel(grp_ref, rows_ref, group_ref, drop_ref, prev_ref, mask_ref, keep_ref, send_ref, sums, pick):
    steps, seqs, own = rows_ref.shape
    place = pl.program_id(0)

    @pl.when(place == 0)
    def _():
        sums[...] = jnp.zeros_like(sums)
        one = (column_of(group_ref[...]) == 0.0).astype(F32).astype(BF16)
        for at in range(0, own, LANES):
            width = min(LANES, own - at)
            pick[:, at : at + width] = one[:, :width]

    grads = rows_ref[...]
    first = (grads * pick[...][None]).reshape(steps * seqs, own)
    second = grads.reshape(steps * seqs, own) - first
    start = 0
    for ref in (drop_ref, prev_ref):
        width = ref.shape[2]
        values = ref[...].reshape(steps * seqs, width)
        for at, part in enumerate((first, second)):
            sums[at, :own, start : start + width] += lax.dot_general(
                part, values, OVER_ROWS, preferred_element_type=F32
            )
        start += width

    @pl.when(place == pl.num_programs(0) - 1)
    def _():
        scale = mask_ref[...].astype(F32) * (1.0 / KEEP_WEIGHT)
        for at in range(2):
            part = (at, slice(0, own), slice(start - width, start))
            sums[part] = sums[part] * scale
        hand_out(grp_ref[0], sums, keep_ref, send_ref)


def params(megabytes):
    return pltpu.CompilerParams(
        dimension_semantics=("arbitrary",), vmem_limit_bytes=megabytes << 20
    )


def fixed(*shape):
    return pl.BlockSpec(shape, lambda *_: (0,) * len(shape), pipeline_mode=pl.Buffered(1))


def column_of(row):
    return jnp.broadcast_to(row, (LANES, row.shape[1])).T


def gather_pieces(plan, mine, counts, beside):
    hold = lax.optimization_barrier
    cut = plan.cut
    one, two, beside, counts = hold(
        (flip(mine, "row", 1), flip(mine, "row", 2), beside, counts + flip(counts, "grp", 1))
    )
    near = jnp.stack([one, two])
    near_x, near_y, three, counts = hold(
        (
            flip(near[:, : plan.first], "seq", 1),
            flip(near[:, plan.first :], "seq", 2),
            flip(two, "row", 1),
            counts + flip(counts, "seq", 1),
        )
    )
    early = jnp.concatenate([part.reshape(-1, cut) for part in (near, near_x, near_y, three)], 0)
    last_x, last_y, early_other, counts = hold(
        (
            flip(three[: plan.first], "seq", 1),
            flip(three[plan.first :], "seq", 2),
            flip(early, "grp", 1),
            counts + flip(counts, "seq", 2),
        )
    )
    late = jnp.concatenate([last_x, last_y], 0)
    return early, late, early_other, flip(late, "grp", 1), counts, beside


def local(
    tokens,
    in_mask,
    out_mask,
    lengths,
    groups,
    input_gate_weight,
    w_recur,
    weight_mask,
    bias,
    cotangent,
):
    seq_count, time_steps, width_in = tokens.shape
    hidden = cotangent.shape[2]
    row_count = input_gate_weight.shape[0]
    row_at = lax.axis_index("row")
    grp_at = lax.axis_index("grp")
    seq_at = lax.axis_index("seq")
    rows_n, seq_n = lax.axis_size("row"), lax.axis_size("seq")
    cols = Columns(hidden)
    wide = ceil_to(width_in + 2, LANES)
    share = seq_count // rows_n
    own = row_count == hidden
    pieced = own and rows_n == 4 and seq_n == 4 and lax.axis_size("grp") == 2

    plan = Plan(hidden, wide)
    at = jnp.stack([row_at, seq_at, grp_at]).astype(jnp.int32)
    own_weights, *mine = pl.pallas_call(
        functools.partial(shard_kernel, plan),
        grid_spec=pltpu.PrefetchScalarGridSpec(
            num_scalar_prefetch=1,
            grid=(1,),
            in_specs=[
                fixed(row_count, width_in),
                fixed(row_count, hidden),
                fixed(row_count, hidden),
                fixed(1, row_count),
            ],
            out_specs=[fixed(row_count, plan.columns)] + [fixed(plan.rows, plan.cut)] * pieced,
        ),
        out_shape=[jax.ShapeDtypeStruct((row_count, plan.columns), BF16)]
        + [jax.ShapeDtypeStruct((plan.rows, plan.cut), BF16)] * pieced,
        compiler_params=params(58),
        name="shard",
    )(at, input_gate_weight, w_recur, weight_mask, bias[None])
    sub = max(s for s in range(1, 8) if time_steps % (2 * s) == 0)
    steps = 2 * sub
    blocks = time_steps // steps

    def at_time(width):
        return pl.BlockSpec((steps, seq_count, width), lambda b, *_: (b, 0, 0))

    dropped = pl.pallas_call(
        functools.partial(drop_kernel, width_in),
        grid=(blocks,),
        in_specs=[at_time(width_in), fixed(seq_count, width_in)],
        out_specs=at_time(wide),
        out_shape=jax.ShapeDtypeStruct((time_steps, seq_count, wide), BF16),
        compiler_params=params(58),
        name="drop",
    )(jnp.swapaxes(tokens, 0, 1), in_mask)
    cot_time = jnp.swapaxes(cotangent, 0, 1)

    group_hot = (groups[:, None] == jnp.arange(2)[None, :]).astype(F32)
    valid_count = jnp.clip(lengths, 0, time_steps).astype(F32)
    counts = jnp.sum(group_hot * valid_count[:, None], 0)
    if pieced:
        *pieces, counts, dropped = gather_pieces(plan, mine[0], counts, dropped)
        sources = [own_weights] + pieces
    else:
        counts = lax.psum(counts, ("grp", "seq"))
        whole = lax.all_gather(own_weights, "row", axis=0, tiled=True)
        sources = [whole.reshape(4, hidden, plan.columns)]
    group_ratio = jnp.sum(counts) / counts
    seq_ratio = jnp.sum(group_hot * group_ratio[None, :], 1)

    acts, cells, prev_low, weights, w_rec = pl.pallas_call(
        functools.partial(forward_kernel, cols, plan, sub, pieced),
        grid_spec=pltpu.PrefetchScalarGridSpec(
            num_scalar_prefetch=1,
            grid=(blocks,),
            in_specs=[
                fixed(sub, seq_count, wide),
                pl.BlockSpec((sub, seq_count, wide), lambda b, *_: (2 * b + 1, 0, 0)),
                pl.BlockSpec(
                    (sub, seq_count, wide),
                    lambda b, *_: (jnp.minimum(2 * b + 2, 2 * blocks - 1), 0, 0),
                ),
            ]
            + [fixed(*source.shape) for source in sources],
            out_specs=[
                at_time(cols.total),
                at_time(hidden),
                at_time(hidden),
                pl.BlockSpec(memory_space=pl.ANY),
                pl.BlockSpec(memory_space=pl.ANY),
            ],
            scratch_shapes=[
                pltpu.VMEM((4, hidden, plan.columns), BF16),
                pltpu.VMEM((hidden, cols.total), BF16),
                pltpu.VMEM((sub * seq_count, cols.total), F32),
                pltpu.VMEM((sub * seq_count, cols.total), F32),
                pltpu.VMEM((seq_count, hidden), F32),
                pltpu.VMEM((seq_count, hidden), BF16),
                pltpu.SemaphoreType.DMA((2,)),
            ],
        ),
        out_shape=[
            jax.ShapeDtypeStruct((time_steps, seq_count, cols.total), F32),
            jax.ShapeDtypeStruct((time_steps, seq_count, hidden), F32),
            jax.ShapeDtypeStruct((time_steps, seq_count, hidden), BF16),
            jax.ShapeDtypeStruct((4, hidden, wide), BF16),
            jax.ShapeDtypeStruct((4, hidden, plan.columns - wide), BF16),
        ],
        compiler_params=params(52),
        name="forward",
    )(at, dropped, dropped, dropped, *sources)

    back_steps = sub
    back_blocks = time_steps // back_steps

    def back(b):
        return back_blocks - 1 - b

    def before(width):
        return pl.BlockSpec(
            (1, seq_count, width), lambda b, *_: (jnp.maximum(back(b) * back_steps - 1, 0), 0, 0)
        )

    def back_time(width):
        return pl.BlockSpec((back_steps, seq_count, width), lambda b, *_: (back(b), 0, 0))

    def later_time(width):
        return pl.BlockSpec(
            (back_steps, seq_count, width),
            lambda b, *_: (jnp.minimum(back(b) + 1, back_blocks - 1), 0, 0),
        )

    part_rows = ceil_to(-(-row_count // seq_n), 8)
    columns = wide + hidden
    group_row = groups.astype(F32)[None]
    sum_specs = [fixed(seq_n, part_rows, columns)] * 2
    sum_shapes = [
        jax.ShapeDtypeStruct((seq_n, part_rows, columns), F32),
        jax.ShapeDtypeStruct((seq_n, part_rows, columns), BF16),
    ]
    sum_scratch = pltpu.VMEM((2, seq_n * part_rows, columns), F32)
    per_unit = pltpu.VMEM((seq_count, hidden), F32)
    own_specs, own_arrays, own_scratch = [], [], []
    if own:
        own_specs = [
            later_time(wide),
            later_time(hidden),
            fixed(back_steps, seq_count, wide),
            fixed(back_steps, seq_count, hidden),
            fixed(1, seq_count),
            fixed(row_count, hidden),
        ]
        own_arrays = [dropped, prev_low, dropped, prev_low, group_row, weight_mask]
        own_scratch = [
            pltpu.VMEM((back_steps * seq_count, hidden), BF16),
            pltpu.VMEM((2, hidden, back_steps * seq_count), BF16),
            pltpu.VMEM((1, back_steps * seq_count), BF16),
            sum_scratch,
        ]
    grads, *sums = pl.pallas_call(
        functools.partial(backward_kernel, cols, own),
        grid_spec=pltpu.PrefetchScalarGridSpec(
            num_scalar_prefetch=1,
            grid=(back_blocks,),
            in_specs=[
                back_time(cols.total),
                back_time(hidden),
                before(hidden),
                before(cols.total),
                back_time(hidden),
                fixed(seq_count, hidden),
                fixed(1, seq_count),
                fixed(1, seq_count),
                fixed(4, hidden, plan.columns - wide),
            ]
            + own_specs,
            out_specs=[back_time(cols.total)] + sum_specs * own,
            scratch_shapes=own_scratch
            + [per_unit] * 6
            + [pltpu.VMEM((seq_count, LANES), F32)] * 2,
        ),
        out_shape=[jax.ShapeDtypeStruct((time_steps, seq_count, cols.total), BF16)]
        + sum_shapes * own,
        compiler_params=params(52),
        name="backward",
    )(
        at,
        acts,
        cells,
        cells,
        acts,
        cot_time,
        out_mask,
        seq_ratio[None],
        lengths.astype(F32)[None],
        w_rec,
        *own_arrays,
    )

    if not own:
        own_rows = lax.dynamic_slice_in_dim(
            cols.unpack_lanes(grads), row_at * row_count, row_count, 2
        )
        sums = pl.pallas_call(
            weight_kernel,
            grid_spec=pltpu.PrefetchScalarGridSpec(
                num_scalar_prefetch=1,
                grid=(blocks,),
                in_specs=[
                    at_time(row_count),
                    fixed(1, seq_count),
                    at_time(wide),
                    at_time(hidden),
                    fixed(row_count, hidden),
                ],
                out_specs=sum_specs,
                scratch_shapes=[sum_scratch, pltpu.VMEM((seq_count, row_count), BF16)],
            ),
            out_shape=sum_shapes,
            compiler_params=params(58),
            name="weights",
        )(grp_at[None], own_rows, group_row, dropped, prev_low, weight_mask)
    keep, send = sums

    hold = lax.optimization_barrier
    block = (keep + flip(send, "grp", 1).astype(F32)).astype(BF16)
    swapped = lax.all_to_all(block, "seq", 0, 0, tiled=True)

    own_seqs = lax.dynamic_slice_in_dim(grads, row_at * share, share, 1)
    own_scale = lax.dynamic_slice_in_dim(in_mask, row_at * share, share, 0).astype(F32) / KEEP_INPUT
    w_in = cols.pack(weights[:, :, :width_in])
    input_time = jnp.einsum("tsr,rk->tsk", own_seqs, w_in, preferred_element_type=F32)
    input_grad = jnp.swapaxes(input_time * own_scale[None], 0, 1)
    swapped, input_grad = hold((swapped, input_grad))

    total = jnp.sum(swapped.astype(F32), 0).astype(BF16)
    copies = jnp.broadcast_to(total[None], (seq_n,) + total.shape)
    parts = lax.all_to_all(copies, "seq", 0, 0, tiled=True)
    peer = flip(total, "grp", 1)
    ours, theirs = (
        jnp.concatenate([part[:, : width_in + 1], part[:, wide:]], 1).astype(F32)
        for part in (total, peer)
    )
    first = jnp.where(grp_at == 0, ours, theirs)
    second = jnp.where(grp_at == 0, theirs, ours)
    dots = [jnp.sum(a * b) for a, b in ((first, first), (first, second), (second, second))]
    gram = jnp.stack([dots[0], dots[1], dots[1], dots[2]]).reshape(2, 2)
    gram = exchange_sum(gram, "row")
    first, *rest = [flip(gram, "seq", bit) for bit in range(1, seq_n)]
    parts, first = hold((parts, first))
    gram = (gram + first) + (rest[0] + rest[1])
    everyone = parts.reshape(seq_n * part_rows, wide + hidden)[:row_count].astype(F32)
    return (
        input_grad,
        everyone[None, :, :width_in],
        everyone[None, :, wide:],
        everyone[None, :, width_in],
        gram,
    )


def solution(mesh):
    return jax.shard_map(
        local,
        mesh=mesh,
        in_specs=(
            P(("grp", "seq"), None, None),
            P(("grp", "seq"), None),
            P(("grp", "seq"), None),
            P(("grp", "seq")),
            P(("grp", "seq")),
            P("row", None),
            P("row", None),
            P("row", None),
            P("row"),
            P(("grp", "seq"), None, None),
        ),
        out_specs=(
            P(("grp", "seq", "row"), None, None),
            P("grp", "row", None),
            P("grp", "row", None),
            P("grp", "row"),
            P(),
        ),
        check_vma=False,
    )
```

```python
import functools

import jax
import jax.numpy as jnp
from jax import lax
from jax.experimental import pallas as pl
from jax.experimental.pallas import tpu as pltpu
from jax.sharding import PartitionSpec as P

ACTIVATION_COEF = 2.0
TAR_BETA = 1.0
KEEP_INPUT = 0.75
KEEP_OUTPUT = 0.6
KEEP_WEIGHT = 0.5
LANES = 128
TILE = 256
BF16 = jnp.bfloat16
F32 = jnp.float32
OVER_ROWS = (((0,), (0,)), ((), ()))


def ceil_to(value, step):
    return -(-value // step) * step


def dot(left, right):
    return jnp.dot(left, right, preferred_element_type=F32)


def flip(block, axis, bit):
    count = lax.axis_size(axis)
    return lax.ppermute(block, axis, [(at, at ^ bit) for at in range(count)])


def exchange_sum(block, axis):
    count = lax.axis_size(axis)
    if count not in (2, 4):
        return lax.psum(block, axis)
    parts = [block] + [flip(block, axis, bit) for bit in range(1, count)]
    while len(parts) > 1:
        parts = [parts[at] + parts[at + 1] for at in range(0, len(parts), 2)]
    return parts[0]


def sigmoid(value):
    return 0.5 * jnp.tanh(0.5 * value) + 0.5


class Columns:
    def __init__(self, hidden):
        self.hidden = hidden
        self.full = hidden // LANES
        self.rest = hidden - self.full * LANES
        assert 0 < 4 * self.rest <= LANES
        self.total = 4 * hidden
        self.order = (self.full,) + tuple(range(self.full))

    def units(self, j):
        return j * LANES, min((j + 1) * LANES, self.hidden)

    def gates(self, j):
        return 4 * j * LANES, min(4 * (j + 1) * LANES, self.total)

    def gate(self, j, q):
        width = LANES if j < self.full else self.rest
        start = 4 * j * LANES + q * width
        return start, start + width

    def pack(self, gated):
        parts = []
        for j in range(self.full + 1):
            first, last = self.units(j)
            parts.append(gated[:, first:last].reshape((-1,) + gated.shape[2:]))
        return jnp.concatenate(parts, 0)

    def unpack_lanes(self, packed):
        parts = []
        for q in range(4):
            for j in range(self.full + 1):
                first, last = self.gate(j, q)
                parts.append(packed[..., first:last])
        return jnp.concatenate(parts, -1)


def drop_kernel(width, tok_ref, mask_ref, drop_ref):
    scale = mask_ref[...].astype(F32) * (1.0 / KEEP_INPUT)
    for k in range(tok_ref.shape[0]):
        drop_ref[k, :, :width] = (tok_ref[k].astype(F32) * scale).astype(BF16)
        drop_ref[k, :, width:] = jnp.ones_like(drop_ref[k, :, width:])


def turned_dot(left, right):
    return lax.dot_general(left, right, (((1,), (1,)), ((), ())), preferred_element_type=F32)


def identity(size):
    line = lax.broadcasted_iota(jnp.int32, (size, size), 0)
    same = line == lax.broadcasted_iota(jnp.int32, (size, size), 1)
    return same.astype(F32).astype(BF16)


def shard_kernel(plan, at_ref, in_ref, rec_ref, mask_ref, bias_ref, own_ref, *mine_ref):
    rows, width = in_ref.shape
    hidden = rec_ref.shape[1]
    bias = bias_ref[...]
    high = bias.astype(BF16)
    pair = jnp.concatenate([high, (bias - high.astype(F32)).astype(BF16)], 0)
    scale = mask_ref[...].astype(F32) / KEEP_WEIGHT
    own_ref[:, :width] = in_ref[...]
    own_ref[:, width : width + 2] = turned_dot(identity(rows), pair).astype(BF16)
    own_ref[:, plan.wide : plan.wide + hidden] = (rec_ref[...].astype(F32) * scale).astype(BF16)
    own_ref[:, plan.wide + hidden :] = jnp.zeros_like(own_ref[:, plan.wide + hidden :])
    for ref in mine_ref:
        ref[...] = own_ref[plan.window(at_ref[1], at_ref[2], 0, plan.rows)]


class Plan:
    def __init__(self, hidden, wide):
        self.wide = wide
        self.columns = ceil_to(wide + hidden, LANES)
        self.row_step = hidden // 32 * 16
        self.rows = hidden - self.row_step
        self.first = ceil_to(self.rows // 2, 16)
        self.column_step = self.columns // LANES // 2 * LANES
        self.cut = self.columns - self.column_step

    def window(self, seq_at, grp_at, start, count):
        half = (seq_at ^ (seq_at >> 1)) & 1
        return (
            pl.ds(pl.multiple_of(half * self.row_step + start, 16), count),
            pl.ds(pl.multiple_of(grp_at * self.column_step, LANES), self.cut),
        )

    def places(self):
        first, rest = self.first, self.rows - self.first
        return [
            (0, 1, 0, 0, self.rows),
            (0, 2, 0, 0, self.rows),
            (0, 1, 1, 0, first),
            (0, 2, 1, 0, first),
            (0, 1, 1, first, rest),
            (0, 2, 1, first, rest),
            (0, 3, 0, 0, self.rows),
            (1, 3, 1, 0, first),
            (1, 3, 1, first, rest),
        ]


def forward_kernel(cols, plan, sub, pieced, at_ref, first_ref, second_ref, third_ref, *refs):
    count = 5 if pieced else 1
    sources = refs[:count]
    act_ref, cell_ref, prev_ref, w_out, rec_out, w_ref, turned, even, odd, cell_s, low_s, sems = refs[
        count:
    ]
    seqs, width = first_ref.shape[1:]
    steps = act_ref.shape[0]
    hidden = cols.hidden

    def columns_of(rows_ref, start, stop, first, last):
        parts = []
        for j in range(cols.full + 1):
            unit, _ = cols.units(j)
            for q in range(4):
                low, high = cols.gate(j, q)
                if low >= start and high <= stop:
                    parts.append(rows_ref[q, unit : unit + high - low, first:last])
        return jnp.concatenate(parts, 0)

    copies = [
        pltpu.make_async_copy(w_ref.at[:, :, :width], w_out, sems.at[0]),
        pltpu.make_async_copy(w_ref.at[:, :, width:], rec_out, sems.at[1]),
    ]

    @pl.when(pl.program_id(0) == 0)
    def _():
        if pieced:
            row_at, seq_at, grp_at = at_ref[0], at_ref[1], at_ref[2]
            w_ref[row_at] = sources[0][...]
            for gi in range(2):
                line = [0, 0]
                for array, k, m, start, size in plan.places():
                    window = plan.window(seq_at ^ m, grp_at ^ gi, start, size)
                    piece = sources[1 + 2 * gi + array][line[array] : line[array] + size]
                    w_ref[(row_at ^ k,) + window] = piece
                    line[array] += size
        else:
            w_ref[...] = sources[0][...]
        for copy in copies:
            copy.start()
        turned[...] = turned_dot(
            identity(hidden), columns_of(w_ref, 0, cols.total, width, width + hidden)
        ).astype(BF16)
        cell_s[...] = jnp.zeros_like(cell_s)
        low_s[...] = jnp.zeros_like(low_s)
        even[...] = turned_dot(
            first_ref[...].reshape(sub * seqs, width), columns_of(w_ref, 0, cols.total, 0, width)
        )

    lane = lax.broadcasted_iota(jnp.int32, (1, 4 * cols.rest), 1)
    tanh_lane = (lane >= 2 * cols.rest) & (lane < 3 * cols.rest)
    rest_mul = jnp.where(tanh_lane, 1.0, 0.5)
    rest_add = jnp.where(tanh_lane, 0.0, 0.5)
    spans = [cols.units(j) for j in range(cols.full + 1)]
    cells = [cell_s[:, a:b] for a, b in spans]
    lows = [low_s[:, a:b] for a, b in spans]
    chunk = ceil_to(-(-cols.total // sub), TILE)
    for k in range(steps):
        u, v = divmod(k, sub)
        now, later = (even, odd) if u % 2 == 0 else (odd, even)
        start, stop = chunk * v, min(chunk * (v + 1), cols.total)
        if start < stop:
            rows = (second_ref, third_ref)[u][...].reshape(sub * seqs, width)
            later[:, start:stop] = turned_dot(rows, columns_of(w_ref, start, stop, 0, width))
        for (a, b), low in zip(spans, lows):
            prev_ref[k, :, a:b] = low
        low = jnp.concatenate(lows, 1)
        lows = [None] * len(spans)
        for j in cols.order:
            first, last = cols.gates(j)
            pre = now[v * seqs : (v + 1) * seqs, first:last] + dot(low, turned[:, first:last])
            if j < cols.full:
                gate_i, gate_f, gate_g, gate_o = (
                    pre[:, q * LANES : (q + 1) * LANES] for q in range(4)
                )
                gate_i, gate_f, gate_o = sigmoid(gate_i), sigmoid(gate_f), sigmoid(gate_o)
                gate_g = jnp.tanh(gate_g)
                for q, gate in enumerate((gate_i, gate_f, gate_g, gate_o)):
                    a, b = cols.gate(j, q)
                    act_ref[k, :, a:b] = gate
            else:
                act = rest_mul * jnp.tanh(rest_mul * pre) + rest_add
                act_ref[k, :, first:last] = act
                gate_i, gate_f, gate_g, gate_o = (
                    act[:, q * cols.rest : (q + 1) * cols.rest] for q in range(4)
                )
            a, b = spans[j]
            cells[j] = gate_f * cells[j] + gate_i * gate_g
            cell_ref[k, :, a:b] = cells[j]
            lows[j] = (gate_o * jnp.tanh(cells[j])).astype(BF16)
    for j, (a, b) in enumerate(spans):
        cell_s[:, a:b] = cells[j]
        low_s[:, a:b] = lows[j]

    @pl.when(pl.program_id(0) == pl.num_programs(0) - 1)
    def _():
        for copy in copies:
            copy.wait()


def backward_kernel(
    cols,
    own,
    at_ref,
    act_ref,
    cell_ref,
    before_ref,
    act_before_ref,
    cot_ref,
    mask_ref,
    ratio_ref,
    length_row_ref,
    rec_ref,
    *refs,
):
    grad_ref = refs[6 if own else 0]
    if own:
        drop_ref, prev_ref, drop_end_ref, prev_end_ref, group_ref, weight_mask_ref = refs[:6]
        keep_ref, send_ref = refs[7:9]
        own_s, sides, pick, sums = refs[9:13]
    dcell_s, recur_s, smooth_s, tanh_s, scale_s, coef_s, smooth_coef_s, length_s = refs[-8:]
    steps, seqs, _ = act_ref.shape
    hidden_n = cols.hidden
    place = pl.program_id(0)
    block = pl.num_programs(0) - 1 - place
    spans = [cols.units(j) for j in range(cols.full + 1)]

    @pl.when(place == 0)
    def _():
        dcell_s[...] = jnp.zeros_like(dcell_s)
        recur_s[...] = jnp.zeros_like(recur_s)
        smooth_s[...] = jnp.zeros_like(smooth_s)
        tanh_s[...] = jnp.tanh(cell_ref[steps - 1])
        ratio = column_of(ratio_ref[...])
        length_s[...] = column_of(length_row_ref[...])
        smooth_coef_s[...] = 2.0 * TAR_BETA * ratio
        scale_s[...] = mask_ref[...].astype(F32) * (1.0 / KEEP_OUTPUT)
        for a, b in spans:
            scale = scale_s[:, a:b]
            coef_s[:, a:b] = 2.0 * ACTIVATION_COEF * ratio[:, : b - a] * scale * scale
        if own:
            sums[...] = jnp.zeros_like(sums)
            sides[...] = jnp.zeros_like(sides)
            first = (group_ref[...] == 0.0).astype(F32).astype(BF16)
            for k in range(steps):
                pick[:, k * seqs : (k + 1) * seqs] = first

    inner = (block > 0).astype(F32)
    rec = jnp.concatenate([rec_ref[q, a:b, :hidden_n] for a, b in spans for q in range(4)], 0)
    jobs = []
    if own:
        width = drop_ref.shape[2]
        for kind, count in enumerate((width, hidden_n)):
            for start in range(0, count, TILE):
                jobs += [(kind, start, min(start + TILE, count), q) for q in range(2)]

    def weight_job(n, data):
        kind, start, stop, q = jobs[n]
        values = data[kind][...].reshape(steps * seqs, data[kind].shape[2])[:, start:stop]
        base = kind * width
        sums[q, :hidden_n, base + start : base + stop] += dot(sides[q], values)

    def gates_at(k, j):
        if j < cols.full:
            return [act_ref[k, :, a:b] for a, b in (cols.gate(j, q) for q in range(4))]
        first, last = cols.gates(j)
        packed = act_ref[k, :, first:last]
        return [packed[:, q * cols.rest : (q + 1) * cols.rest] for q in range(4)]

    for k in range(steps - 1, -1, -1):
        late = steps - 1 - k
        for n in range(late * len(jobs) // steps, (late + 1) * len(jobs) // steps):
            weight_job(n, (drop_ref, prev_ref))
        for j in cols.order:
            a, b = spans[j]
            gate_i, gate_f, gate_g, gate_o = gates_at(k, j)
            tanh_cell = tanh_s[:, a:b]
            hidden = gate_o * tanh_cell
            low, high = cols.gate(j, 3)
            if k > 0:
                cell_before = cell_ref[k - 1, :, a:b]
                out_before = act_ref[k - 1, :, low:high]
            else:
                cell_before = before_ref[0, :, a:b] * inner
                out_before = act_before_ref[0, :, low:high]
            tanh_before = jnp.tanh(cell_before)
            tanh_s[:, a:b] = tanh_before
            valid = length_s[:, : b - a] > (block * steps + k).astype(F32)
            smooth = smooth_coef_s[:, : b - a] * (hidden - out_before * tanh_before)
            if k == 0:
                smooth = smooth * inner
            smooth = jnp.where(valid, smooth, 0.0)
            direct = scale_s[:, a:b] * cot_ref[k, :, a:b].astype(F32) + coef_s[:, a:b] * hidden
            direct = jnp.where(valid, direct, 0.0) + smooth - smooth_s[:, a:b]
            smooth_s[:, a:b] = smooth
            dhidden = direct + recur_s[:, a:b]
            total = dcell_s[:, a:b] + dhidden * (gate_o * (1.0 - tanh_cell * tanh_cell))
            dcell_s[:, a:b] = total * gate_f
            grads = [
                (total * (gate_g * gate_i * (1.0 - gate_i))).astype(BF16),
                (total * (cell_before * gate_f * (1.0 - gate_f))).astype(BF16),
                (total * (gate_i * (1.0 - gate_g * gate_g))).astype(BF16),
                (dhidden * (tanh_cell * gate_o * (1.0 - gate_o))).astype(BF16),
            ]
            first, last = cols.gates(j)
            grad_ref[k, :, first:last] = jnp.concatenate(grads, 1)
            if own:
                mine = grads[3]
                for q in range(3):
                    mine = jnp.where(at_ref[0] == q, grads[q], mine)
                own_s[k * seqs : (k + 1) * seqs, a:b] = mine
        recur_s[...] = dot(grad_ref[k], rec)
    if own:
        turned = own_s[...].T
        first = turned * pick[...]
        sides[0] = first
        sides[1] = turned - first

        @pl.when(block == 0)
        def _():
            for n in range(len(jobs)):
                weight_job(n, (drop_end_ref, prev_end_ref))
            scale = weight_mask_ref[...].astype(F32) * (1.0 / KEEP_WEIGHT)
            for q in range(2):
                sums[q, :hidden_n, width:] = sums[q, :hidden_n, width:] * scale
            hand_out(at_ref[2], sums, keep_ref, send_ref)


def hand_out(grp_at, sums, keep_ref, send_ref):
    rows = keep_ref.shape[1]
    for part in range(keep_ref.shape[0]):
        span = slice(part * rows, (part + 1) * rows)
        keep_ref[part] = sums[grp_at, span].astype(BF16)
        send_ref[part] = sums[1 - grp_at, span].astype(BF16)


def weight_kernel(grp_ref, rows_ref, group_ref, drop_ref, prev_ref, mask_ref, keep_ref, send_ref, sums, pick):
    steps, seqs, own = rows_ref.shape
    place = pl.program_id(0)

    @pl.when(place == 0)
    def _():
        sums[...] = jnp.zeros_like(sums)
        one = (column_of(group_ref[...]) == 0.0).astype(F32).astype(BF16)
        for at in range(0, own, LANES):
            width = min(LANES, own - at)
            pick[:, at : at + width] = one[:, :width]

    grads = rows_ref[...]
    first = (grads * pick[...][None]).reshape(steps * seqs, own)
    second = grads.reshape(steps * seqs, own) - first
    start = 0
    for ref in (drop_ref, prev_ref):
        width = ref.shape[2]
        values = ref[...].reshape(steps * seqs, width)
        for at, part in enumerate((first, second)):
            sums[at, :own, start : start + width] += lax.dot_general(
                part, values, OVER_ROWS, preferred_element_type=F32
            )
        start += width

    @pl.when(place == pl.num_programs(0) - 1)
    def _():
        scale = mask_ref[...].astype(F32) * (1.0 / KEEP_WEIGHT)
        for at in range(2):
            part = (at, slice(0, own), slice(start - width, start))
            sums[part] = sums[part] * scale
        hand_out(grp_ref[0], sums, keep_ref, send_ref)


def params(megabytes):
    return pltpu.CompilerParams(
        dimension_semantics=("arbitrary",), vmem_limit_bytes=megabytes << 20
    )


def fixed(*shape):
    return pl.BlockSpec(shape, lambda *_: (0,) * len(shape), pipeline_mode=pl.Buffered(1))


def column_of(row):
    return jnp.broadcast_to(row, (LANES, row.shape[1])).T


def gather_pieces(plan, mine, counts, beside):
    hold = lax.optimization_barrier
    cut = plan.cut
    one, two, beside, counts = hold(
        (flip(mine, "row", 1), flip(mine, "row", 2), beside, counts + flip(counts, "grp", 1))
    )
    near = jnp.stack([one, two])
    near_x, near_y, three, counts = hold(
        (
            flip(near[:, : plan.first], "seq", 1),
            flip(near[:, plan.first :], "seq", 2),
            flip(two, "row", 1),
            counts + flip(counts, "seq", 1),
        )
    )
    early = jnp.concatenate([part.reshape(-1, cut) for part in (near, near_x, near_y, three)], 0)
    last_x, last_y, early_other, counts = hold(
        (
            flip(three[: plan.first], "seq", 1),
            flip(three[plan.first :], "seq", 2),
            flip(early, "grp", 1),
            counts + flip(counts, "seq", 2),
        )
    )
    late = jnp.concatenate([last_x, last_y], 0)
    return early, late, early_other, flip(late, "grp", 1), counts, beside


def local(
    tokens,
    in_mask,
    out_mask,
    lengths,
    groups,
    input_gate_weight,
    w_recur,
    weight_mask,
    bias,
    cotangent,
):
    seq_count, time_steps, width_in = tokens.shape
    hidden = cotangent.shape[2]
    row_count = input_gate_weight.shape[0]
    row_at = lax.axis_index("row")
    grp_at = lax.axis_index("grp")
    seq_at = lax.axis_index("seq")
    rows_n, seq_n = lax.axis_size("row"), lax.axis_size("seq")
    cols = Columns(hidden)
    wide = ceil_to(width_in + 2, LANES)
    share = seq_count // rows_n
    own = row_count == hidden
    pieced = own and rows_n == 4 and seq_n == 4 and lax.axis_size("grp") == 2

    plan = Plan(hidden, wide)
    at = jnp.stack([row_at, seq_at, grp_at]).astype(jnp.int32)
    own_weights, *mine = pl.pallas_call(
        functools.partial(shard_kernel, plan),
        grid_spec=pltpu.PrefetchScalarGridSpec(
            num_scalar_prefetch=1,
            grid=(1,),
            in_specs=[
                fixed(row_count, width_in),
                fixed(row_count, hidden),
                fixed(row_count, hidden),
                fixed(1, row_count),
            ],
            out_specs=[fixed(row_count, plan.columns)] + [fixed(plan.rows, plan.cut)] * pieced,
        ),
        out_shape=[jax.ShapeDtypeStruct((row_count, plan.columns), BF16)]
        + [jax.ShapeDtypeStruct((plan.rows, plan.cut), BF16)] * pieced,
        compiler_params=params(58),
        name="shard",
    )(at, input_gate_weight, w_recur, weight_mask, bias[None])
    sub = max(s for s in range(1, 8) if time_steps % (2 * s) == 0)
    steps = 2 * sub
    blocks = time_steps // steps

    def at_time(width):
        return pl.BlockSpec((steps, seq_count, width), lambda b, *_: (b, 0, 0))

    dropped = pl.pallas_call(
        functools.partial(drop_kernel, width_in),
        grid=(blocks,),
        in_specs=[at_time(width_in), fixed(seq_count, width_in)],
        out_specs=at_time(wide),
        out_shape=jax.ShapeDtypeStruct((time_steps, seq_count, wide), BF16),
        compiler_params=params(58),
        name="drop",
    )(jnp.swapaxes(tokens, 0, 1), in_mask)
    cot_time = jnp.swapaxes(cotangent, 0, 1)

    group_hot = (groups[:, None] == jnp.arange(2)[None, :]).astype(F32)
    valid_count = jnp.clip(lengths, 0, time_steps).astype(F32)
    counts = jnp.sum(group_hot * valid_count[:, None], 0)
    if pieced:
        *pieces, counts, dropped = gather_pieces(plan, mine[0], counts, dropped)
        sources = [own_weights] + pieces
    else:
        counts = lax.psum(counts, ("grp", "seq"))
        whole = lax.all_gather(own_weights, "row", axis=0, tiled=True)
        sources = [whole.reshape(4, hidden, plan.columns)]
    group_ratio = jnp.sum(counts) / counts
    seq_ratio = jnp.sum(group_hot * group_ratio[None, :], 1)

    acts, cells, prev_low, weights, w_rec = pl.pallas_call(
        functools.partial(forward_kernel, cols, plan, sub, pieced),
        grid_spec=pltpu.PrefetchScalarGridSpec(
            num_scalar_prefetch=1,
            grid=(blocks,),
            in_specs=[
                fixed(sub, seq_count, wide),
                pl.BlockSpec((sub, seq_count, wide), lambda b, *_: (2 * b + 1, 0, 0)),
                pl.BlockSpec(
                    (sub, seq_count, wide),
                    lambda b, *_: (jnp.minimum(2 * b + 2, 2 * blocks - 1), 0, 0),
                ),
            ]
            + [fixed(*source.shape) for source in sources],
            out_specs=[
                at_time(cols.total),
                at_time(hidden),
                at_time(hidden),
                pl.BlockSpec(memory_space=pl.ANY),
                pl.BlockSpec(memory_space=pl.ANY),
            ],
            scratch_shapes=[
                pltpu.VMEM((4, hidden, plan.columns), BF16),
                pltpu.VMEM((hidden, cols.total), BF16),
                pltpu.VMEM((sub * seq_count, cols.total), F32),
                pltpu.VMEM((sub * seq_count, cols.total), F32),
                pltpu.VMEM((seq_count, hidden), F32),
                pltpu.VMEM((seq_count, hidden), BF16),
                pltpu.SemaphoreType.DMA((2,)),
            ],
        ),
        out_shape=[
            jax.ShapeDtypeStruct((time_steps, seq_count, cols.total), F32),
            jax.ShapeDtypeStruct((time_steps, seq_count, hidden), F32),
            jax.ShapeDtypeStruct((time_steps, seq_count, hidden), BF16),
            jax.ShapeDtypeStruct((4, hidden, wide), BF16),
            jax.ShapeDtypeStruct((4, hidden, plan.columns - wide), BF16),
        ],
        compiler_params=params(52),
        name="forward",
    )(at, dropped, dropped, dropped, *sources)

    back_steps = sub
    back_blocks = time_steps // back_steps

    def back(b):
        return back_blocks - 1 - b

    def before(width):
        return pl.BlockSpec(
            (1, seq_count, width), lambda b, *_: (jnp.maximum(back(b) * back_steps - 1, 0), 0, 0)
        )

    def back_time(width):
        return pl.BlockSpec((back_steps, seq_count, width), lambda b, *_: (back(b), 0, 0))

    def later_time(width):
        return pl.BlockSpec(
            (back_steps, seq_count, width),
            lambda b, *_: (jnp.minimum(back(b) + 1, back_blocks - 1), 0, 0),
        )

    part_rows = ceil_to(-(-row_count // seq_n), 8)
    columns = wide + hidden
    group_row = groups.astype(F32)[None]
    sum_specs = [fixed(seq_n, part_rows, columns)] * 2
    sum_shapes = [jax.ShapeDtypeStruct((seq_n, part_rows, columns), BF16)] * 2
    sum_scratch = pltpu.VMEM((2, seq_n * part_rows, columns), F32)
    per_unit = pltpu.VMEM((seq_count, hidden), F32)
    own_specs, own_arrays, own_scratch = [], [], []
    if own:
        own_specs = [
            later_time(wide),
            later_time(hidden),
            fixed(back_steps, seq_count, wide),
            fixed(back_steps, seq_count, hidden),
            fixed(1, seq_count),
            fixed(row_count, hidden),
        ]
        own_arrays = [dropped, prev_low, dropped, prev_low, group_row, weight_mask]
        own_scratch = [
            pltpu.VMEM((back_steps * seq_count, hidden), BF16),
            pltpu.VMEM((2, hidden, back_steps * seq_count), BF16),
            pltpu.VMEM((1, back_steps * seq_count), BF16),
            sum_scratch,
        ]
    grads, *sums = pl.pallas_call(
        functools.partial(backward_kernel, cols, own),
        grid_spec=pltpu.PrefetchScalarGridSpec(
            num_scalar_prefetch=1,
            grid=(back_blocks,),
            in_specs=[
                back_time(cols.total),
                back_time(hidden),
                before(hidden),
                before(cols.total),
                back_time(hidden),
                fixed(seq_count, hidden),
                fixed(1, seq_count),
                fixed(1, seq_count),
                fixed(4, hidden, plan.columns - wide),
            ]
            + own_specs,
            out_specs=[back_time(cols.total)] + sum_specs * own,
            scratch_shapes=own_scratch
            + [per_unit] * 6
            + [pltpu.VMEM((seq_count, LANES), F32)] * 2,
        ),
        out_shape=[jax.ShapeDtypeStruct((time_steps, seq_count, cols.total), BF16)]
        + sum_shapes * own,
        compiler_params=params(52),
        name="backward",
    )(
        at,
        acts,
        cells,
        cells,
        acts,
        cot_time,
        out_mask,
        seq_ratio[None],
        lengths.astype(F32)[None],
        w_rec,
        *own_arrays,
    )

    if not own:
        own_rows = lax.dynamic_slice_in_dim(
            cols.unpack_lanes(grads), row_at * row_count, row_count, 2
        )
        sums = pl.pallas_call(
            weight_kernel,
            grid_spec=pltpu.PrefetchScalarGridSpec(
                num_scalar_prefetch=1,
                grid=(blocks,),
                in_specs=[
                    at_time(row_count),
                    fixed(1, seq_count),
                    at_time(wide),
                    at_time(hidden),
                    fixed(row_count, hidden),
                ],
                out_specs=sum_specs,
                scratch_shapes=[sum_scratch, pltpu.VMEM((seq_count, row_count), BF16)],
            ),
            out_shape=sum_shapes,
            compiler_params=params(58),
            name="weights",
        )(grp_at[None], own_rows, group_row, dropped, prev_low, weight_mask)
    keep, send = sums

    hold = lax.optimization_barrier
    block = (keep.astype(F32) + flip(send, "grp", 1).astype(F32)).astype(BF16)
    swapped = lax.all_to_all(block, "seq", 0, 0, tiled=True)

    own_seqs = lax.dynamic_slice_in_dim(grads, row_at * share, share, 1)
    own_scale = lax.dynamic_slice_in_dim(in_mask, row_at * share, share, 0).astype(F32) / KEEP_INPUT
    w_in = cols.pack(weights[:, :, :width_in])
    input_time = jnp.einsum("tsr,rk->tsk", own_seqs, w_in, preferred_element_type=F32)
    input_grad = jnp.swapaxes(input_time * own_scale[None], 0, 1)
    swapped, input_grad = hold((swapped, input_grad))

    total = jnp.sum(swapped.astype(F32), 0).astype(BF16)
    copies = jnp.broadcast_to(total[None], (seq_n,) + total.shape)
    parts = lax.all_to_all(copies, "seq", 0, 0, tiled=True)
    peer = flip(total, "grp", 1)
    ours, theirs = (
        jnp.concatenate([part[:, : width_in + 1], part[:, wide:]], 1).astype(F32)
        for part in (total, peer)
    )
    first = jnp.where(grp_at == 0, ours, theirs)
    second = jnp.where(grp_at == 0, theirs, ours)
    dots = [jnp.sum(a * b) for a, b in ((first, first), (first, second), (second, second))]
    gram = jnp.stack([dots[0], dots[1], dots[1], dots[2]]).reshape(2, 2)
    gram = exchange_sum(gram, "row")
    first, *rest = [flip(gram, "seq", bit) for bit in range(1, seq_n)]
    parts, first = hold((parts, first))
    gram = (gram + first) + (rest[0] + rest[1])
    everyone = parts.reshape(seq_n * part_rows, wide + hidden)[:row_count].astype(F32)
    return (
        input_grad,
        everyone[None, :, :width_in],
        everyone[None, :, wide:],
        everyone[None, :, width_in],
        gram,
    )


def solution(mesh):
    return jax.shard_map(
        local,
        mesh=mesh,
        in_specs=(
            P(("grp", "seq"), None, None),
            P(("grp", "seq"), None),
            P(("grp", "seq"), None),
            P(("grp", "seq")),
            P(("grp", "seq")),
            P("row", None),
            P("row", None),
            P("row", None),
            P("row"),
            P(("grp", "seq"), None, None),
        ),
        out_specs=(
            P(("grp", "seq", "row"), None, None),
            P("grp", "row", None),
            P("grp", "row", None),
            P("grp", "row"),
            P(),
        ),
        check_vma=False,
    )
```
